512 devices in a mesh: lat: 64 (over z, x, core), lev: 8 (over y).
Axes of the slice: x: 4, y: 8, z: 8, core: 2. Of those that a mesh axis runs over, the one named last changes fastest.
Arguments:
- wind_east: float32 [64, 192, 1152], P('lev', 'lat'), may hold values from -6 to 6
- wind_north: float32 [64, 192, 1152], P('lev', 'lat'), may hold values from -6 to 6
- layer_mass: float32 [64, 192, 1152], P('lev', 'lat'), may hold values from 0.5 to 1.5
- theta_field: float32 [64, 192, 1152], P('lev', 'lat'), may hold values from 0.4 to 2
- surface_height: float32 [192, 1152], P('lat'), may hold values from -6 to 6
- filter_cutoff: int32 [192], replicated, may hold values from 1 to 576, as said below
Outputs:
- new_east: float32 [64, 192, 1152], P('lev', 'lat')
- new_north: float32 [64, 192, 1152], P('lev', 'lat')
- new_mass: float32 [64, 192, 1152], P('lev', 'lat')
- new_heat: float32 [64, 192, 1152], P('lev', 'lat')
- height: float32 [64, 192, 1152], P('lev', 'lat')
The draws below stay inside these ranges and needn't reach their ends.
Inputs may be any that keep to these rules, and one draw needn't show every extreme that they name: filter_cutoff[j] equals 1152/2 (no filtering) for every latitude j with 24 <= j < 168; only the first and last 24 latitudes are filtered.
All inputs are finite; a program needn't handle non-finite values.
Results may differ from the reference program's by a relative error of at most 0.0003.
Values sent between devices are 32-bit elements; how exact they have to be, the bound alone decides.
No kernel may reach another device: no remote copies, remote signals or barrier semaphores. Data moves between devices by JAX's collectives and lax.ppermute only.
A program may use at most 64 MiB of HBM per device.

```python
import math
from functools import partial
import jax
import jax.numpy as jnp
from jax import lax

NLON = 1152
NLAT = 192
NLEV = 64


def draw_filter_cutoff(key, part):
    lat_ids = jnp.arange(NLAT, dtype=jnp.int32)
    band_rows = NLAT // 8
    polar_row = (lat_ids < band_rows) | (lat_ids >= NLAT - band_rows)
    picked = jax.random.randint(key, (NLAT,), 1, NLON // 2 + 1, dtype=jnp.int32)
    picked = jnp.where(lat_ids == 0, 1, picked)
    return jnp.where(polar_row, picked, NLON // 2).astype(jnp.int32)


def level_of(stream_key, dims, split, least, high):
    factor_of = 1.0
    for dim, blocks in split:
        heights = jax.random.uniform(jax.random.fold_in(jax.random.fold_in(stream_key, 6), dim), (blocks,), jnp.float32, least / len(split), high / len(split))
        factor_of = factor_of * jnp.repeat(jnp.exp(heights), dims[dim] // blocks).reshape((-1,) + (1,) * (len(dims) - 1 - dim))
    return factor_of


def centred(key, dims, scale, bound, cuts=(), held_as=jnp.bfloat16):
    gain = level_of(key, dims, cuts, -0.22, 0.18) if cuts else 1.0
    array = jax.random.normal(key, dims, jnp.float32) * scale * gain
    return jnp.minimum(jnp.maximum(array, -bound), bound).astype(held_as)


def setup_inputs(seed: int = 0) -> dict:
    key_list = jax.random.split(jax.random.key(seed), 7)
    return {
        "wind_east": centred(key_list[0], (NLEV, NLAT, NLON), 1.0, 6.0, ((0, 8), (1, 64)), jnp.float32),
        "wind_north": centred(key_list[1], (NLEV, NLAT, NLON), 1.0, 6.0, ((0, 8), (1, 64)), jnp.float32),
        "layer_mass": jnp.clip(0.5 + 1.0 * jax.random.uniform(key_list[2], (NLEV, NLAT, NLON), jnp.float32) ** level_of(key_list[2], (NLEV, NLAT, NLON), ((0, 8), (1, 64)), -0.2, 0.2), 0.5, 1.5),
        "theta_field": jnp.clip(jnp.exp(math.log(2.0) - 1.609438 * jax.random.uniform(key_list[3], (NLEV, NLAT, NLON), jnp.float32) ** level_of(key_list[3], (NLEV, NLAT, NLON), ((0, 8), (1, 64)), -0.2, 0.2)), 0.4, 2.0),
        "surface_height": centred(key_list[4], (NLAT, NLON), 1.0, 6.0, ((0, 64),), jnp.float32),
        "filter_cutoff": draw_filter_cutoff(jax.random.fold_in(key_list[6], 71), 0),
    }


TIME_STEP = 0.25
GAS_CONST = 1.0
TOP_PRESSURE = 1.0


def face_lon(values):
    return (37.0 * (jnp.roll(values, 1, -1) + values) - 8.0 * (jnp.roll(values, 2, -1) + jnp.roll(values, -1, -1)) + (jnp.roll(values, 3, -1) + jnp.roll(values, -2, -1))) / 60.0


def face_lat(padded, count):
    return (37.0 * (padded[..., 2:2 + count, :] + padded[..., 3:3 + count, :]) - 8.0 * (padded[..., 1:1 + count, :] + padded[..., 4:4 + count, :]) + (padded[..., 0:count, :] + padded[..., 5:5 + count, :])) / 60.0


def polar_filter(values, cutoff):
    spectrum = jnp.fft.rfft(values, axis=-1)
    waves = jnp.arange(NLON // 2 + 1, dtype=jnp.int32)
    keep = waves[None, :] <= cutoff[:, None]
    return jnp.fft.irfft(jnp.where(keep, spectrum, 0.0), n=NLON, axis=-1).astype(values.dtype)


def horizontal(fields, cutoff):
    wind_east, wind_north, layer_mass, theta_field = fields
    lat_rows = layer_mass.shape[0]
    coslat = jnp.sin(jnp.pi * jnp.arange(lat_rows).astype(jnp.float32) / lat_rows)[:, None]
    mass_pad = jnp.pad(layer_mass, ((3, 3), (0, 0)))
    theta_pad = jnp.pad(theta_field, ((3, 3), (0, 0)))
    flux_east = wind_east * face_lon(layer_mass)
    flux_north = wind_north * face_lat(mass_pad, lat_rows) * coslat
    east_smooth = polar_filter(wind_east, cutoff)
    north_smooth = polar_filter(wind_north, cutoff)
    east_flux = polar_filter(flux_east, cutoff)
    north_flux = polar_filter(flux_north, cutoff)
    north_full = jnp.concatenate([north_flux, jnp.zeros((1, north_flux.shape[1]), north_flux.dtype)], axis=0)
    new_mass = layer_mass - TIME_STEP * ((jnp.roll(east_flux, -1, -1) - east_flux) + (north_full[1:] - north_full[:-1]))
    heat_east = east_flux * face_lon(theta_field)
    heat_north = north_full * face_lat(theta_pad, lat_rows + 1)
    new_heat = theta_field * layer_mass - TIME_STEP * ((jnp.roll(heat_east, -1, -1) - heat_east) + (heat_north[1:] - heat_north[:-1]))
    return east_smooth, north_smooth, new_mass, new_heat


def reference(wind_east, wind_north, layer_mass, theta_field, surface_height, filter_cutoff):
    east_smooth, north_smooth, new_mass, new_heat = lax.map(partial(horizontal, cutoff=filter_cutoff), (wind_east, wind_north, layer_mass, theta_field))
    bottom = TOP_PRESSURE + jnp.cumsum(layer_mass, axis=0)
    top_press = bottom - layer_mass
    thickness = GAS_CONST * theta_field * (jnp.log(bottom) - jnp.log(top_press))
    inclusive = jnp.flip(jnp.cumsum(jnp.flip(thickness, 0), axis=0), 0)
    height = surface_height[None] + (inclusive - thickness) + 0.5 * thickness
    new_east = east_smooth - TIME_STEP * (height - jnp.roll(height, 1, -1))
    height_south = jnp.concatenate([jnp.zeros_like(height[:, :1]), height[:, :-1]], axis=1)
    inside = (jnp.arange(height.shape[1]) > 0).astype(height.dtype)[None, :, None]
    new_north = (north_smooth - TIME_STEP * (height - height_south)) * inside
    return (new_east, new_north, new_mass, new_heat, height)
```

```python
import numpy as np
import jax
import jax.numpy as jnp
from jax import lax
from jax.sharding import PartitionSpec as P

TIME_STEP = 0.25
GAS_CONST = 1.0
TOP_PRESSURE = 1.0


def extended(cells, sides, width):
    for axis, dim in sides:
        count = lax.axis_size(axis)
        ends = count - 1
        head = lax.slice_in_dim(cells, 0, width, axis=dim)
        tail = lax.slice_in_dim(cells, cells.shape[dim] - width, cells.shape[dim], axis=dim)
        cells = jnp.concatenate(
            [
                lax.ppermute(tail, axis, [(i, (i + 1) % count) for i in range(ends)]),
                cells,
                lax.ppermute(head, axis, [((i + 1) % count, i) for i in range(ends)]),
            ],
            axis=dim,
        )
    return cells


def from_behind(block, axis, distance):
    devices = range(lax.axis_size(axis))
    route = [(i - distance, i) for i in devices if i - distance in devices]
    return lax.ppermute(block, axis, route)


def face_lon(values):
    return (
        37.0 * (jnp.roll(values, 1, -1) + values)
        - 8.0 * (jnp.roll(values, 2, -1) + jnp.roll(values, -1, -1))
        + (jnp.roll(values, 3, -1) + jnp.roll(values, -2, -1))
    ) / 60.0


def face_lat(padded, count):
    return (
        37.0 * (padded[..., 2 : 2 + count, :] + padded[..., 3 : 3 + count, :])
        - 8.0 * (padded[..., 1 : 1 + count, :] + padded[..., 4 : 4 + count, :])
        + (padded[..., 0:count, :] + padded[..., 5 : 5 + count, :])
    ) / 60.0


FACTOR_ROWS = 9
FACTOR_LANES = 128


def fft_tables(length):
    rows, lanes = FACTOR_ROWS, FACTOR_LANES
    small = np.arange(rows)
    small_phase = 2.0 * np.pi * np.outer(small, small) / rows
    low = np.arange(rows)[:, None]
    high = np.arange(lanes)[None, :]
    twist = 2.0 * np.pi * ((low * high) % length) / length
    waves = np.arange(lanes)
    wave_phase = 2.0 * np.pi * (np.outer(waves, waves) % lanes) / lanes
    wc, ws = np.cos(wave_phase), np.sin(wave_phase)
    forward = np.block([[wc, -ws], [ws, wc]]).astype(np.float32)
    inverse = np.block([[wc, ws], [-ws, wc]]).astype(np.float32)
    number = np.arange(rows)[:, None] + rows * np.arange(lanes)[None, :]
    folded = np.minimum(number, length - number)
    folded = np.concatenate([folded, folded], axis=1)[:, None, :].astype(np.int32)
    return (
        np.cos(small_phase),
        np.sin(small_phase),
        np.cos(twist).reshape(1, length).astype(np.float32),
        np.sin(twist).reshape(1, length).astype(np.float32),
        forward,
        inverse,
        folded,
    )


def filter_rows(values, cuts):
    rows, lanes = FACTOR_ROWS, FACTOR_LANES
    count, length = values.shape
    c9, s9, twc, tws, forward, inverse, folded = fft_tables(length)
    highest = lax.Precision.HIGHEST
    parts = [values[:, n * lanes : (n + 1) * lanes] for n in range(rows)]
    real_a = jnp.concatenate(
        [sum(float(c9[k, n]) * parts[n] for n in range(rows)) for k in range(rows)], axis=1
    )
    imag_a = jnp.concatenate(
        [sum(float(-s9[k, n]) * parts[n] for n in range(rows)) for k in range(rows)], axis=1
    )
    real_b = real_a * twc + imag_a * tws
    imag_b = imag_a * twc - real_a * tws
    stacked = jnp.concatenate(
        [
            jnp.concatenate(
                [real_b[:, k * lanes : (k + 1) * lanes], imag_b[:, k * lanes : (k + 1) * lanes]],
                axis=1,
            )
            for k in range(rows)
        ],
        axis=0,
    )
    spectrum = jnp.dot(stacked, forward, precision=highest)
    keep = (folded <= cuts[None, :, None]).astype(jnp.float32).reshape(rows * count, 2 * lanes)
    back = jnp.dot(spectrum * keep, inverse, precision=highest)
    real_c = jnp.concatenate([back[k * count : (k + 1) * count, :lanes] for k in range(rows)], axis=1)
    imag_c = jnp.concatenate([back[k * count : (k + 1) * count, lanes:] for k in range(rows)], axis=1)
    real_d = real_c * twc - imag_c * tws
    imag_d = imag_c * twc + real_c * tws
    real_parts = [real_d[:, k * lanes : (k + 1) * lanes] for k in range(rows)]
    imag_parts = [imag_d[:, k * lanes : (k + 1) * lanes] for k in range(rows)]
    return jnp.concatenate(
        [
            sum(
                float(c9[k, n] / length) * real_parts[k] - float(s9[k, n] / length) * imag_parts[k]
                for k in range(rows)
            )
            for n in range(rows)
        ],
        axis=1,
    )


def prefix_over(value, axis, before):
    count = lax.axis_size(axis)
    total = jnp.zeros_like(value)
    for step in range(1, count):
        if before:
            route = [(i, i + step) for i in range(count - step)]
        else:
            route = [(i + step, i) for i in range(count - step)]
        total = total + lax.ppermute(value, axis, route)
    return total


def local(wind_east, wind_north, layer_mass, theta_field, surface_height, filter_cutoff):
    levels, lat_rows, length = wind_east.shape
    lat_count = lax.axis_size("lat")
    lat_rank = lax.axis_index("lat")
    nlat_all = lat_rows * lat_count
    first_row = lat_rank * lat_rows
    row_ids = first_row + jnp.arange(lat_rows, dtype=jnp.int32)
    coslat = jnp.sin(jnp.pi * row_ids.astype(jnp.float32) / nlat_all)[None, :, None]
    stacked = jnp.stack([layer_mass, theta_field])
    padded = extended(stacked, (("lat", 2),), 3)
    mass_faces = face_lat(padded[0], lat_rows)
    theta_faces = face_lat(padded[1], lat_rows + 1)
    flux_east = wind_east * face_lon(layer_mass)
    flux_north = wind_north * mass_faces * coslat
    fields = jnp.stack([wind_east, wind_north, flux_east, flux_north])
    own_cuts = lax.dynamic_slice_in_dim(filter_cutoff, first_row, lat_rows)
    row_cuts = jnp.broadcast_to(own_cuts, (4, levels, lat_rows)).reshape(-1)
    smooth = filter_rows(fields.reshape(-1, length), row_cuts).reshape(fields.shape)
    east_smooth = smooth[0]
    north_smooth = smooth[1]
    east_flux = smooth[2]
    north_flux = smooth[3]
    next_face = from_behind(north_flux[:, :1], "lat", -1)
    north_full = jnp.concatenate([north_flux, next_face], axis=1)
    new_mass = layer_mass - TIME_STEP * (
        jnp.roll(east_flux, -1, -1) - east_flux + (north_full[:, 1:] - north_full[:, :-1])
    )
    heat_east = east_flux * face_lon(theta_field)
    heat_north = north_full * theta_faces
    new_heat = theta_field * layer_mass - TIME_STEP * (
        jnp.roll(heat_east, -1, -1) - heat_east + (heat_north[:, 1:] - heat_north[:, :-1])
    )
    column = jnp.sum(layer_mass, axis=0)
    above_mass = prefix_over(column, "lev", True)
    bottom = TOP_PRESSURE + above_mass[None] + jnp.cumsum(layer_mass, axis=0)
    top_press = bottom - layer_mass
    thickness = GAS_CONST * theta_field * (jnp.log(bottom) - jnp.log(top_press))
    depth_sum = jnp.sum(thickness, axis=0)
    below_depth = prefix_over(depth_sum, "lev", False)
    inclusive = jnp.flip(jnp.cumsum(jnp.flip(thickness, 0), axis=0), 0)
    height_cols = (
        surface_height[None] + below_depth[None] + (inclusive - thickness) + 0.5 * thickness
    )
    lower_row = from_behind(height_cols[:, -1:], "lat", 1)
    height_south = jnp.concatenate([lower_row, height_cols[:, :-1]], axis=1)
    new_east = east_smooth - TIME_STEP * (height_cols - jnp.roll(height_cols, 1, -1))
    inside = (row_ids > 0).astype(jnp.float32)[None, :, None]
    new_north = (north_smooth - TIME_STEP * (height_cols - height_south)) * inside
    return (new_east, new_north, new_mass, new_heat, height_cols)


def solution(mesh):
    in_specs = (
        P("lev", "lat", None),
        P("lev", "lat", None),
        P("lev", "lat", None),
        P("lev", "lat", None),
        P("lat", None),
        P(),
    )
    out_specs = (
        P("lev", "lat", None),
        P("lev", "lat", None),
        P("lev", "lat", None),
        P("lev", "lat", None),
        P("lev", "lat", None),
    )
    return jax.shard_map(local, mesh=mesh, in_specs=in_specs, out_specs=out_specs, check_vma=False)
```

```python
import numpy as np
import jax
import jax.numpy as jnp
from jax import lax
from jax.sharding import PartitionSpec as P

TIME_STEP = 0.25
GAS_CONST = 1.0
TOP_PRESSURE = 1.0


def extended(cells, sides, width):
    for axis, dim in sides:
        count = lax.axis_size(axis)
        ends = count - 1
        head = lax.slice_in_dim(cells, 0, width, axis=dim)
        tail = lax.slice_in_dim(cells, cells.shape[dim] - width, cells.shape[dim], axis=dim)
        cells = jnp.concatenate(
            [
                lax.ppermute(tail, axis, [(i, (i + 1) % count) for i in range(ends)]),
                cells,
                lax.ppermute(head, axis, [((i + 1) % count, i) for i in range(ends)]),
            ],
            axis=dim,
        )
    return cells


def from_behind(block, axis, distance):
    devices = range(lax.axis_size(axis))
    route = [(i - distance, i) for i in devices if i - distance in devices]
    return lax.ppermute(block, axis, route)


def face_lon(values):
    return (
        37.0 * (jnp.roll(values, 1, -1) + values)
        - 8.0 * (jnp.roll(values, 2, -1) + jnp.roll(values, -1, -1))
        + (jnp.roll(values, 3, -1) + jnp.roll(values, -2, -1))
    ) / 60.0


def face_lat(padded, count):
    return (
        37.0 * (padded[..., 2 : 2 + count, :] + padded[..., 3 : 3 + count, :])
        - 8.0 * (padded[..., 1 : 1 + count, :] + padded[..., 4 : 4 + count, :])
        + (padded[..., 0:count, :] + padded[..., 5 : 5 + count, :])
    ) / 60.0


FACTOR_ROWS = 9
FACTOR_LANES = 128


def fft_tables(length):
    rows, lanes = FACTOR_ROWS, FACTOR_LANES
    small = np.arange(rows)
    small_phase = 2.0 * np.pi * np.outer(small, small) / rows
    low = np.arange(rows)[:, None]
    high = np.arange(lanes)[None, :]
    twist = 2.0 * np.pi * ((low * high) % length) / length
    waves = np.arange(lanes)
    wave_phase = 2.0 * np.pi * (np.outer(waves, waves) % lanes) / lanes
    wc, ws = np.cos(wave_phase), np.sin(wave_phase)
    forward = np.block([[wc, -ws], [ws, wc]]).astype(np.float32)
    inverse = np.block([[wc, ws], [-ws, wc]]).astype(np.float32)
    number = np.arange(rows)[:, None] + rows * np.arange(lanes)[None, :]
    folded = np.minimum(number, length - number)
    folded = np.concatenate([folded, folded], axis=1)[:, None, :].astype(np.int32)
    return (
        np.cos(small_phase),
        np.sin(small_phase),
        np.cos(twist).reshape(1, length).astype(np.float32),
        np.sin(twist).reshape(1, length).astype(np.float32),
        forward,
        inverse,
        folded,
    )


def filter_rows(values, cuts):
    rows, lanes = FACTOR_ROWS, FACTOR_LANES
    count, length = values.shape
    c9, s9, twc, tws, forward, inverse, folded = fft_tables(length)
    highest = lax.Precision.HIGHEST
    parts = [values[:, n * lanes : (n + 1) * lanes] for n in range(rows)]
    real_a = jnp.concatenate(
        [sum(float(c9[k, n]) * parts[n] for n in range(rows)) for k in range(rows)], axis=1
    )
    imag_a = jnp.concatenate(
        [sum(float(-s9[k, n]) * parts[n] for n in range(rows)) for k in range(rows)], axis=1
    )
    real_b = real_a * twc + imag_a * tws
    imag_b = imag_a * twc - real_a * tws
    stacked = jnp.concatenate(
        [
            jnp.concatenate(
                [real_b[:, k * lanes : (k + 1) * lanes], imag_b[:, k * lanes : (k + 1) * lanes]],
                axis=1,
            )
            for k in range(rows)
        ],
        axis=0,
    )
    spectrum = jnp.dot(stacked, forward, precision=highest)
    keep = (folded <= cuts[None, :, None]).astype(jnp.float32).reshape(rows * count, 2 * lanes)
    back = jnp.dot(spectrum * keep, inverse, precision=highest)
    real_c = jnp.concatenate([back[k * count : (k + 1) * count, :lanes] for k in range(rows)], axis=1)
    imag_c = jnp.concatenate([back[k * count : (k + 1) * count, lanes:] for k in range(rows)], axis=1)
    real_d = real_c * twc - imag_c * tws
    imag_d = imag_c * twc + real_c * tws
    real_parts = [real_d[:, k * lanes : (k + 1) * lanes] for k in range(rows)]
    imag_parts = [imag_d[:, k * lanes : (k + 1) * lanes] for k in range(rows)]
    return jnp.concatenate(
        [
            sum(
                float(c9[k, n] / length) * real_parts[k] - float(s9[k, n] / length) * imag_parts[k]
                for k in range(rows)
            )
            for n in range(rows)
        ],
        axis=1,
    )


def prefix_over(value, axis, before):
    count = lax.axis_size(axis)
    reach = max(1, count // 2)

    def shifted(block, step):
        if before:
            route = [(i, i + step) for i in range(count - step)]
        else:
            route = [(i + step, i) for i in range(count - step)]
        return lax.ppermute(block, axis, route)

    window = value
    for step in range(1, min(reach, count)):
        window = window + shifted(value, step)
    total = window
    step = reach
    while step < count:
        total = total + shifted(total, step)
        step *= 2
    return total - value


def local(wind_east, wind_north, layer_mass, theta_field, surface_height, filter_cutoff):
    levels, lat_rows, length = wind_east.shape
    lat_count = lax.axis_size("lat")
    lat_rank = lax.axis_index("lat")
    nlat_all = lat_rows * lat_count
    first_row = lat_rank * lat_rows
    row_ids = first_row + jnp.arange(lat_rows, dtype=jnp.int32)
    coslat = jnp.sin(jnp.pi * row_ids.astype(jnp.float32) / nlat_all)[None, :, None]
    stacked = jnp.stack([layer_mass, theta_field])
    padded = extended(stacked, (("lat", 2),), 3)
    mass_faces = face_lat(padded[0], lat_rows)
    theta_faces = face_lat(padded[1], lat_rows + 1)
    flux_east = wind_east * face_lon(layer_mass)
    flux_north = wind_north * mass_faces * coslat
    fields = jnp.stack([wind_east, wind_north, flux_east, flux_north])
    own_cuts = lax.dynamic_slice_in_dim(filter_cutoff, first_row, lat_rows)
    row_cuts = jnp.broadcast_to(own_cuts, (4, levels, lat_rows)).reshape(-1)
    smooth = filter_rows(fields.reshape(-1, length), row_cuts).reshape(fields.shape)
    east_smooth = smooth[0]
    north_smooth = smooth[1]
    east_flux = smooth[2]
    north_flux = smooth[3]
    next_face = from_behind(north_flux[:, :1], "lat", -1)
    north_full = jnp.concatenate([north_flux, next_face], axis=1)
    new_mass = layer_mass - TIME_STEP * (
        jnp.roll(east_flux, -1, -1) - east_flux + (north_full[:, 1:] - north_full[:, :-1])
    )
    heat_east = east_flux * face_lon(theta_field)
    heat_north = north_full * theta_faces
    new_heat = theta_field * layer_mass - TIME_STEP * (
        jnp.roll(heat_east, -1, -1) - heat_east + (heat_north[:, 1:] - heat_north[:, :-1])
    )
    column = jnp.sum(layer_mass, axis=0)
    above_mass = prefix_over(column, "lev", True)
    bottom = TOP_PRESSURE + above_mass[None] + jnp.cumsum(layer_mass, axis=0)
    top_press = bottom - layer_mass
    thickness = GAS_CONST * theta_field * (jnp.log(bottom) - jnp.log(top_press))
    depth_sum = jnp.sum(thickness, axis=0)
    below_depth = prefix_over(depth_sum, "lev", False)
    inclusive = jnp.flip(jnp.cumsum(jnp.flip(thickness, 0), axis=0), 0)
    height_cols = (
        surface_height[None] + below_depth[None] + (inclusive - thickness) + 0.5 * thickness
    )
    lower_row = from_behind(height_cols[:, -1:], "lat", 1)
    height_south = jnp.concatenate([lower_row, height_cols[:, :-1]], axis=1)
    new_east = east_smooth - TIME_STEP * (height_cols - jnp.roll(height_cols, 1, -1))
    inside = (row_ids > 0).astype(jnp.float32)[None, :, None]
    new_north = (north_smooth - TIME_STEP * (height_cols - height_south)) * inside
    return (new_east, new_north, new_mass, new_heat, height_cols)


def solution(mesh):
    in_specs = (
        P("lev", "lat", None),
        P("lev", "lat", None),
        P("lev", "lat", None),
        P("lev", "lat", None),
        P("lat", None),
        P(),
    )
    out_specs = (
        P("lev", "lat", None),
        P("lev", "lat", None),
        P("lev", "lat", None),
        P("lev", "lat", None),
        P("lev", "lat", None),
    )
    return jax.shard_map(local, mesh=mesh, in_specs=in_specs, out_specs=out_specs, check_vma=False)
```

```python
import numpy as np
import jax
import jax.numpy as jnp
from jax import lax
from jax.sharding import PartitionSpec as P

TIME_STEP = 0.25
GAS_CONST = 1.0
TOP_PRESSURE = 1.0


def extended(cells, sides, width):
    for axis, dim in sides:
        count = lax.axis_size(axis)
        ends = count - 1
        head = lax.slice_in_dim(cells, 0, width, axis=dim)
        tail = lax.slice_in_dim(cells, cells.shape[dim] - width, cells.shape[dim], axis=dim)
        cells = jnp.concatenate(
            [
                lax.ppermute(tail, axis, [(i, (i + 1) % count) for i in range(ends)]),
                cells,
                lax.ppermute(head, axis, [((i + 1) % count, i) for i in range(ends)]),
            ],
            axis=dim,
        )
    return cells


def from_behind(block, axis, distance):
    devices = range(lax.axis_size(axis))
    route = [(i - distance, i) for i in devices if i - distance in devices]
    return lax.ppermute(block, axis, route)


def face_lon(values):
    return (
        37.0 * (jnp.roll(values, 1, -1) + values)
        - 8.0 * (jnp.roll(values, 2, -1) + jnp.roll(values, -1, -1))
        + (jnp.roll(values, 3, -1) + jnp.roll(values, -2, -1))
    ) / 60.0


def face_lat(padded, count):
    return (
        37.0 * (padded[2 : 2 + count] + padded[3 : 3 + count])
        - 8.0 * (padded[1 : 1 + count] + padded[4 : 4 + count])
        + (padded[0:count] + padded[5 : 5 + count])
    ) / 60.0


FACTOR_ROWS = 9
FACTOR_LANES = 128


def fft_tables(length):
    rows, lanes = FACTOR_ROWS, FACTOR_LANES
    small = np.arange(rows)
    small_phase = 2.0 * np.pi * np.outer(small, small) / rows
    low = np.arange(rows)[:, None]
    high = np.arange(lanes)[None, :]
    twist = 2.0 * np.pi * ((low * high) % length) / length
    waves = np.arange(lanes)
    wave_phase = 2.0 * np.pi * (np.outer(waves, waves) % lanes) / lanes
    wc, ws = np.cos(wave_phase), np.sin(wave_phase)
    forward = np.block([[wc, -ws], [ws, wc]]).astype(np.float32)
    inverse = np.block([[wc, ws], [-ws, wc]]).astype(np.float32)
    number = np.arange(rows)[:, None] + rows * np.arange(lanes)[None, :]
    folded = np.minimum(number, length - number)
    folded = np.concatenate([folded, folded], axis=1)[:, None, :].astype(np.int32)
    return (
        np.cos(small_phase),
        np.sin(small_phase),
        np.cos(twist).reshape(1, length).astype(np.float32),
        np.sin(twist).reshape(1, length).astype(np.float32),
        forward,
        inverse,
        folded,
    )


def filter_rows(values, cuts):
    rows, lanes = FACTOR_ROWS, FACTOR_LANES
    count, length = values.shape
    c9, s9, twc, tws, forward, inverse, folded = fft_tables(length)
    highest = lax.Precision.HIGHEST
    parts = [values[:, n * lanes : (n + 1) * lanes] for n in range(rows)]
    real_a = jnp.concatenate(
        [sum(float(c9[k, n]) * parts[n] for n in range(rows)) for k in range(rows)], axis=1
    )
    imag_a = jnp.concatenate(
        [sum(float(-s9[k, n]) * parts[n] for n in range(rows)) for k in range(rows)], axis=1
    )
    real_b = real_a * twc + imag_a * tws
    imag_b = imag_a * twc - real_a * tws
    stacked = jnp.concatenate(
        [
            jnp.concatenate(
                [real_b[:, k * lanes : (k + 1) * lanes], imag_b[:, k * lanes : (k + 1) * lanes]],
                axis=1,
            )
            for k in range(rows)
        ],
        axis=0,
    )
    spectrum = jnp.dot(stacked, forward, precision=highest)
    keep = (folded <= cuts[None, :, None]).astype(jnp.float32).reshape(rows * count, 2 * lanes)
    back = jnp.dot(spectrum * keep, inverse, precision=highest)
    real_c = jnp.concatenate([back[k * count : (k + 1) * count, :lanes] for k in range(rows)], axis=1)
    imag_c = jnp.concatenate([back[k * count : (k + 1) * count, lanes:] for k in range(rows)], axis=1)
    real_d = real_c * twc - imag_c * tws
    imag_d = imag_c * twc + real_c * tws
    real_parts = [real_d[:, k * lanes : (k + 1) * lanes] for k in range(rows)]
    imag_parts = [imag_d[:, k * lanes : (k + 1) * lanes] for k in range(rows)]
    return jnp.concatenate(
        [
            sum(
                float(c9[k, n] / length) * real_parts[k] - float(s9[k, n] / length) * imag_parts[k]
                for k in range(rows)
            )
            for n in range(rows)
        ],
        axis=1,
    )


def prefix_over(value, axis, before):
    count = lax.axis_size(axis)
    total = jnp.zeros_like(value)
    for step in range(1, count):
        if before:
            route = [(i, i + step) for i in range(count - step)]
        else:
            route = [(i + step, i) for i in range(count - step)]
        total = total + lax.ppermute(value, axis, route)
    return total


def local(wind_east, wind_north, layer_mass, theta_field, surface_height, filter_cutoff):
    levels, lat_rows, length = wind_east.shape
    wind_east, wind_north, layer_mass, theta_field = (
        jnp.transpose(v, (1, 0, 2)) for v in (wind_east, wind_north, layer_mass, theta_field)
    )
    lat_count = lax.axis_size("lat")
    lat_rank = lax.axis_index("lat")
    nlat_all = lat_rows * lat_count
    first_row = lat_rank * lat_rows
    row_ids = first_row + jnp.arange(lat_rows, dtype=jnp.int32)
    coslat = jnp.sin(jnp.pi * row_ids.astype(jnp.float32) / nlat_all)[:, None, None]
    stacked = jnp.stack([layer_mass, theta_field])
    padded = extended(stacked, (("lat", 1),), 3)
    mass_faces = face_lat(padded[0], lat_rows)
    theta_faces = face_lat(padded[1], lat_rows + 1)
    flux_east = wind_east * face_lon(layer_mass)
    flux_north = wind_north * mass_faces * coslat
    fields = jnp.stack([wind_east, wind_north, flux_east, flux_north])
    own_cuts = lax.dynamic_slice_in_dim(filter_cutoff, first_row, lat_rows)
    row_cuts = jnp.broadcast_to(own_cuts[None, :, None], fields.shape[:3]).reshape(-1)
    smooth = filter_rows(fields.reshape(-1, length), row_cuts).reshape(fields.shape)
    east_smooth = smooth[0]
    north_smooth = smooth[1]
    east_flux = smooth[2]
    north_flux = smooth[3]
    next_face = from_behind(north_flux[:1], "lat", -1)
    north_full = jnp.concatenate([north_flux, next_face], axis=0)
    new_mass = layer_mass - TIME_STEP * (
        jnp.roll(east_flux, -1, -1) - east_flux + (north_full[1:] - north_full[:-1])
    )
    heat_east = east_flux * face_lon(theta_field)
    heat_north = north_full * theta_faces
    new_heat = theta_field * layer_mass - TIME_STEP * (
        jnp.roll(heat_east, -1, -1) - heat_east + (heat_north[1:] - heat_north[:-1])
    )
    column = jnp.sum(layer_mass, axis=1)
    above_mass = prefix_over(column, "lev", True)
    bottom = TOP_PRESSURE + above_mass[:, None] + jnp.cumsum(layer_mass, axis=1)
    top_press = bottom - layer_mass
    thickness = GAS_CONST * theta_field * (jnp.log(bottom) - jnp.log(top_press))
    depth_sum = jnp.sum(thickness, axis=1)
    below_depth = prefix_over(depth_sum, "lev", False)
    inclusive = jnp.flip(jnp.cumsum(jnp.flip(thickness, 1), axis=1), 1)
    height = (
        surface_height[:, None] + below_depth[:, None] + (inclusive - thickness) + 0.5 * thickness
    )
    lower_row = from_behind(height[-1:], "lat", 1)
    height_south = jnp.concatenate([lower_row, height[:-1]], axis=0)
    new_east = east_smooth - TIME_STEP * (height - jnp.roll(height, 1, -1))
    inside = (row_ids > 0).astype(jnp.float32)[:, None, None]
    new_north = (north_smooth - TIME_STEP * (height - height_south)) * inside
    outputs = (new_east, new_north, new_mass, new_heat, height)
    return tuple(jnp.transpose(v, (1, 0, 2)) for v in outputs)


def solution(mesh):
    in_specs = (
        P("lev", "lat", None),
        P("lev", "lat", None),
        P("lev", "lat", None),
        P("lev", "lat", None),
        P("lat", None),
        P(),
    )
    out_specs = (
        P("lev", "lat", None),
        P("lev", "lat", None),
        P("lev", "lat", None),
        P("lev", "lat", None),
        P("lev", "lat", None),
    )
    return jax.shard_map(local, mesh=mesh, in_specs=in_specs, out_specs=out_specs, check_vma=False)
```

```python
import numpy as np
import jax
import jax.numpy as jnp
from jax import lax
from jax.sharding import PartitionSpec as P

TIME_STEP = 0.25
GAS_CONST = 1.0
TOP_PRESSURE = 1.0


def extended(cells, sides, width):
    for axis, dim in sides:
        count = lax.axis_size(axis)
        ends = count - 1
        head = lax.slice_in_dim(cells, 0, width, axis=dim)
        tail = lax.slice_in_dim(cells, cells.shape[dim] - width, cells.shape[dim], axis=dim)
        cells = jnp.concatenate(
            [
                lax.ppermute(tail, axis, [(i, (i + 1) % count) for i in range(ends)]),
                cells,
                lax.ppermute(head, axis, [((i + 1) % count, i) for i in range(ends)]),
            ],
            axis=dim,
        )
    return cells


def from_behind(block, axis, distance):
    devices = range(lax.axis_size(axis))
    route = [(i - distance, i) for i in devices if i - distance in devices]
    return lax.ppermute(block, axis, route)


def face_lon(values):
    return (
        37.0 * (jnp.roll(values, 1, -1) + values)
        - 8.0 * (jnp.roll(values, 2, -1) + jnp.roll(values, -1, -1))
        + (jnp.roll(values, 3, -1) + jnp.roll(values, -2, -1))
    ) / 60.0


def face_lat(padded, count):
    return (
        37.0 * (padded[2 : 2 + count] + padded[3 : 3 + count])
        - 8.0 * (padded[1 : 1 + count] + padded[4 : 4 + count])
        + (padded[0:count] + padded[5 : 5 + count])
    ) / 60.0


FACTOR_ROWS = 9
FACTOR_LANES = 128


def fft_tables(length):
    rows, lanes = FACTOR_ROWS, FACTOR_LANES
    small = np.arange(rows)
    small_phase = 2.0 * np.pi * np.outer(small, small) / rows
    low = np.arange(rows)[:, None]
    high = np.arange(lanes)[None, :]
    twist = 2.0 * np.pi * ((low * high) % length) / length
    waves = np.arange(lanes)
    wave_phase = 2.0 * np.pi * (np.outer(waves, waves) % lanes) / lanes
    wc, ws = np.cos(wave_phase), np.sin(wave_phase)
    forward = np.block([[wc, -ws], [ws, wc]]).astype(np.float32)
    inverse = np.block([[wc, ws], [-ws, wc]]).astype(np.float32)
    number = np.arange(rows)[:, None] + rows * np.arange(lanes)[None, :]
    folded = np.minimum(number, length - number)
    folded = np.concatenate([folded, folded], axis=1)[:, None, :].astype(np.int32)
    return (
        np.cos(small_phase),
        np.sin(small_phase),
        np.cos(twist).reshape(1, length).astype(np.float32),
        np.sin(twist).reshape(1, length).astype(np.float32),
        forward,
        inverse,
        folded,
    )


def filter_rows(values, cuts):
    rows, lanes = FACTOR_ROWS, FACTOR_LANES
    count, length = values.shape
    c9, s9, twc, tws, forward, inverse, folded = fft_tables(length)
    highest = lax.Precision.HIGHEST
    parts = [values[:, n * lanes : (n + 1) * lanes] for n in range(rows)]
    real_a = jnp.concatenate(
        [sum(float(c9[k, n]) * parts[n] for n in range(rows)) for k in range(rows)], axis=1
    )
    imag_a = jnp.concatenate(
        [sum(float(-s9[k, n]) * parts[n] for n in range(rows)) for k in range(rows)], axis=1
    )
    real_b = real_a * twc + imag_a * tws
    imag_b = imag_a * twc - real_a * tws
    stacked = jnp.concatenate(
        [
            jnp.concatenate(
                [real_b[:, k * lanes : (k + 1) * lanes], imag_b[:, k * lanes : (k + 1) * lanes]],
                axis=1,
            )
            for k in range(rows)
        ],
        axis=0,
    )
    spectrum = jnp.dot(stacked, forward, precision=highest)
    keep = (folded <= cuts[None, :, None]).astype(jnp.float32).reshape(rows * count, 2 * lanes)
    back = jnp.dot(spectrum * keep, inverse, precision=highest)
    real_c = jnp.concatenate([back[k * count : (k + 1) * count, :lanes] for k in range(rows)], axis=1)
    imag_c = jnp.concatenate([back[k * count : (k + 1) * count, lanes:] for k in range(rows)], axis=1)
    real_d = real_c * twc - imag_c * tws
    imag_d = imag_c * twc + real_c * tws
    real_parts = [real_d[:, k * lanes : (k + 1) * lanes] for k in range(rows)]
    imag_parts = [imag_d[:, k * lanes : (k + 1) * lanes] for k in range(rows)]
    return jnp.concatenate(
        [
            sum(
                float(c9[k, n] / length) * real_parts[k] - float(s9[k, n] / length) * imag_parts[k]
                for k in range(rows)
            )
            for n in range(rows)
        ],
        axis=1,
    )


def prefix_over(value, axis, before):
    count = lax.axis_size(axis)
    rank = lax.axis_index(axis)
    copies = jnp.broadcast_to(value, (count, *value.shape))
    pieces = lax.all_to_all(copies, axis, split_axis=0, concat_axis=0, tiled=True)
    owners = jnp.arange(count, dtype=jnp.int32)
    chosen = owners < rank if before else owners > rank
    return jnp.sum(jnp.where(chosen[:, None, None], pieces, 0.0), axis=0)


def local(wind_east, wind_north, layer_mass, theta_field, surface_height, filter_cutoff):
    levels, lat_rows, length = wind_east.shape
    wind_east, wind_north, layer_mass, theta_field = (
        jnp.transpose(v, (1, 0, 2)) for v in (wind_east, wind_north, layer_mass, theta_field)
    )
    lat_count = lax.axis_size("lat")
    lat_rank = lax.axis_index("lat")
    nlat_all = lat_rows * lat_count
    first_row = lat_rank * lat_rows
    row_ids = first_row + jnp.arange(lat_rows, dtype=jnp.int32)
    coslat = jnp.sin(jnp.pi * row_ids.astype(jnp.float32) / nlat_all)[:, None, None]
    stacked = jnp.stack([layer_mass, theta_field])
    padded = extended(stacked, (("lat", 1),), 3)
    mass_faces = face_lat(padded[0], lat_rows)
    theta_faces = face_lat(padded[1], lat_rows + 1)
    flux_east = wind_east * face_lon(layer_mass)
    flux_north = wind_north * mass_faces * coslat
    column = jnp.sum(layer_mass, axis=1)
    above_mass = prefix_over(column, "lev", True)
    bottom = TOP_PRESSURE + above_mass[:, None] + jnp.cumsum(layer_mass, axis=1)
    top_press = bottom - layer_mass
    thickness = GAS_CONST * theta_field * (jnp.log(bottom) - jnp.log(top_press))
    depth_sum = jnp.sum(thickness, axis=1)
    below_depth = prefix_over(depth_sum, "lev", False)
    inclusive = jnp.flip(jnp.cumsum(jnp.flip(thickness, 1), axis=1), 1)
    height = (
        surface_height[:, None] + below_depth[:, None] + (inclusive - thickness) + 0.5 * thickness
    )
    fields = jnp.stack([wind_east, wind_north, flux_east, flux_north])
    fields, height = lax.optimization_barrier((fields, height))
    own_cuts = lax.dynamic_slice_in_dim(filter_cutoff, first_row, lat_rows)
    row_cuts = jnp.broadcast_to(own_cuts[None, :, None], fields.shape[:3]).reshape(-1)
    smooth = filter_rows(fields.reshape(-1, length), row_cuts).reshape(fields.shape)
    east_smooth = smooth[0]
    north_smooth = smooth[1]
    east_flux = smooth[2]
    north_flux = smooth[3]
    next_face = from_behind(north_flux[:1], "lat", -1)
    north_full = jnp.concatenate([north_flux, next_face], axis=0)
    new_mass = layer_mass - TIME_STEP * (
        jnp.roll(east_flux, -1, -1) - east_flux + (north_full[1:] - north_full[:-1])
    )
    heat_east = east_flux * face_lon(theta_field)
    heat_north = north_full * theta_faces
    new_heat = theta_field * layer_mass - TIME_STEP * (
        jnp.roll(heat_east, -1, -1) - heat_east + (heat_north[1:] - heat_north[:-1])
    )
    lower_row = from_behind(height[-1:], "lat", 1)
    height_south = jnp.concatenate([lower_row, height[:-1]], axis=0)
    new_east = east_smooth - TIME_STEP * (height - jnp.roll(height, 1, -1))
    inside = (row_ids > 0).astype(jnp.float32)[:, None, None]
    new_north = (north_smooth - TIME_STEP * (height - height_south)) * inside
    outputs = (new_east, new_north, new_mass, new_heat, height)
    return tuple(jnp.transpose(v, (1, 0, 2)) for v in outputs)


def solution(mesh):
    in_specs = (
        P("lev", "lat", None),
        P("lev", "lat", None),
        P("lev", "lat", None),
        P("lev", "lat", None),
        P("lat", None),
        P(),
    )
    out_specs = (
        P("lev", "lat", None),
        P("lev", "lat", None),
        P("lev", "lat", None),
        P("lev", "lat", None),
        P("lev", "lat", None),
    )
    return jax.shard_map(local, mesh=mesh, in_specs=in_specs, out_specs=out_specs, check_vma=False)
```

```python
import numpy as np
import jax
import jax.numpy as jnp
from jax import lax
from jax.sharding import PartitionSpec as P

TIME_STEP = 0.25
GAS_CONST = 1.0
TOP_PRESSURE = 1.0


def face_lon(values):
    return (
        37.0 * (jnp.roll(values, 1, -1) + values)
        - 8.0 * (jnp.roll(values, 2, -1) + jnp.roll(values, -1, -1))
        + (jnp.roll(values, 3, -1) + jnp.roll(values, -2, -1))
    ) / 60.0


def face_lat(padded, count):
    return (
        37.0 * (padded[2 : 2 + count] + padded[3 : 3 + count])
        - 8.0 * (padded[1 : 1 + count] + padded[4 : 4 + count])
        + (padded[0:count] + padded[5 : 5 + count])
    ) / 60.0


FACTOR_ROWS = 9
FACTOR_LANES = 128


def fft_tables(length):
    rows, lanes = FACTOR_ROWS, FACTOR_LANES
    small = np.arange(rows)
    small_phase = 2.0 * np.pi * np.outer(small, small) / rows
    low = np.arange(rows)[:, None]
    high = np.arange(lanes)[None, :]
    twist = 2.0 * np.pi * ((low * high) % length) / length
    waves = np.arange(lanes)
    wave_phase = 2.0 * np.pi * (np.outer(waves, waves) % lanes) / lanes
    wc, ws = np.cos(wave_phase), np.sin(wave_phase)
    forward = np.block([[wc, -ws], [ws, wc]]).astype(np.float32)
    inverse = np.block([[wc, ws], [-ws, wc]]).astype(np.float32)
    number = np.arange(rows)[:, None] + rows * np.arange(lanes)[None, :]
    folded = np.minimum(number, length - number)
    folded = np.concatenate([folded, folded], axis=1)[:, None, :].astype(np.int32)
    return (
        np.cos(small_phase),
        np.sin(small_phase),
        np.cos(twist).reshape(1, length).astype(np.float32),
        np.sin(twist).reshape(1, length).astype(np.float32),
        forward,
        inverse,
        folded,
    )


def filter_rows(values, cuts):
    rows, lanes = FACTOR_ROWS, FACTOR_LANES
    count, length = values.shape
    c9, s9, twc, tws, forward, inverse, folded = fft_tables(length)
    highest = lax.Precision.HIGHEST
    parts = [values[:, n * lanes : (n + 1) * lanes] for n in range(rows)]
    real_a = jnp.concatenate(
        [sum(float(c9[k, n]) * parts[n] for n in range(rows)) for k in range(rows)], axis=1
    )
    imag_a = jnp.concatenate(
        [sum(float(-s9[k, n]) * parts[n] for n in range(rows)) for k in range(rows)], axis=1
    )
    real_b = real_a * twc + imag_a * tws
    imag_b = imag_a * twc - real_a * tws
    stacked = jnp.concatenate(
        [
            jnp.concatenate(
                [real_b[:, k * lanes : (k + 1) * lanes], imag_b[:, k * lanes : (k + 1) * lanes]],
                axis=1,
            )
            for k in range(rows)
        ],
        axis=0,
    )
    spectrum = jnp.dot(stacked, forward, precision=highest)
    keep = (folded <= cuts[None, :, None]).astype(jnp.float32).reshape(rows * count, 2 * lanes)
    back = jnp.dot(spectrum * keep, inverse, precision=highest)
    real_c = jnp.concatenate([back[k * count : (k + 1) * count, :lanes] for k in range(rows)], axis=1)
    imag_c = jnp.concatenate([back[k * count : (k + 1) * count, lanes:] for k in range(rows)], axis=1)
    real_d = real_c * twc - imag_c * tws
    imag_d = imag_c * twc + real_c * tws
    real_parts = [real_d[:, k * lanes : (k + 1) * lanes] for k in range(rows)]
    imag_parts = [imag_d[:, k * lanes : (k + 1) * lanes] for k in range(rows)]
    return jnp.concatenate(
        [
            sum(
                float(c9[k, n] / length) * real_parts[k] - float(s9[k, n] / length) * imag_parts[k]
                for k in range(rows)
            )
            for n in range(rows)
        ],
        axis=1,
    )


def prefix_over(value, axis, before):
    count = lax.axis_size(axis)
    rank = lax.axis_index(axis)
    copies = jnp.broadcast_to(value, (count, *value.shape))
    pieces = lax.all_to_all(copies, axis, split_axis=0, concat_axis=0, tiled=True)
    owners = jnp.arange(count, dtype=jnp.int32)
    chosen = owners < rank if before else owners > rank
    return jnp.sum(jnp.where(chosen[:, None, None], pieces, 0.0), axis=0)


def local(wind_east, wind_north, layer_mass, theta_field, surface_height, filter_cutoff):
    levels, lat_rows, length = wind_east.shape
    wind_east, wind_north, layer_mass, theta_field = (
        jnp.transpose(v, (1, 0, 2)) for v in (wind_east, wind_north, layer_mass, theta_field)
    )
    lat_count = lax.axis_size("lat")
    lat_rank = lax.axis_index("lat")
    nlat_all = lat_rows * lat_count
    first_row = lat_rank * lat_rows
    surface = jnp.broadcast_to(surface_height[:, None], (lat_rows, levels, length))
    to_north = jnp.concatenate([layer_mass, theta_field, surface[-1:]], axis=0)
    to_south = jnp.concatenate([layer_mass, theta_field, wind_north[:1]], axis=0)
    count = lat_count
    from_south = lax.ppermute(to_north, "lat", [(i, i + 1) for i in range(count - 1)])
    from_north = lax.ppermute(to_south, "lat", [(i + 1, i) for i in range(count - 1)])
    rows = lat_rows
    mass_pad = jnp.concatenate([from_south[:rows], layer_mass, from_north[:rows]], axis=0)
    theta_pad = jnp.concatenate(
        [from_south[rows : 2 * rows], theta_field, from_north[rows : 2 * rows]], axis=0
    )
    face_rows = first_row + jnp.arange(lat_rows + 1, dtype=jnp.int32)
    coslat = jnp.sin(jnp.pi * face_rows.astype(jnp.float32) / nlat_all)[:, None, None]
    mass_faces = face_lat(mass_pad, lat_rows + 1)
    theta_faces = face_lat(theta_pad, lat_rows + 1)
    north_ext = jnp.concatenate([wind_north, from_north[2 * rows :]], axis=0)
    flux_east = wind_east * face_lon(layer_mass)
    flux_north = north_ext * mass_faces * coslat
    mass_ext = jnp.concatenate([from_south[rows - 1 : rows], layer_mass], axis=0)
    theta_ext = jnp.concatenate([from_south[2 * rows - 1 : 2 * rows], theta_field], axis=0)
    surface_ext = jnp.concatenate([from_south[2 * rows :], surface], axis=0)
    column = jnp.sum(mass_ext, axis=1)
    above_mass = prefix_over(column, "lev", True)
    bottom = TOP_PRESSURE + above_mass[:, None] + jnp.cumsum(mass_ext, axis=1)
    top_press = bottom - mass_ext
    thickness = GAS_CONST * theta_ext * (jnp.log(bottom) - jnp.log(top_press))
    depth_sum = jnp.sum(thickness, axis=1)
    below_depth = prefix_over(depth_sum, "lev", False)
    inclusive = jnp.flip(jnp.cumsum(jnp.flip(thickness, 1), axis=1), 1)
    height_ext = surface_ext + below_depth[:, None] + (inclusive - thickness) + 0.5 * thickness
    fields = jnp.concatenate([wind_east, wind_north, flux_east, flux_north], axis=0)
    fields, height_ext = lax.optimization_barrier((fields, height_ext))
    cut_rows = jnp.concatenate([face_rows[:-1], face_rows[:-1], face_rows[:-1], face_rows])
    row_cuts = jnp.broadcast_to(
        filter_cutoff[jnp.minimum(cut_rows, nlat_all - 1)][:, None], fields.shape[:2]
    ).reshape(-1)
    smooth = filter_rows(fields.reshape(-1, length), row_cuts).reshape(fields.shape)
    east_smooth = smooth[:rows]
    north_smooth = smooth[rows : 2 * rows]
    east_flux = smooth[2 * rows : 3 * rows]
    north_full = smooth[3 * rows :]
    new_mass = layer_mass - TIME_STEP * (
        jnp.roll(east_flux, -1, -1) - east_flux + (north_full[1:] - north_full[:-1])
    )
    heat_east = east_flux * face_lon(theta_field)
    heat_north = north_full * theta_faces
    new_heat = theta_field * layer_mass - TIME_STEP * (
        jnp.roll(heat_east, -1, -1) - heat_east + (heat_north[1:] - heat_north[:-1])
    )
    height = height_ext[1:]
    new_east = east_smooth - TIME_STEP * (height - jnp.roll(height, 1, -1))
    inside = (face_rows[:-1] > 0).astype(jnp.float32)[:, None, None]
    new_north = (north_smooth - TIME_STEP * (height - height_ext[:-1])) * inside
    outputs = (new_east, new_north, new_mass, new_heat, height)
    return tuple(jnp.transpose(v, (1, 0, 2)) for v in outputs)


def solution(mesh):
    in_specs = (
        P("lev", "lat", None),
        P("lev", "lat", None),
        P("lev", "lat", None),
        P("lev", "lat", None),
        P("lat", None),
        P(),
    )
    out_specs = (
        P("lev", "lat", None),
        P("lev", "lat", None),
        P("lev", "lat", None),
        P("lev", "lat", None),
        P("lev", "lat", None),
    )
    return jax.shard_map(local, mesh=mesh, in_specs=in_specs, out_specs=out_specs, check_vma=False)
```

```python
import numpy as np
import jax
import jax.numpy as jnp
from jax import lax
from jax.experimental import pallas as pl
from jax.sharding import PartitionSpec as P

TIME_STEP = 0.25
GAS_CONST = 1.0
TOP_PRESSURE = 1.0


def face_lon(values):
    return (
        37.0 * (jnp.roll(values, 1, -1) + values)
        - 8.0 * (jnp.roll(values, 2, -1) + jnp.roll(values, -1, -1))
        + (jnp.roll(values, 3, -1) + jnp.roll(values, -2, -1))
    ) / 60.0


def face_lat(padded, count):
    return (
        37.0 * (padded[2 : 2 + count] + padded[3 : 3 + count])
        - 8.0 * (padded[1 : 1 + count] + padded[4 : 4 + count])
        + (padded[0:count] + padded[5 : 5 + count])
    ) / 60.0


FACTOR_ROWS = 9
FACTOR_LANES = 128

def fft_tables(length):
    rows, lanes = FACTOR_ROWS, FACTOR_LANES
    small = np.arange(rows)
    small_phase = 2.0 * np.pi * np.outer(small, small) / rows
    low = np.arange(rows)[:, None]
    high = np.arange(lanes)[None, :]
    twist = 2.0 * np.pi * ((low * high) % length) / length
    waves = np.arange(lanes)
    wave_phase = 2.0 * np.pi * (np.outer(waves, waves) % lanes) / lanes
    wc, ws = np.cos(wave_phase), np.sin(wave_phase)
    forward = np.block([[wc, -ws], [ws, wc]]).astype(np.float32)
    inverse = np.block([[wc, ws], [-ws, wc]]).astype(np.float32)
    number = np.arange(rows)[:, None] + rows * np.arange(lanes)[None, :]
    folded = np.minimum(number, length - number)
    folded = np.concatenate([folded, folded], axis=1).astype(np.int32)
    return (np.cos(small_phase), np.sin(small_phase), np.cos(twist).astype(np.float32),
            np.sin(twist).astype(np.float32), forward, inverse, folded)

def filter_kernel(x_ref, cut_ref, twc_ref, tws_ref, fwd_ref, inv_ref, fold_ref, o_ref):
    rows, lanes = FACTOR_ROWS, FACTOR_LANES
    count, length = x_ref.shape
    c9, s9 = fft_tables(length)[:2]
    highest = lax.Precision.HIGHEST
    parts = [x_ref[:, n * lanes:(n + 1) * lanes] for n in range(rows)]
    half = rows // 2 + 1
    real_a = [sum(float(c9[k, n]) * parts[n] for n in range(rows)) for k in range(half)]
    imag_a = [sum(float(-s9[k, n]) * parts[n] for n in range(1, rows)) for k in range(half)]
    real_a += [real_a[rows - k] for k in range(half, rows)]
    imag_a += [-imag_a[rows - k] for k in range(half, rows)]
    pieces = []
    for k in range(rows):
        twc = twc_ref[k:k + 1, :]
        tws = tws_ref[k:k + 1, :]
        pieces.append(jnp.concatenate(
            [real_a[k] * twc + imag_a[k] * tws, imag_a[k] * twc - real_a[k] * tws], axis=1))
    spectrum = jnp.dot(jnp.concatenate(pieces, axis=0), fwd_ref[...], precision=highest,
                       preferred_element_type=jnp.float32)
    cuts = cut_ref[...]
    keep = jnp.concatenate(
        [(fold_ref[k:k + 1, :] <= cuts).astype(jnp.float32) for k in range(rows)], axis=0)
    back = jnp.dot(spectrum * keep, inv_ref[...], precision=highest,
                   preferred_element_type=jnp.float32)
    real_d, imag_d = [], []
    for k in range(rows):
        twc = twc_ref[k:k + 1, :]
        tws = tws_ref[k:k + 1, :]
        real_c = back[k * count:(k + 1) * count, :lanes]
        imag_c = back[k * count:(k + 1) * count, lanes:]
        real_d.append(real_c * twc - imag_c * tws)
        imag_d.append(imag_c * twc + real_c * tws)
    for n in range(rows):
        o_ref[:, n * lanes:(n + 1) * lanes] = sum(
            float(c9[k, n] / length) * real_d[k] - float(s9[k, n] / length) * imag_d[k]
            for k in range(rows))

def filter_rows(values, cuts):
    count, length = values.shape
    _, _, twc, tws, forward, inverse, folded = fft_tables(length)
    return pl.pallas_call(
        filter_kernel,
        out_shape=jax.ShapeDtypeStruct(values.shape, values.dtype),
    )(values, cuts.reshape(count, 1), jnp.asarray(twc), jnp.asarray(tws), jnp.asarray(forward),
      jnp.asarray(inverse), jnp.asarray(folded))

def prefix_over(value, axis, before):
    count = lax.axis_size(axis)
    rank = lax.axis_index(axis)
    copies = jnp.broadcast_to(value, (count, *value.shape))
    pieces = lax.all_to_all(copies, axis, split_axis=0, concat_axis=0, tiled=True)
    owners = jnp.arange(count, dtype=jnp.int32)
    chosen = owners < rank if before else owners > rank
    return jnp.sum(jnp.where(chosen[:, None, None], pieces, 0.0), axis=0)


def local(wind_east, wind_north, layer_mass, theta_field, surface_height, filter_cutoff):
    levels, lat_rows, length = wind_east.shape
    wind_east, wind_north, layer_mass, theta_field = (
        jnp.transpose(v, (1, 0, 2)) for v in (wind_east, wind_north, layer_mass, theta_field)
    )
    lat_count = lax.axis_size("lat")
    lat_rank = lax.axis_index("lat")
    nlat_all = lat_rows * lat_count
    first_row = lat_rank * lat_rows
    surface = jnp.broadcast_to(surface_height[:, None], (lat_rows, levels, length))
    to_north = jnp.concatenate([layer_mass, theta_field, surface[-1:]], axis=0)
    to_south = jnp.concatenate([layer_mass, theta_field, wind_north[:1]], axis=0)
    count = lat_count
    from_south = lax.ppermute(to_north, "lat", [(i, i + 1) for i in range(count - 1)])
    from_north = lax.ppermute(to_south, "lat", [(i + 1, i) for i in range(count - 1)])
    rows = lat_rows
    mass_pad = jnp.concatenate([from_south[:rows], layer_mass, from_north[:rows]], axis=0)
    theta_pad = jnp.concatenate(
        [from_south[rows : 2 * rows], theta_field, from_north[rows : 2 * rows]], axis=0
    )
    face_rows = first_row + jnp.arange(lat_rows + 1, dtype=jnp.int32)
    coslat = jnp.sin(jnp.pi * face_rows.astype(jnp.float32) / nlat_all)[:, None, None]
    mass_faces = face_lat(mass_pad, lat_rows + 1)
    theta_faces = face_lat(theta_pad, lat_rows + 1)
    north_ext = jnp.concatenate([wind_north, from_north[2 * rows :]], axis=0)
    flux_east = wind_east * face_lon(layer_mass)
    flux_north = north_ext * mass_faces * coslat
    mass_ext = jnp.concatenate([from_south[rows - 1 : rows], layer_mass], axis=0)
    theta_ext = jnp.concatenate([from_south[2 * rows - 1 : 2 * rows], theta_field], axis=0)
    surface_ext = jnp.concatenate([from_south[2 * rows :], surface], axis=0)
    column = jnp.sum(mass_ext, axis=1)
    above_mass = prefix_over(column, "lev", True)
    bottom = TOP_PRESSURE + above_mass[:, None] + jnp.cumsum(mass_ext, axis=1)
    top_press = bottom - mass_ext
    thickness = GAS_CONST * theta_ext * (jnp.log(bottom) - jnp.log(top_press))
    depth_sum = jnp.sum(thickness, axis=1)
    below_depth = prefix_over(depth_sum, "lev", False)
    inclusive = jnp.flip(jnp.cumsum(jnp.flip(thickness, 1), axis=1), 1)
    height_ext = surface_ext + below_depth[:, None] + (inclusive - thickness) + 0.5 * thickness
    fields = jnp.concatenate([wind_east, wind_north, flux_east, flux_north], axis=0)
    fields, height_ext = lax.optimization_barrier((fields, height_ext))
    cut_rows = jnp.concatenate([face_rows[:-1], face_rows[:-1], face_rows[:-1], face_rows])
    row_cuts = jnp.broadcast_to(
        filter_cutoff[jnp.minimum(cut_rows, nlat_all - 1)][:, None], fields.shape[:2]
    ).reshape(-1)
    smooth = filter_rows(fields.reshape(-1, length), row_cuts).reshape(fields.shape)
    east_smooth = smooth[:rows]
    north_smooth = smooth[rows : 2 * rows]
    east_flux = smooth[2 * rows : 3 * rows]
    north_full = smooth[3 * rows :]
    new_mass = layer_mass - TIME_STEP * (
        jnp.roll(east_flux, -1, -1) - east_flux + (north_full[1:] - north_full[:-1])
    )
    heat_east = east_flux * face_lon(theta_field)
    heat_north = north_full * theta_faces
    new_heat = theta_field * layer_mass - TIME_STEP * (
        jnp.roll(heat_east, -1, -1) - heat_east + (heat_north[1:] - heat_north[:-1])
    )
    height = height_ext[1:]
    new_east = east_smooth - TIME_STEP * (height - jnp.roll(height, 1, -1))
    inside = (face_rows[:-1] > 0).astype(jnp.float32)[:, None, None]
    new_north = (north_smooth - TIME_STEP * (height - height_ext[:-1])) * inside
    outputs = (new_east, new_north, new_mass, new_heat, height)
    return tuple(jnp.transpose(v, (1, 0, 2)) for v in outputs)


def solution(mesh):
    in_specs = (
        P("lev", "lat", None),
        P("lev", "lat", None),
        P("lev", "lat", None),
        P("lev", "lat", None),
        P("lat", None),
        P(),
    )
    out_specs = (
        P("lev", "lat", None),
        P("lev", "lat", None),
        P("lev", "lat", None),
        P("lev", "lat", None),
        P("lev", "lat", None),
    )
    return jax.shard_map(local, mesh=mesh, in_specs=in_specs, out_specs=out_specs, check_vma=False)
```

```python
import numpy as np
import jax
import jax.numpy as jnp
from jax import lax
from jax.experimental import pallas as pl
from jax.sharding import PartitionSpec as P

TIME_STEP = 0.25
GAS_CONST = 1.0
TOP_PRESSURE = 1.0


def face_lon(values):
    return (
        37.0 * (jnp.roll(values, 1, -1) + values)
        - 8.0 * (jnp.roll(values, 2, -1) + jnp.roll(values, -1, -1))
        + (jnp.roll(values, 3, -1) + jnp.roll(values, -2, -1))
    ) / 60.0


def face_lat(padded, count):
    return (
        37.0 * (padded[2 : 2 + count] + padded[3 : 3 + count])
        - 8.0 * (padded[1 : 1 + count] + padded[4 : 4 + count])
        + (padded[0:count] + padded[5 : 5 + count])
    ) / 60.0


FACTOR_ROWS = 9
FACTOR_LANES = 128

def fft_tables(length):
    rows, lanes = FACTOR_ROWS, FACTOR_LANES
    small = np.arange(rows)
    small_phase = 2.0 * np.pi * np.outer(small, small) / rows
    low = np.arange(rows)[:, None]
    high = np.arange(lanes)[None, :]
    twist = 2.0 * np.pi * ((low * high) % length) / length
    waves = np.arange(lanes)
    wave_phase = 2.0 * np.pi * (np.outer(waves, waves) % lanes) / lanes
    wc, ws = np.cos(wave_phase), np.sin(wave_phase)
    forward = np.block([[wc, -ws], [ws, wc]]).astype(np.float32)
    inverse = np.block([[wc, ws], [-ws, wc]]).astype(np.float32)
    number = np.arange(rows)[:, None] + rows * np.arange(lanes)[None, :]
    folded = np.minimum(number, length - number)
    folded = np.concatenate([folded, folded], axis=1).astype(np.int32)
    return (np.cos(small_phase), np.sin(small_phase), np.cos(twist).astype(np.float32),
            np.sin(twist).astype(np.float32), forward, inverse, folded)

def filter_kernel(x_ref, cut_ref, twc_ref, tws_ref, fwd_ref, inv_ref, fold_ref, o_ref):
    rows, lanes = FACTOR_ROWS, FACTOR_LANES
    count, length = x_ref.shape
    c9, s9 = fft_tables(length)[:2]
    highest = lax.Precision.HIGHEST
    half = rows // 2 + 1
    parts = [x_ref[:, n * lanes : (n + 1) * lanes] for n in range(rows)]
    pieces = []
    for k in range(half):
        real_a = sum(float(c9[k, n]) * parts[n] for n in range(rows))
        imag_a = sum(float(-s9[k, n]) * parts[n] for n in range(1, rows))
        twc = twc_ref[k : k + 1, :]
        tws = tws_ref[k : k + 1, :]
        pieces.append(
            jnp.concatenate([real_a * twc + imag_a * tws, imag_a * twc - real_a * tws], axis=1)
        )
    spectrum = jnp.dot(
        jnp.concatenate(pieces, axis=0),
        fwd_ref[...],
        precision=highest,
        preferred_element_type=jnp.float32,
    )
    cuts = cut_ref[...]
    keep = jnp.concatenate(
        [(fold_ref[k : k + 1, :] <= cuts).astype(jnp.float32) for k in range(half)], axis=0
    )
    back = jnp.dot(
        spectrum * keep, inv_ref[...], precision=highest, preferred_element_type=jnp.float32
    )
    real_d, imag_d = [], []
    for k in range(half):
        twc = twc_ref[k : k + 1, :]
        tws = tws_ref[k : k + 1, :]
        real_c = back[k * count : (k + 1) * count, :lanes]
        imag_c = back[k * count : (k + 1) * count, lanes:]
        real_d.append(real_c * twc - imag_c * tws)
        imag_d.append(imag_c * twc + real_c * tws)
    for n in range(rows):
        o_ref[:, n * lanes : (n + 1) * lanes] = float(1.0 / length) * real_d[0] + sum(
            float(2.0 * c9[k, n] / length) * real_d[k] - float(2.0 * s9[k, n] / length) * imag_d[k]
            for k in range(1, half)
        )


def filter_rows(values, cuts):
    count, length = values.shape
    _, _, twc, tws, forward, inverse, folded = fft_tables(length)
    return pl.pallas_call(
        filter_kernel,
        out_shape=jax.ShapeDtypeStruct(values.shape, values.dtype),
    )(values, cuts.reshape(count, 1), jnp.asarray(twc), jnp.asarray(tws), jnp.asarray(forward),
      jnp.asarray(inverse), jnp.asarray(folded))

def prefix_over(value, axis, before):
    count = lax.axis_size(axis)
    rank = lax.axis_index(axis)
    copies = jnp.broadcast_to(value, (count, *value.shape))
    pieces = lax.all_to_all(copies, axis, split_axis=0, concat_axis=0, tiled=True)
    owners = jnp.arange(count, dtype=jnp.int32)
    chosen = owners < rank if before else owners > rank
    return jnp.sum(jnp.where(chosen[:, None, None], pieces, 0.0), axis=0)


def local(wind_east, wind_north, layer_mass, theta_field, surface_height, filter_cutoff):
    levels, lat_rows, length = wind_east.shape
    wind_east, wind_north, layer_mass, theta_field = (
        jnp.transpose(v, (1, 0, 2)) for v in (wind_east, wind_north, layer_mass, theta_field)
    )
    lat_count = lax.axis_size("lat")
    lat_rank = lax.axis_index("lat")
    nlat_all = lat_rows * lat_count
    first_row = lat_rank * lat_rows
    surface = jnp.broadcast_to(surface_height[:, None], (lat_rows, levels, length))
    to_north = jnp.concatenate([layer_mass, theta_field, surface[-1:]], axis=0)
    to_south = jnp.concatenate([layer_mass, theta_field, wind_north[:1]], axis=0)
    count = lat_count
    from_south = lax.ppermute(to_north, "lat", [(i, i + 1) for i in range(count - 1)])
    from_north = lax.ppermute(to_south, "lat", [(i + 1, i) for i in range(count - 1)])
    rows = lat_rows
    mass_pad = jnp.concatenate([from_south[:rows], layer_mass, from_north[:rows]], axis=0)
    theta_pad = jnp.concatenate(
        [from_south[rows : 2 * rows], theta_field, from_north[rows : 2 * rows]], axis=0
    )
    face_rows = first_row + jnp.arange(lat_rows + 1, dtype=jnp.int32)
    coslat = jnp.sin(jnp.pi * face_rows.astype(jnp.float32) / nlat_all)[:, None, None]
    mass_faces = face_lat(mass_pad, lat_rows + 1)
    theta_faces = face_lat(theta_pad, lat_rows + 1)
    north_ext = jnp.concatenate([wind_north, from_north[2 * rows :]], axis=0)
    flux_east = wind_east * face_lon(layer_mass)
    flux_north = north_ext * mass_faces * coslat
    mass_ext = jnp.concatenate([from_south[rows - 1 : rows], layer_mass], axis=0)
    theta_ext = jnp.concatenate([from_south[2 * rows - 1 : 2 * rows], theta_field], axis=0)
    surface_ext = jnp.concatenate([from_south[2 * rows :], surface], axis=0)
    column = jnp.sum(mass_ext, axis=1)
    above_mass = prefix_over(column, "lev", True)
    bottom = TOP_PRESSURE + above_mass[:, None] + jnp.cumsum(mass_ext, axis=1)
    top_press = bottom - mass_ext
    thickness = GAS_CONST * theta_ext * (jnp.log(bottom) - jnp.log(top_press))
    depth_sum = jnp.sum(thickness, axis=1)
    below_depth = prefix_over(depth_sum, "lev", False)
    inclusive = jnp.flip(jnp.cumsum(jnp.flip(thickness, 1), axis=1), 1)
    height_ext = surface_ext + below_depth[:, None] + (inclusive - thickness) + 0.5 * thickness
    fields = jnp.concatenate([wind_east, wind_north, flux_east, flux_north], axis=0)
    fields, height_ext = lax.optimization_barrier((fields, height_ext))
    cut_rows = jnp.concatenate([face_rows[:-1], face_rows[:-1], face_rows[:-1], face_rows])
    row_cuts = jnp.broadcast_to(
        filter_cutoff[jnp.minimum(cut_rows, nlat_all - 1)][:, None], fields.shape[:2]
    ).reshape(-1)
    smooth = filter_rows(fields.reshape(-1, length), row_cuts).reshape(fields.shape)
    east_smooth = smooth[:rows]
    north_smooth = smooth[rows : 2 * rows]
    east_flux = smooth[2 * rows : 3 * rows]
    north_full = smooth[3 * rows :]
    new_mass = layer_mass - TIME_STEP * (
        jnp.roll(east_flux, -1, -1) - east_flux + (north_full[1:] - north_full[:-1])
    )
    heat_east = east_flux * face_lon(theta_field)
    heat_north = north_full * theta_faces
    new_heat = theta_field * layer_mass - TIME_STEP * (
        jnp.roll(heat_east, -1, -1) - heat_east + (heat_north[1:] - heat_north[:-1])
    )
    height = height_ext[1:]
    new_east = east_smooth - TIME_STEP * (height - jnp.roll(height, 1, -1))
    inside = (face_rows[:-1] > 0).astype(jnp.float32)[:, None, None]
    new_north = (north_smooth - TIME_STEP * (height - height_ext[:-1])) * inside
    outputs = (new_east, new_north, new_mass, new_heat, height)
    return tuple(jnp.transpose(v, (1, 0, 2)) for v in outputs)


def solution(mesh):
    in_specs = (
        P("lev", "lat", None),
        P("lev", "lat", None),
        P("lev", "lat", None),
        P("lev", "lat", None),
        P("lat", None),
        P(),
    )
    out_specs = (
        P("lev", "lat", None),
        P("lev", "lat", None),
        P("lev", "lat", None),
        P("lev", "lat", None),
        P("lev", "lat", None),
    )
    return jax.shard_map(local, mesh=mesh, in_specs=in_specs, out_specs=out_specs, check_vma=False)
```

```python
import numpy as np
import jax
import jax.numpy as jnp
from jax import lax
from jax.experimental import pallas as pl
from jax.sharding import PartitionSpec as P

TIME_STEP = 0.25
GAS_CONST = 1.0
TOP_PRESSURE = 1.0


def face_lon(values):
    return (
        37.0 * (jnp.roll(values, 1, -1) + values)
        - 8.0 * (jnp.roll(values, 2, -1) + jnp.roll(values, -1, -1))
        + (jnp.roll(values, 3, -1) + jnp.roll(values, -2, -1))
    ) / 60.0


def face_lat(padded, count):
    return (
        37.0 * (padded[2 : 2 + count] + padded[3 : 3 + count])
        - 8.0 * (padded[1 : 1 + count] + padded[4 : 4 + count])
        + (padded[0:count] + padded[5 : 5 + count])
    ) / 60.0


FACTOR_ROWS = 9
FACTOR_LANES = 128

def fft_tables(length):
    rows, lanes = FACTOR_ROWS, FACTOR_LANES
    small = np.arange(rows)
    small_phase = 2.0 * np.pi * np.outer(small, small) / rows
    low = np.arange(rows)[:, None]
    high = np.arange(lanes)[None, :]
    twist = 2.0 * np.pi * ((low * high) % length) / length
    waves = np.arange(lanes)
    wave_phase = 2.0 * np.pi * (np.outer(waves, waves) % lanes) / lanes
    wc, ws = np.cos(wave_phase), np.sin(wave_phase)
    forward = np.block([[wc, -ws], [ws, wc]]).astype(np.float32)
    inverse = np.block([[wc, ws], [-ws, wc]]).astype(np.float32)
    number = np.arange(rows)[:, None] + rows * np.arange(lanes)[None, :]
    folded = np.minimum(number, length - number)
    folded = np.concatenate([folded, folded], axis=1).astype(np.int32)
    return (np.cos(small_phase), np.sin(small_phase), np.cos(twist).astype(np.float32),
            np.sin(twist).astype(np.float32), forward, inverse, folded)

def filter_kernel(x_ref, cut_ref, twc_ref, tws_ref, fwd_ref, inv_ref, fold_ref, o_ref):
    rows, lanes = FACTOR_ROWS, FACTOR_LANES
    count, length = x_ref.shape
    c9, s9 = fft_tables(length)[:2]
    highest = lax.Precision.HIGHEST
    half = rows // 2 + 1
    parts = [x_ref[:, n * lanes : (n + 1) * lanes] for n in range(rows)]
    pieces = []
    for k in range(half):
        real_a = sum(float(c9[k, n]) * parts[n] for n in range(rows))
        imag_a = sum(float(-s9[k, n]) * parts[n] for n in range(1, rows))
        twc = twc_ref[k : k + 1, :]
        tws = tws_ref[k : k + 1, :]
        pieces.append(
            jnp.concatenate([real_a * twc + imag_a * tws, imag_a * twc - real_a * tws], axis=1)
        )
    spectrum = jnp.dot(
        jnp.concatenate(pieces, axis=0),
        fwd_ref[...],
        precision=highest,
        preferred_element_type=jnp.float32,
    )
    cuts = cut_ref[...]
    keep = jnp.concatenate(
        [(fold_ref[k : k + 1, :] <= cuts).astype(jnp.float32) for k in range(half)], axis=0
    )
    back = jnp.dot(
        spectrum * keep, inv_ref[...], precision=highest, preferred_element_type=jnp.float32
    )
    real_d, imag_d = [], []
    for k in range(half):
        twc = twc_ref[k : k + 1, :]
        tws = tws_ref[k : k + 1, :]
        real_c = back[k * count : (k + 1) * count, :lanes]
        imag_c = back[k * count : (k + 1) * count, lanes:]
        real_d.append(real_c * twc - imag_c * tws)
        imag_d.append(imag_c * twc + real_c * tws)
    for n in range(rows):
        o_ref[:, n * lanes : (n + 1) * lanes] = float(1.0 / length) * real_d[0] + sum(
            float(2.0 * c9[k, n] / length) * real_d[k] - float(2.0 * s9[k, n] / length) * imag_d[k]
            for k in range(1, half)
        )


def filter_rows(values, cuts):
    count, length = values.shape
    _, _, twc, tws, forward, inverse, folded = fft_tables(length)
    return pl.pallas_call(
        filter_kernel,
        out_shape=jax.ShapeDtypeStruct(values.shape, values.dtype),
    )(values, cuts.reshape(count, 1), jnp.asarray(twc), jnp.asarray(tws), jnp.asarray(forward),
      jnp.asarray(inverse), jnp.asarray(folded))

def prefix_over(value, axis, before):
    count = lax.axis_size(axis)
    rank = lax.axis_index(axis)
    copies = jnp.broadcast_to(value, (count, *value.shape))
    pieces = lax.all_to_all(copies, axis, split_axis=0, concat_axis=0, tiled=True)
    owners = jnp.arange(count, dtype=jnp.int32)
    chosen = owners < rank if before else owners > rank
    return jnp.sum(jnp.where(chosen[:, None, None], pieces, 0.0), axis=0)


def local(wind_east, wind_north, layer_mass, theta_field, surface_height, filter_cutoff):
    levels, lat_rows, length = wind_east.shape
    wind_east, wind_north, layer_mass, theta_field = (
        jnp.transpose(v, (1, 0, 2)) for v in (wind_east, wind_north, layer_mass, theta_field)
    )
    lat_count = lax.axis_size("lat")
    lat_rank = lax.axis_index("lat")
    nlat_all = lat_rows * lat_count
    first_row = lat_rank * lat_rows
    surface = jnp.broadcast_to(surface_height[:, None], (lat_rows, levels, length))
    to_north = jnp.concatenate([layer_mass, theta_field, surface[-1:]], axis=0)
    to_south = jnp.concatenate([layer_mass, theta_field, wind_north[:1]], axis=0)
    count = lat_count
    from_south = lax.ppermute(to_north, "lat", [(i, i + 1) for i in range(count - 1)])
    from_north = lax.ppermute(to_south, "lat", [(i + 1, i) for i in range(count - 1)])
    rows = lat_rows
    mass_pad = jnp.concatenate([from_south[:rows], layer_mass, from_north[:rows]], axis=0)
    theta_pad = jnp.concatenate(
        [from_south[rows : 2 * rows], theta_field, from_north[rows : 2 * rows]], axis=0
    )
    face_rows = first_row + jnp.arange(lat_rows + 1, dtype=jnp.int32)
    coslat = jnp.sin(jnp.pi * face_rows.astype(jnp.float32) / nlat_all)[:, None, None]
    mass_faces = face_lat(mass_pad, lat_rows + 1)
    theta_faces = face_lat(theta_pad, lat_rows + 1)
    north_ext = jnp.concatenate([wind_north, from_north[2 * rows :]], axis=0)
    flux_east = wind_east * face_lon(layer_mass)
    flux_north = north_ext * mass_faces * coslat
    mass_ext = jnp.concatenate([from_south[rows - 1 : rows], layer_mass], axis=0)
    theta_ext = jnp.concatenate([from_south[2 * rows - 1 : 2 * rows], theta_field], axis=0)
    surface_ext = jnp.concatenate([from_south[2 * rows :], surface], axis=0)
    column = jnp.sum(mass_ext, axis=1)
    above_mass = prefix_over(column, "lev", True)
    bottom = TOP_PRESSURE + above_mass[:, None] + jnp.cumsum(mass_ext, axis=1)
    top_press = bottom - mass_ext
    thickness = GAS_CONST * theta_ext * (jnp.log(bottom) - jnp.log(top_press))
    depth_sum = jnp.sum(thickness, axis=1)
    below_depth = prefix_over(depth_sum, "lev", False)
    inclusive = jnp.flip(jnp.cumsum(jnp.flip(thickness, 1), axis=1), 1)
    height_ext = surface_ext + below_depth[:, None] + (inclusive - thickness) + 0.5 * thickness
    fields = jnp.concatenate([wind_east, wind_north, flux_east, flux_north], axis=0)
    fields, height_ext = lax.optimization_barrier((fields, height_ext))
    cut_rows = jnp.concatenate([face_rows[:-1], face_rows[:-1], face_rows[:-1], face_rows])
    row_cuts = jnp.broadcast_to(
        filter_cutoff[jnp.minimum(cut_rows, nlat_all - 1)][:, None], fields.shape[:2]
    ).reshape(-1)
    flat = fields.reshape(-1, length)
    smooth = lax.cond(
        jnp.any(row_cuts < length // 2),
        filter_rows,
        lambda values, cuts: values,
        flat,
        row_cuts,
    ).reshape(fields.shape)
    east_smooth = smooth[:rows]
    north_smooth = smooth[rows : 2 * rows]
    east_flux = smooth[2 * rows : 3 * rows]
    north_full = smooth[3 * rows :]
    new_mass = layer_mass - TIME_STEP * (
        jnp.roll(east_flux, -1, -1) - east_flux + (north_full[1:] - north_full[:-1])
    )
    heat_east = east_flux * face_lon(theta_field)
    heat_north = north_full * theta_faces
    new_heat = theta_field * layer_mass - TIME_STEP * (
        jnp.roll(heat_east, -1, -1) - heat_east + (heat_north[1:] - heat_north[:-1])
    )
    height = height_ext[1:]
    new_east = east_smooth - TIME_STEP * (height - jnp.roll(height, 1, -1))
    inside = (face_rows[:-1] > 0).astype(jnp.float32)[:, None, None]
    new_north = (north_smooth - TIME_STEP * (height - height_ext[:-1])) * inside
    outputs = (new_east, new_north, new_mass, new_heat, height)
    return tuple(jnp.transpose(v, (1, 0, 2)) for v in outputs)


def solution(mesh):
    in_specs = (
        P("lev", "lat", None),
        P("lev", "lat", None),
        P("lev", "lat", None),
        P("lev", "lat", None),
        P("lat", None),
        P(),
    )
    out_specs = (
        P("lev", "lat", None),
        P("lev", "lat", None),
        P("lev", "lat", None),
        P("lev", "lat", None),
        P("lev", "lat", None),
    )
    return jax.shard_map(local, mesh=mesh, in_specs=in_specs, out_specs=out_specs, check_vma=False)
```

```python
import numpy as np
import jax
import jax.numpy as jnp
from jax import lax
from jax.experimental import pallas as pl
from jax.sharding import PartitionSpec as P

TIME_STEP = 0.25
GAS_CONST = 1.0
TOP_PRESSURE = 1.0


def face_lon(values):
    return (
        37.0 * (jnp.roll(values, 1, -1) + values)
        - 8.0 * (jnp.roll(values, 2, -1) + jnp.roll(values, -1, -1))
        + (jnp.roll(values, 3, -1) + jnp.roll(values, -2, -1))
    ) / 60.0


def face_lat(padded, count):
    return (
        37.0 * (padded[2 : 2 + count] + padded[3 : 3 + count])
        - 8.0 * (padded[1 : 1 + count] + padded[4 : 4 + count])
        + (padded[0:count] + padded[5 : 5 + count])
    ) / 60.0


FACTOR_ROWS = 9
FACTOR_LANES = 128

def fft_tables(length):
    rows, lanes = FACTOR_ROWS, FACTOR_LANES
    small = np.arange(rows)
    small_phase = 2.0 * np.pi * np.outer(small, small) / rows
    low = np.arange(rows)[:, None]
    high = np.arange(lanes)[None, :]
    twist = 2.0 * np.pi * ((low * high) % length) / length
    waves = np.arange(lanes)
    wave_phase = 2.0 * np.pi * (np.outer(waves, waves) % lanes) / lanes
    wc, ws = np.cos(wave_phase), np.sin(wave_phase)
    forward = np.block([[wc, -ws], [ws, wc]]).astype(np.float32)
    inverse = np.block([[wc, ws], [-ws, wc]]).astype(np.float32)
    number = np.arange(rows)[:, None] + rows * np.arange(lanes)[None, :]
    folded = np.minimum(number, length - number)
    folded = np.concatenate([folded, folded], axis=1).astype(np.int32)
    return (np.cos(small_phase), np.sin(small_phase), np.cos(twist).astype(np.float32),
            np.sin(twist).astype(np.float32), forward, inverse, folded)

def filter_kernel(x_ref, cut_ref, twc_ref, tws_ref, fwd_ref, inv_ref, fold_ref, o_ref):
    rows, lanes = FACTOR_ROWS, FACTOR_LANES
    count, length = x_ref.shape
    c9, s9 = fft_tables(length)[:2]
    highest = lax.Precision.HIGHEST
    half = rows // 2 + 1
    parts = [x_ref[:, n * lanes : (n + 1) * lanes] for n in range(rows)]
    pieces = []
    for k in range(half):
        real_a = sum(float(c9[k, n]) * parts[n] for n in range(rows))
        imag_a = sum(float(-s9[k, n]) * parts[n] for n in range(1, rows))
        twc = twc_ref[k : k + 1, :]
        tws = tws_ref[k : k + 1, :]
        pieces.append(
            jnp.concatenate([real_a * twc + imag_a * tws, imag_a * twc - real_a * tws], axis=1)
        )
    spectrum = jnp.dot(
        jnp.concatenate(pieces, axis=0),
        fwd_ref[...],
        precision=highest,
        preferred_element_type=jnp.float32,
    )
    cuts = cut_ref[...]
    keep = jnp.concatenate(
        [(fold_ref[k : k + 1, :] <= cuts).astype(jnp.float32) for k in range(half)], axis=0
    )
    back = jnp.dot(
        spectrum * keep, inv_ref[...], precision=highest, preferred_element_type=jnp.float32
    )
    real_d, imag_d = [], []
    for k in range(half):
        twc = twc_ref[k : k + 1, :]
        tws = tws_ref[k : k + 1, :]
        real_c = back[k * count : (k + 1) * count, :lanes]
        imag_c = back[k * count : (k + 1) * count, lanes:]
        real_d.append(real_c * twc - imag_c * tws)
        imag_d.append(imag_c * twc + real_c * tws)
    for n in range(rows):
        o_ref[:, n * lanes : (n + 1) * lanes] = float(1.0 / length) * real_d[0] + sum(
            float(2.0 * c9[k, n] / length) * real_d[k] - float(2.0 * s9[k, n] / length) * imag_d[k]
            for k in range(1, half)
        )


def filter_rows(values, cuts):
    count, length = values.shape
    _, _, twc, tws, forward, inverse, folded = fft_tables(length)
    return pl.pallas_call(
        filter_kernel,
        out_shape=jax.ShapeDtypeStruct(values.shape, values.dtype),
    )(values, cuts.reshape(count, 1), jnp.asarray(twc), jnp.asarray(tws), jnp.asarray(forward),
      jnp.asarray(inverse), jnp.asarray(folded))

def prefix_over(value, axis, before):
    count = lax.axis_size(axis)
    total = value
    step = 1
    while step < count:
        if before:
            route = [(i, i + step) for i in range(count - step)]
        else:
            route = [(i + step, i) for i in range(count - step)]
        total = total + lax.ppermute(total, axis, route)
        step *= 2
    return total - value


def local(wind_east, wind_north, layer_mass, theta_field, surface_height, filter_cutoff):
    levels, lat_rows, length = wind_east.shape
    wind_east, wind_north, layer_mass, theta_field = (
        jnp.transpose(v, (1, 0, 2)) for v in (wind_east, wind_north, layer_mass, theta_field)
    )
    lat_count = lax.axis_size("lat")
    lat_rank = lax.axis_index("lat")
    nlat_all = lat_rows * lat_count
    first_row = lat_rank * lat_rows
    surface = jnp.broadcast_to(surface_height[:, None], (lat_rows, levels, length))
    to_north = jnp.concatenate([layer_mass, theta_field, surface[-1:]], axis=0)
    to_south = jnp.concatenate([layer_mass, theta_field, wind_north[:1]], axis=0)
    count = lat_count
    from_south = lax.ppermute(to_north, "lat", [(i, i + 1) for i in range(count - 1)])
    from_north = lax.ppermute(to_south, "lat", [(i + 1, i) for i in range(count - 1)])
    rows = lat_rows
    mass_pad = jnp.concatenate([from_south[:rows], layer_mass, from_north[:rows]], axis=0)
    theta_pad = jnp.concatenate(
        [from_south[rows : 2 * rows], theta_field, from_north[rows : 2 * rows]], axis=0
    )
    face_rows = first_row + jnp.arange(lat_rows + 1, dtype=jnp.int32)
    coslat = jnp.sin(jnp.pi * face_rows.astype(jnp.float32) / nlat_all)[:, None, None]
    mass_faces = face_lat(mass_pad, lat_rows + 1)
    theta_faces = face_lat(theta_pad, lat_rows + 1)
    north_ext = jnp.concatenate([wind_north, from_north[2 * rows :]], axis=0)
    flux_east = wind_east * face_lon(layer_mass)
    flux_north = north_ext * mass_faces * coslat
    mass_ext = jnp.concatenate([from_south[rows - 1 : rows], layer_mass], axis=0)
    theta_ext = jnp.concatenate([from_south[2 * rows - 1 : 2 * rows], theta_field], axis=0)
    surface_ext = jnp.concatenate([from_south[2 * rows :], surface], axis=0)
    column = jnp.sum(mass_ext, axis=1)
    above_mass = prefix_over(column, "lev", True)
    bottom = TOP_PRESSURE + above_mass[:, None] + jnp.cumsum(mass_ext, axis=1)
    top_press = bottom - mass_ext
    thickness = GAS_CONST * theta_ext * (jnp.log(bottom) - jnp.log(top_press))
    depth_sum = jnp.sum(thickness, axis=1)
    below_depth = prefix_over(depth_sum, "lev", False)
    inclusive = jnp.flip(jnp.cumsum(jnp.flip(thickness, 1), axis=1), 1)
    height_ext = surface_ext + below_depth[:, None] + (inclusive - thickness) + 0.5 * thickness
    fields = jnp.concatenate([wind_east, wind_north, flux_east, flux_north], axis=0)
    fields, height_ext = lax.optimization_barrier((fields, height_ext))
    cut_rows = jnp.concatenate([face_rows[:-1], face_rows[:-1], face_rows[:-1], face_rows])
    row_cuts = jnp.broadcast_to(
        filter_cutoff[jnp.minimum(cut_rows, nlat_all - 1)][:, None], fields.shape[:2]
    ).reshape(-1)
    flat = fields.reshape(-1, length)
    smooth = lax.cond(
        jnp.any(row_cuts < length // 2),
        filter_rows,
        lambda values, cuts: values,
        flat,
        row_cuts,
    ).reshape(fields.shape)
    east_smooth = smooth[:rows]
    north_smooth = smooth[rows : 2 * rows]
    east_flux = smooth[2 * rows : 3 * rows]
    north_full = smooth[3 * rows :]
    new_mass = layer_mass - TIME_STEP * (
        jnp.roll(east_flux, -1, -1) - east_flux + (north_full[1:] - north_full[:-1])
    )
    heat_east = east_flux * face_lon(theta_field)
    heat_north = north_full * theta_faces
    new_heat = theta_field * layer_mass - TIME_STEP * (
        jnp.roll(heat_east, -1, -1) - heat_east + (heat_north[1:] - heat_north[:-1])
    )
    height = height_ext[1:]
    new_east = east_smooth - TIME_STEP * (height - jnp.roll(height, 1, -1))
    inside = (face_rows[:-1] > 0).astype(jnp.float32)[:, None, None]
    new_north = (north_smooth - TIME_STEP * (height - height_ext[:-1])) * inside
    outputs = (new_east, new_north, new_mass, new_heat, height)
    return tuple(jnp.transpose(v, (1, 0, 2)) for v in outputs)


def solution(mesh):
    in_specs = (
        P("lev", "lat", None),
        P("lev", "lat", None),
        P("lev", "lat", None),
        P("lev", "lat", None),
        P("lat", None),
        P(),
    )
    out_specs = (
        P("lev", "lat", None),
        P("lev", "lat", None),
        P("lev", "lat", None),
        P("lev", "lat", None),
        P("lev", "lat", None),
    )
    return jax.shard_map(local, mesh=mesh, in_specs=in_specs, out_specs=out_specs, check_vma=False)
```

```python
import numpy as np
import jax
import jax.numpy as jnp
from jax import lax
from jax.experimental import pallas as pl
from jax.sharding import PartitionSpec as P

TIME_STEP = 0.25
GAS_CONST = 1.0
TOP_PRESSURE = 1.0


def face_lon(values):
    return (
        37.0 * (jnp.roll(values, 1, -1) + values)
        - 8.0 * (jnp.roll(values, 2, -1) + jnp.roll(values, -1, -1))
        + (jnp.roll(values, 3, -1) + jnp.roll(values, -2, -1))
    ) / 60.0


def face_lat(padded, count):
    return (
        37.0 * (padded[2 : 2 + count] + padded[3 : 3 + count])
        - 8.0 * (padded[1 : 1 + count] + padded[4 : 4 + count])
        + (padded[0:count] + padded[5 : 5 + count])
    ) / 60.0


FACTOR_ROWS = 9
FACTOR_LANES = 128

def fft_tables(length):
    rows, lanes = FACTOR_ROWS, FACTOR_LANES
    small = np.arange(rows)
    small_phase = 2.0 * np.pi * np.outer(small, small) / rows
    low = np.arange(rows)[:, None]
    high = np.arange(lanes)[None, :]
    twist = 2.0 * np.pi * ((low * high) % length) / length
    waves = np.arange(lanes)
    wave_phase = 2.0 * np.pi * (np.outer(waves, waves) % lanes) / lanes
    wc, ws = np.cos(wave_phase), np.sin(wave_phase)
    forward = np.block([[wc, -ws], [ws, wc]]).astype(np.float32)
    inverse = np.block([[wc, ws], [-ws, wc]]).astype(np.float32)
    number = np.arange(rows)[:, None] + rows * np.arange(lanes)[None, :]
    folded = np.minimum(number, length - number)
    folded = np.concatenate([folded, folded], axis=1).astype(np.int32)
    return (np.cos(small_phase), np.sin(small_phase), np.cos(twist).astype(np.float32),
            np.sin(twist).astype(np.float32), forward, inverse, folded)

def filter_kernel(x_ref, cut_ref, twc_ref, tws_ref, fwd_ref, inv_ref, fold_ref, o_ref):
    rows, lanes = FACTOR_ROWS, FACTOR_LANES
    count, length = x_ref.shape
    c9, s9 = fft_tables(length)[:2]
    highest = lax.Precision.HIGHEST
    half = rows // 2 + 1
    parts = [x_ref[:, n * lanes : (n + 1) * lanes] for n in range(rows)]
    pieces = []
    for k in range(half):
        real_a = sum(float(c9[k, n]) * parts[n] for n in range(rows))
        imag_a = sum(float(-s9[k, n]) * parts[n] for n in range(1, rows))
        twc = twc_ref[k : k + 1, :]
        tws = tws_ref[k : k + 1, :]
        pieces.append(
            jnp.concatenate([real_a * twc + imag_a * tws, imag_a * twc - real_a * tws], axis=1)
        )
    spectrum = jnp.dot(
        jnp.concatenate(pieces, axis=0),
        fwd_ref[...],
        precision=highest,
        preferred_element_type=jnp.float32,
    )
    cuts = cut_ref[...]
    keep = jnp.concatenate(
        [(fold_ref[k : k + 1, :] <= cuts).astype(jnp.float32) for k in range(half)], axis=0
    )
    back = jnp.dot(
        spectrum * keep, inv_ref[...], precision=highest, preferred_element_type=jnp.float32
    )
    real_d, imag_d = [], []
    for k in range(half):
        twc = twc_ref[k : k + 1, :]
        tws = tws_ref[k : k + 1, :]
        real_c = back[k * count : (k + 1) * count, :lanes]
        imag_c = back[k * count : (k + 1) * count, lanes:]
        real_d.append(real_c * twc - imag_c * tws)
        imag_d.append(imag_c * twc + real_c * tws)
    for n in range(rows):
        o_ref[:, n * lanes : (n + 1) * lanes] = float(1.0 / length) * real_d[0] + sum(
            float(2.0 * c9[k, n] / length) * real_d[k] - float(2.0 * s9[k, n] / length) * imag_d[k]
            for k in range(1, half)
        )


def filter_rows(values, cuts):
    count, length = values.shape
    _, _, twc, tws, forward, inverse, folded = fft_tables(length)
    return pl.pallas_call(
        filter_kernel,
        out_shape=jax.ShapeDtypeStruct(values.shape, values.dtype),
    )(values, cuts.reshape(count, 1), jnp.asarray(twc), jnp.asarray(tws), jnp.asarray(forward),
      jnp.asarray(inverse), jnp.asarray(folded))

def prefix_over(value, axis, before):
    count = lax.axis_size(axis)
    rank = lax.axis_index(axis)
    copies = jnp.broadcast_to(value, (count, *value.shape))
    pieces = lax.all_to_all(copies, axis, split_axis=0, concat_axis=0, tiled=True)
    owners = jnp.arange(count, dtype=jnp.int32)
    chosen = owners < rank if before else owners > rank
    return jnp.sum(jnp.where(chosen[:, None, None], pieces, 0.0), axis=0)


def local(wind_east, wind_north, layer_mass, theta_field, surface_height, filter_cutoff):
    levels, lat_rows, length = wind_east.shape
    wind_east, wind_north, layer_mass, theta_field = (
        jnp.transpose(v, (1, 0, 2)) for v in (wind_east, wind_north, layer_mass, theta_field)
    )
    lat_count = lax.axis_size("lat")
    lat_rank = lax.axis_index("lat")
    nlat_all = lat_rows * lat_count
    first_row = lat_rank * lat_rows
    surface = jnp.broadcast_to(surface_height[:, None], (lat_rows, levels, length))
    to_north = jnp.concatenate([layer_mass, theta_field, surface[-1:]], axis=0)
    to_south = jnp.concatenate([layer_mass, theta_field, wind_north[:1]], axis=0)
    count = lat_count
    from_south = lax.ppermute(to_north, "lat", [(i, i + 1) for i in range(count - 1)])
    from_north = lax.ppermute(to_south, "lat", [(i + 1, i) for i in range(count - 1)])
    rows = lat_rows
    mass_pad = jnp.concatenate([from_south[:rows], layer_mass, from_north[:rows]], axis=0)
    theta_pad = jnp.concatenate(
        [from_south[rows : 2 * rows], theta_field, from_north[rows : 2 * rows]], axis=0
    )
    face_rows = first_row + jnp.arange(lat_rows + 1, dtype=jnp.int32)
    coslat = jnp.sin(jnp.pi * face_rows.astype(jnp.float32) / nlat_all)[:, None, None]
    mass_faces = face_lat(mass_pad, lat_rows + 1)
    theta_faces = face_lat(theta_pad, lat_rows + 1)
    north_ext = jnp.concatenate([wind_north, from_north[2 * rows :]], axis=0)
    flux_east = wind_east * face_lon(layer_mass)
    flux_north = north_ext * mass_faces * coslat
    mass_ext = jnp.concatenate([from_south[rows - 1 : rows], layer_mass], axis=0)
    theta_ext = jnp.concatenate([from_south[2 * rows - 1 : 2 * rows], theta_field], axis=0)
    surface_ext = jnp.concatenate([from_south[2 * rows :], surface], axis=0)
    column = jnp.sum(mass_ext, axis=1)
    above_mass = prefix_over(column, "lev", True)
    bottom = TOP_PRESSURE + above_mass[:, None] + jnp.cumsum(mass_ext, axis=1)
    top_press = bottom - mass_ext
    thickness = GAS_CONST * theta_ext * (jnp.log(bottom) - jnp.log(top_press))
    depth_sum = jnp.sum(thickness, axis=1)
    below_depth = prefix_over(depth_sum, "lev", False)
    inclusive = jnp.flip(jnp.cumsum(jnp.flip(thickness, 1), axis=1), 1)
    height_ext = surface_ext + below_depth[:, None] + (inclusive - thickness) + 0.5 * thickness
    early = jnp.concatenate([wind_east, wind_north, flux_east], axis=0)
    early_cuts = jnp.broadcast_to(
        filter_cutoff[jnp.minimum(face_rows[:-1], nlat_all - 1)][None, :, None],
        (3, lat_rows, levels),
    ).reshape(-1)
    smooth = filter_rows(early.reshape(-1, length), early_cuts).reshape(early.shape)
    flux_north, height_ext = lax.optimization_barrier((flux_north, height_ext))
    late_cuts = jnp.broadcast_to(
        filter_cutoff[jnp.minimum(face_rows, nlat_all - 1)][:, None], flux_north.shape[:2]
    ).reshape(-1)
    north_full = filter_rows(flux_north.reshape(-1, length), late_cuts).reshape(flux_north.shape)
    east_smooth = smooth[:rows]
    north_smooth = smooth[rows : 2 * rows]
    east_flux = smooth[2 * rows : 3 * rows]
    new_mass = layer_mass - TIME_STEP * (
        jnp.roll(east_flux, -1, -1) - east_flux + (north_full[1:] - north_full[:-1])
    )
    heat_east = east_flux * face_lon(theta_field)
    heat_north = north_full * theta_faces
    new_heat = theta_field * layer_mass - TIME_STEP * (
        jnp.roll(heat_east, -1, -1) - heat_east + (heat_north[1:] - heat_north[:-1])
    )
    height = height_ext[1:]
    new_east = east_smooth - TIME_STEP * (height - jnp.roll(height, 1, -1))
    inside = (face_rows[:-1] > 0).astype(jnp.float32)[:, None, None]
    new_north = (north_smooth - TIME_STEP * (height - height_ext[:-1])) * inside
    outputs = (new_east, new_north, new_mass, new_heat, height)
    return tuple(jnp.transpose(v, (1, 0, 2)) for v in outputs)


def solution(mesh):
    in_specs = (
        P("lev", "lat", None),
        P("lev", "lat", None),
        P("lev", "lat", None),
        P("lev", "lat", None),
        P("lat", None),
        P(),
    )
    out_specs = (
        P("lev", "lat", None),
        P("lev", "lat", None),
        P("lev", "lat", None),
        P("lev", "lat", None),
        P("lev", "lat", None),
    )
    return jax.shard_map(local, mesh=mesh, in_specs=in_specs, out_specs=out_specs, check_vma=False)
```

```python
import numpy as np
import jax
import jax.numpy as jnp
from jax import lax
from jax.experimental import pallas as pl
from jax.experimental.pallas import tpu as pltpu
from jax.sharding import PartitionSpec as P

TIME_STEP = 0.25
GAS_CONST = 1.0
TOP_PRESSURE = 1.0


def face_lon(values):
    return (
        37.0 * (jnp.roll(values, 1, -1) + values)
        - 8.0 * (jnp.roll(values, 2, -1) + jnp.roll(values, -1, -1))
        + (jnp.roll(values, 3, -1) + jnp.roll(values, -2, -1))
    ) / 60.0


def face_lat(padded, count):
    return (
        37.0 * (padded[2 : 2 + count] + padded[3 : 3 + count])
        - 8.0 * (padded[1 : 1 + count] + padded[4 : 4 + count])
        + (padded[0:count] + padded[5 : 5 + count])
    ) / 60.0


FACTOR_ROWS = 9
FACTOR_LANES = 128

def fft_tables(length):
    rows, lanes = FACTOR_ROWS, FACTOR_LANES
    small = np.arange(rows)
    small_phase = 2.0 * np.pi * np.outer(small, small) / rows
    low = np.arange(rows)[:, None]
    high = np.arange(lanes)[None, :]
    twist = 2.0 * np.pi * ((low * high) % length) / length
    waves = np.arange(lanes)
    wave_phase = 2.0 * np.pi * (np.outer(waves, waves) % lanes) / lanes
    wc, ws = np.cos(wave_phase), np.sin(wave_phase)
    forward = np.block([[wc, -ws], [ws, wc]]).astype(np.float32)
    inverse = np.block([[wc, ws], [-ws, wc]]).astype(np.float32)
    number = np.arange(rows)[:, None] + rows * np.arange(lanes)[None, :]
    folded = np.minimum(number, length - number)
    folded = np.concatenate([folded, folded], axis=1).astype(np.int32)
    return (np.cos(small_phase), np.sin(small_phase), np.cos(twist).astype(np.float32),
            np.sin(twist).astype(np.float32), forward, inverse, folded)

def filter_kernel(
    x_ref, cut_ref, twc_ref, tws_ref, fwd_ref, inv_ref, fold_ref,
    mass_ref, theta_ref, lon_ref, lat_ref, height_ref, inside_ref,
    east_ref, north_ref, new_mass_ref, new_heat_ref, out_height_ref, y_ref,
):
    rows, lanes = FACTOR_ROWS, FACTOR_LANES
    count, length = x_ref.shape
    c9, s9 = fft_tables(length)[:2]
    highest = lax.Precision.HIGHEST
    half = rows // 2 + 1
    parts = [x_ref[:, n * lanes : (n + 1) * lanes] for n in range(rows)]
    pieces = []
    for k in range(half):
        real_a = sum(float(c9[k, n]) * parts[n] for n in range(rows))
        imag_a = sum(float(-s9[k, n]) * parts[n] for n in range(1, rows))
        twc = twc_ref[k : k + 1, :]
        tws = tws_ref[k : k + 1, :]
        pieces.append(
            jnp.concatenate([real_a * twc + imag_a * tws, imag_a * twc - real_a * tws], axis=1)
        )
    spectrum = jnp.dot(
        jnp.concatenate(pieces, axis=0),
        fwd_ref[...],
        precision=highest,
        preferred_element_type=jnp.float32,
    )
    cuts = cut_ref[...]
    keep = jnp.concatenate(
        [(fold_ref[k : k + 1, :] <= cuts).astype(jnp.float32) for k in range(half)], axis=0
    )
    back = jnp.dot(
        spectrum * keep, inv_ref[...], precision=highest, preferred_element_type=jnp.float32
    )
    real_d, imag_d = [], []
    for k in range(half):
        twc = twc_ref[k : k + 1, :]
        tws = tws_ref[k : k + 1, :]
        real_c = back[k * count : (k + 1) * count, :lanes]
        imag_c = back[k * count : (k + 1) * count, lanes:]
        real_d.append(real_c * twc - imag_c * tws)
        imag_d.append(imag_c * twc + real_c * tws)
    for n in range(rows):
        y_ref[:, n * lanes : (n + 1) * lanes] = float(1.0 / length) * real_d[0] + sum(
            float(2.0 * c9[k, n] / length) * real_d[k] - float(2.0 * s9[k, n] / length) * imag_d[k]
            for k in range(1, half)
        )
    block, _ = mass_ref.shape
    step = count - 4 * block
    east_smooth = y_ref[0:block, :]
    north_smooth = y_ref[block : 2 * block, :]
    east_flux = y_ref[2 * block : 3 * block, :]
    north_low = y_ref[3 * block : 4 * block, :]
    north_high = y_ref[3 * block + step : count, :]
    mass = mass_ref[...]
    theta = theta_ref[...]
    new_mass_ref[...] = mass - TIME_STEP * (
        pltpu.roll(east_flux, length - 1, 1) - east_flux + (north_high - north_low)
    )
    heat_east = east_flux * lon_ref[...]
    heat_low = north_low * lat_ref[0:block, :]
    heat_high = north_high * lat_ref[step : step + block, :]
    new_heat_ref[...] = theta * mass - TIME_STEP * (
        pltpu.roll(heat_east, length - 1, 1) - heat_east + (heat_high - heat_low)
    )
    height = height_ref[step : step + block, :]
    south = height_ref[0:block, :]
    out_height_ref[...] = height
    east_ref[...] = east_smooth - TIME_STEP * (height - pltpu.roll(height, 1, 1))
    north_ref[...] = (north_smooth - TIME_STEP * (height - south)) * inside_ref[...]


def filter_rows(values, cuts, mass, theta, lon_theta, lat_theta, height_ext, inside):
    count, length = values.shape
    _, _, twc, tws, forward, inverse, folded = fft_tables(length)
    block = mass.shape[0]
    piece = jax.ShapeDtypeStruct((block, length), values.dtype)
    return pl.pallas_call(
        filter_kernel,
        out_shape=(piece, piece, piece, piece, piece),
        scratch_shapes=[pltpu.VMEM((count, length), jnp.float32)],
    )(
        values, cuts.reshape(count, 1), jnp.asarray(twc), jnp.asarray(tws),
        jnp.asarray(forward), jnp.asarray(inverse), jnp.asarray(folded),
        mass, theta, lon_theta, lat_theta, height_ext, inside,
    )


def prefix_over(value, axis, before):
    count = lax.axis_size(axis)
    rank = lax.axis_index(axis)
    copies = jnp.broadcast_to(value, (count, *value.shape))
    pieces = lax.all_to_all(copies, axis, split_axis=0, concat_axis=0, tiled=True)
    owners = jnp.arange(count, dtype=jnp.int32)
    chosen = owners < rank if before else owners > rank
    return jnp.sum(jnp.where(chosen[:, None, None], pieces, 0.0), axis=0)


def local(wind_east, wind_north, layer_mass, theta_field, surface_height, filter_cutoff):
    levels, lat_rows, length = wind_east.shape
    wind_east, wind_north, layer_mass, theta_field = (
        jnp.transpose(v, (1, 0, 2)) for v in (wind_east, wind_north, layer_mass, theta_field)
    )
    lat_count = lax.axis_size("lat")
    lat_rank = lax.axis_index("lat")
    nlat_all = lat_rows * lat_count
    first_row = lat_rank * lat_rows
    surface = jnp.broadcast_to(surface_height[:, None], (lat_rows, levels, length))
    to_north = jnp.concatenate([layer_mass, theta_field, surface[-1:]], axis=0)
    to_south = jnp.concatenate([layer_mass, theta_field, wind_north[:1]], axis=0)
    count = lat_count
    from_south = lax.ppermute(to_north, "lat", [(i, i + 1) for i in range(count - 1)])
    from_north = lax.ppermute(to_south, "lat", [(i + 1, i) for i in range(count - 1)])
    rows = lat_rows
    mass_pad = jnp.concatenate([from_south[:rows], layer_mass, from_north[:rows]], axis=0)
    theta_pad = jnp.concatenate(
        [from_south[rows : 2 * rows], theta_field, from_north[rows : 2 * rows]], axis=0
    )
    face_rows = first_row + jnp.arange(lat_rows + 1, dtype=jnp.int32)
    coslat = jnp.sin(jnp.pi * face_rows.astype(jnp.float32) / nlat_all)[:, None, None]
    mass_faces = face_lat(mass_pad, lat_rows + 1)
    theta_faces = face_lat(theta_pad, lat_rows + 1)
    north_ext = jnp.concatenate([wind_north, from_north[2 * rows :]], axis=0)
    flux_east = wind_east * face_lon(layer_mass)
    flux_north = north_ext * mass_faces * coslat
    mass_ext = jnp.concatenate([from_south[rows - 1 : rows], layer_mass], axis=0)
    theta_ext = jnp.concatenate([from_south[2 * rows - 1 : 2 * rows], theta_field], axis=0)
    surface_ext = jnp.concatenate([from_south[2 * rows :], surface], axis=0)
    column = jnp.sum(mass_ext, axis=1)
    above_mass = prefix_over(column, "lev", True)
    bottom = TOP_PRESSURE + above_mass[:, None] + jnp.cumsum(mass_ext, axis=1)
    top_press = bottom - mass_ext
    thickness = GAS_CONST * theta_ext * (jnp.log(bottom) - jnp.log(top_press))
    depth_sum = jnp.sum(thickness, axis=1)
    below_depth = prefix_over(depth_sum, "lev", False)
    inclusive = jnp.flip(jnp.cumsum(jnp.flip(thickness, 1), axis=1), 1)
    height_ext = surface_ext + below_depth[:, None] + (inclusive - thickness) + 0.5 * thickness
    fields = jnp.concatenate([wind_east, wind_north, flux_east, flux_north], axis=0)
    cut_rows = jnp.concatenate([face_rows[:-1], face_rows[:-1], face_rows[:-1], face_rows])
    row_cuts = jnp.broadcast_to(
        filter_cutoff[jnp.minimum(cut_rows, nlat_all - 1)][:, None], fields.shape[:2]
    ).reshape(-1)
    inside = jnp.broadcast_to(
        (face_rows[:-1] > 0).astype(jnp.float32)[:, None, None], (lat_rows, levels, 1)
    )
    flat = lambda v: v.reshape(-1, v.shape[-1])
    results = filter_rows(
        flat(fields), row_cuts, flat(layer_mass), flat(theta_field),
        flat(face_lon(theta_field)), flat(theta_faces), flat(height_ext), flat(inside),
    )
    new_east, new_north, new_mass, new_heat, height = (
        v.reshape(lat_rows, levels, length) for v in results
    )
    outputs = (new_east, new_north, new_mass, new_heat, height)
    return tuple(jnp.transpose(v, (1, 0, 2)) for v in outputs)


def solution(mesh):
    in_specs = (
        P("lev", "lat", None),
        P("lev", "lat", None),
        P("lev", "lat", None),
        P("lev", "lat", None),
        P("lat", None),
        P(),
    )
    out_specs = (
        P("lev", "lat", None),
        P("lev", "lat", None),
        P("lev", "lat", None),
        P("lev", "lat", None),
        P("lev", "lat", None),
    )
    return jax.shard_map(local, mesh=mesh, in_specs=in_specs, out_specs=out_specs, check_vma=False)
```

```python
import numpy as np
import jax
import jax.numpy as jnp
from jax import lax
from jax.experimental import pallas as pl
from jax.sharding import PartitionSpec as P

TIME_STEP = 0.25
GAS_CONST = 1.0
TOP_PRESSURE = 1.0


def face_lon(values):
    return (
        37.0 * (jnp.roll(values, 1, -1) + values)
        - 8.0 * (jnp.roll(values, 2, -1) + jnp.roll(values, -1, -1))
        + (jnp.roll(values, 3, -1) + jnp.roll(values, -2, -1))
    ) / 60.0


def face_lat(padded, count):
    return (
        37.0 * (padded[2 : 2 + count] + padded[3 : 3 + count])
        - 8.0 * (padded[1 : 1 + count] + padded[4 : 4 + count])
        + (padded[0:count] + padded[5 : 5 + count])
    ) / 60.0


FACTOR_ROWS = 9
FACTOR_LANES = 128

def fft_tables(length):
    rows, lanes = FACTOR_ROWS, FACTOR_LANES
    small = np.arange(rows)
    small_phase = 2.0 * np.pi * np.outer(small, small) / rows
    low = np.arange(rows)[:, None]
    high = np.arange(lanes)[None, :]
    twist = 2.0 * np.pi * ((low * high) % length) / length
    waves = np.arange(lanes)
    wave_phase = 2.0 * np.pi * (np.outer(waves, waves) % lanes) / lanes
    wc, ws = np.cos(wave_phase), np.sin(wave_phase)
    forward = np.block([[wc, -ws], [ws, wc]]).astype(np.float32)
    inverse = np.block([[wc, ws], [-ws, wc]]).astype(np.float32)
    number = np.arange(rows)[:, None] + rows * np.arange(lanes)[None, :]
    folded = np.minimum(number, length - number)
    folded = np.concatenate([folded, folded], axis=1).astype(np.int32)
    return (np.cos(small_phase), np.sin(small_phase), np.cos(twist).astype(np.float32),
            np.sin(twist).astype(np.float32), forward, inverse, folded)

def split_table(table):
    high = jnp.asarray(table, jnp.float32).astype(jnp.bfloat16)
    low = (jnp.asarray(table, jnp.float32) - high.astype(jnp.float32)).astype(jnp.bfloat16)
    return jnp.stack([high, low])


def split_dot(values, table_high, table_low):
    high = values.astype(jnp.bfloat16)
    low = (values - high.astype(jnp.float32)).astype(jnp.bfloat16)
    product = lambda a, b: jnp.dot(a, b, preferred_element_type=jnp.float32)
    return product(high, table_high) + (product(high, table_low) + product(low, table_high))


def filter_kernel(x_ref, cut_ref, twc_ref, tws_ref, fwd_ref, inv_ref, fold_ref, o_ref):
    rows, lanes = FACTOR_ROWS, FACTOR_LANES
    count, length = x_ref.shape
    c9, s9 = fft_tables(length)[:2]
    half = rows // 2 + 1
    parts = [x_ref[:, n * lanes : (n + 1) * lanes] for n in range(rows)]
    pieces = []
    for k in range(half):
        real_a = sum(float(c9[k, n]) * parts[n] for n in range(rows))
        imag_a = sum(float(-s9[k, n]) * parts[n] for n in range(1, rows))
        twc = twc_ref[k : k + 1, :]
        tws = tws_ref[k : k + 1, :]
        pieces.append(
            jnp.concatenate([real_a * twc + imag_a * tws, imag_a * twc - real_a * tws], axis=1)
        )
    spectrum = split_dot(jnp.concatenate(pieces, axis=0), fwd_ref[0], fwd_ref[1])
    cuts = cut_ref[...]
    keep = jnp.concatenate(
        [(fold_ref[k : k + 1, :] <= cuts).astype(jnp.float32) for k in range(half)], axis=0
    )
    back = split_dot(spectrum * keep, inv_ref[0], inv_ref[1])
    real_d, imag_d = [], []
    for k in range(half):
        twc = twc_ref[k : k + 1, :]
        tws = tws_ref[k : k + 1, :]
        real_c = back[k * count : (k + 1) * count, :lanes]
        imag_c = back[k * count : (k + 1) * count, lanes:]
        real_d.append(real_c * twc - imag_c * tws)
        imag_d.append(imag_c * twc + real_c * tws)
    for n in range(rows):
        o_ref[:, n * lanes : (n + 1) * lanes] = float(1.0 / length) * real_d[0] + sum(
            float(2.0 * c9[k, n] / length) * real_d[k] - float(2.0 * s9[k, n] / length) * imag_d[k]
            for k in range(1, half)
        )


def filter_rows(values, cuts):
    count, length = values.shape
    _, _, twc, tws, forward, inverse, folded = fft_tables(length)
    return pl.pallas_call(
        filter_kernel,
        out_shape=jax.ShapeDtypeStruct(values.shape, values.dtype),
    )(values, cuts.reshape(count, 1), jnp.asarray(twc), jnp.asarray(tws), split_table(forward),
      split_table(inverse), jnp.asarray(folded))

def prefix_over(value, axis, before):
    count = lax.axis_size(axis)
    rank = lax.axis_index(axis)
    copies = jnp.broadcast_to(value, (count, *value.shape))
    pieces = lax.all_to_all(copies, axis, split_axis=0, concat_axis=0, tiled=True)
    owners = jnp.arange(count, dtype=jnp.int32)
    chosen = owners < rank if before else owners > rank
    return jnp.sum(jnp.where(chosen[:, None, None], pieces, 0.0), axis=0)


def local(wind_east, wind_north, layer_mass, theta_field, surface_height, filter_cutoff):
    levels, lat_rows, length = wind_east.shape
    wind_east, wind_north, layer_mass, theta_field = (
        jnp.transpose(v, (1, 0, 2)) for v in (wind_east, wind_north, layer_mass, theta_field)
    )
    lat_count = lax.axis_size("lat")
    lat_rank = lax.axis_index("lat")
    nlat_all = lat_rows * lat_count
    first_row = lat_rank * lat_rows
    surface = jnp.broadcast_to(surface_height[:, None], (lat_rows, levels, length))
    to_north = jnp.concatenate([layer_mass, theta_field, surface[-1:]], axis=0)
    to_south = jnp.concatenate([layer_mass, theta_field, wind_north[:1]], axis=0)
    count = lat_count
    from_south = lax.ppermute(to_north, "lat", [(i, i + 1) for i in range(count - 1)])
    from_north = lax.ppermute(to_south, "lat", [(i + 1, i) for i in range(count - 1)])
    rows = lat_rows
    mass_pad = jnp.concatenate([from_south[:rows], layer_mass, from_north[:rows]], axis=0)
    theta_pad = jnp.concatenate(
        [from_south[rows : 2 * rows], theta_field, from_north[rows : 2 * rows]], axis=0
    )
    face_rows = first_row + jnp.arange(lat_rows + 1, dtype=jnp.int32)
    coslat = jnp.sin(jnp.pi * face_rows.astype(jnp.float32) / nlat_all)[:, None, None]
    mass_faces = face_lat(mass_pad, lat_rows + 1)
    theta_faces = face_lat(theta_pad, lat_rows + 1)
    north_ext = jnp.concatenate([wind_north, from_north[2 * rows :]], axis=0)
    flux_east = wind_east * face_lon(layer_mass)
    flux_north = north_ext * mass_faces * coslat
    mass_ext = jnp.concatenate([from_south[rows - 1 : rows], layer_mass], axis=0)
    theta_ext = jnp.concatenate([from_south[2 * rows - 1 : 2 * rows], theta_field], axis=0)
    surface_ext = jnp.concatenate([from_south[2 * rows :], surface], axis=0)
    column = jnp.sum(mass_ext, axis=1)
    above_mass = prefix_over(column, "lev", True)
    bottom = TOP_PRESSURE + above_mass[:, None] + jnp.cumsum(mass_ext, axis=1)
    top_press = bottom - mass_ext
    thickness = GAS_CONST * theta_ext * (jnp.log(bottom) - jnp.log(top_press))
    depth_sum = jnp.sum(thickness, axis=1)
    below_depth = prefix_over(depth_sum, "lev", False)
    inclusive = jnp.flip(jnp.cumsum(jnp.flip(thickness, 1), axis=1), 1)
    height_ext = surface_ext + below_depth[:, None] + (inclusive - thickness) + 0.5 * thickness
    fields = jnp.concatenate([wind_east, wind_north, flux_east, flux_north], axis=0)
    fields, height_ext = lax.optimization_barrier((fields, height_ext))
    cut_rows = jnp.concatenate([face_rows[:-1], face_rows[:-1], face_rows[:-1], face_rows])
    row_cuts = jnp.broadcast_to(
        filter_cutoff[jnp.minimum(cut_rows, nlat_all - 1)][:, None], fields.shape[:2]
    ).reshape(-1)
    smooth = filter_rows(fields.reshape(-1, length), row_cuts).reshape(fields.shape)
    east_smooth = smooth[:rows]
    north_smooth = smooth[rows : 2 * rows]
    east_flux = smooth[2 * rows : 3 * rows]
    north_full = smooth[3 * rows :]
    new_mass = layer_mass - TIME_STEP * (
        jnp.roll(east_flux, -1, -1) - east_flux + (north_full[1:] - north_full[:-1])
    )
    heat_east = east_flux * face_lon(theta_field)
    heat_north = north_full * theta_faces
    new_heat = theta_field * layer_mass - TIME_STEP * (
        jnp.roll(heat_east, -1, -1) - heat_east + (heat_north[1:] - heat_north[:-1])
    )
    height = height_ext[1:]
    new_east = east_smooth - TIME_STEP * (height - jnp.roll(height, 1, -1))
    inside = (face_rows[:-1] > 0).astype(jnp.float32)[:, None, None]
    new_north = (north_smooth - TIME_STEP * (height - height_ext[:-1])) * inside
    outputs = (new_east, new_north, new_mass, new_heat, height)
    return tuple(jnp.transpose(v, (1, 0, 2)) for v in outputs)


def solution(mesh):
    in_specs = (
        P("lev", "lat", None),
        P("lev", "lat", None),
        P("lev", "lat", None),
        P("lev", "lat", None),
        P("lat", None),
        P(),
    )
    out_specs = (
        P("lev", "lat", None),
        P("lev", "lat", None),
        P("lev", "lat", None),
        P("lev", "lat", None),
        P("lev", "lat", None),
    )
    return jax.shard_map(local, mesh=mesh, in_specs=in_specs, out_specs=out_specs, check_vma=False)
```

```python
import numpy as np
import jax
import jax.numpy as jnp
from jax import lax
from jax.experimental import pallas as pl
from jax.sharding import PartitionSpec as P

TIME_STEP = 0.25
GAS_CONST = 1.0
TOP_PRESSURE = 1.0


def face_lon(values):
    return (
        37.0 * (jnp.roll(values, 1, -1) + values)
        - 8.0 * (jnp.roll(values, 2, -1) + jnp.roll(values, -1, -1))
        + (jnp.roll(values, 3, -1) + jnp.roll(values, -2, -1))
    ) / 60.0


def face_lat(padded, count):
    return (
        37.0 * (padded[2 : 2 + count] + padded[3 : 3 + count])
        - 8.0 * (padded[1 : 1 + count] + padded[4 : 4 + count])
        + (padded[0:count] + padded[5 : 5 + count])
    ) / 60.0


FACTOR_ROWS = 9
FACTOR_LANES = 128

def fft_tables(length):
    rows, lanes = FACTOR_ROWS, FACTOR_LANES
    small = np.arange(rows)
    small_phase = 2.0 * np.pi * np.outer(small, small) / rows
    low = np.arange(rows)[:, None]
    high = np.arange(lanes)[None, :]
    twist = 2.0 * np.pi * ((low * high) % length) / length
    waves = np.arange(lanes)
    wave_phase = 2.0 * np.pi * (np.outer(waves, waves) % lanes) / lanes
    wc, ws = np.cos(wave_phase), np.sin(wave_phase)
    forward = np.block([[wc, -ws], [ws, wc]]).astype(np.float32)
    inverse = np.block([[wc, ws], [-ws, wc]]).astype(np.float32)
    number = np.arange(rows)[:, None] + rows * np.arange(lanes)[None, :]
    folded = np.minimum(number, length - number)
    folded = np.concatenate([folded, folded], axis=1).astype(np.int32)
    return (np.cos(small_phase), np.sin(small_phase), np.cos(twist).astype(np.float32),
            np.sin(twist).astype(np.float32), forward, inverse, folded)

def split_table(table):
    high = jnp.asarray(table, jnp.float32).astype(jnp.bfloat16)
    low = (jnp.asarray(table, jnp.float32) - high.astype(jnp.float32)).astype(jnp.bfloat16)
    return jnp.stack([high, low])


def split_dot(values, table_high, table_low):
    high = values.astype(jnp.bfloat16)
    low = (values - high.astype(jnp.float32)).astype(jnp.bfloat16)
    product = lambda a, b: jnp.dot(a, b, preferred_element_type=jnp.float32)
    return product(high, table_high) + (product(high, table_low) + product(low, table_high))


def filter_kernel(x_ref, cut_ref, twc_ref, tws_ref, fwd_ref, inv_ref, fold_ref, o_ref):
    rows, lanes = FACTOR_ROWS, FACTOR_LANES
    count, length = x_ref.shape
    c9, s9 = fft_tables(length)[:2]
    half = rows // 2 + 1
    parts = [x_ref[:, n * lanes : (n + 1) * lanes] for n in range(rows)]
    pieces = []
    for k in range(half):
        real_a = sum(float(c9[k, n]) * parts[n] for n in range(rows))
        imag_a = sum(float(-s9[k, n]) * parts[n] for n in range(1, rows))
        twc = twc_ref[k : k + 1, :]
        tws = tws_ref[k : k + 1, :]
        pieces.append(
            jnp.concatenate([real_a * twc + imag_a * tws, imag_a * twc - real_a * tws], axis=1)
        )
    spectrum = split_dot(jnp.concatenate(pieces, axis=0), fwd_ref[0], fwd_ref[1])
    cuts = cut_ref[...]
    keep = jnp.concatenate(
        [(fold_ref[k : k + 1, :] <= cuts).astype(jnp.float32) for k in range(half)], axis=0
    )
    back = split_dot(spectrum * keep, inv_ref[0], inv_ref[1])
    real_d, imag_d = [], []
    for k in range(half):
        twc = twc_ref[k : k + 1, :]
        tws = tws_ref[k : k + 1, :]
        real_c = back[k * count : (k + 1) * count, :lanes]
        imag_c = back[k * count : (k + 1) * count, lanes:]
        real_d.append(real_c * twc - imag_c * tws)
        imag_d.append(imag_c * twc + real_c * tws)
    for n in range(rows):
        o_ref[:, n * lanes : (n + 1) * lanes] = float(1.0 / length) * real_d[0] + sum(
            float(2.0 * c9[k, n] / length) * real_d[k] - float(2.0 * s9[k, n] / length) * imag_d[k]
            for k in range(1, half)
        )


def filter_rows(values, cuts):
    count, length = values.shape
    _, _, twc, tws, forward, inverse, folded = fft_tables(length)
    return pl.pallas_call(
        filter_kernel,
        out_shape=jax.ShapeDtypeStruct(values.shape, values.dtype),
    )(values, cuts.reshape(count, 1), jnp.asarray(twc), jnp.asarray(tws), split_table(forward),
      split_table(inverse), jnp.asarray(folded))

def prefix_over(value, axis, before):
    count = lax.axis_size(axis)
    rank = lax.axis_index(axis)
    copies = jnp.broadcast_to(value, (count, *value.shape))
    pieces = lax.all_to_all(copies, axis, split_axis=0, concat_axis=0, tiled=True)
    owners = jnp.arange(count, dtype=jnp.int32)
    chosen = owners < rank if before else owners > rank
    return jnp.sum(jnp.where(chosen[:, None, None], pieces, 0.0), axis=0)


def local(wind_east, wind_north, layer_mass, theta_field, surface_height, filter_cutoff):
    levels, lat_rows, length = wind_east.shape
    wind_east, wind_north, layer_mass, theta_field = (
        jnp.transpose(v, (1, 0, 2)) for v in (wind_east, wind_north, layer_mass, theta_field)
    )
    lat_count = lax.axis_size("lat")
    lat_rank = lax.axis_index("lat")
    nlat_all = lat_rows * lat_count
    first_row = lat_rank * lat_rows
    surface = jnp.broadcast_to(surface_height[:, None], (lat_rows, levels, length))
    to_north = jnp.concatenate([layer_mass, theta_field, surface], axis=0)
    to_south = jnp.concatenate([layer_mass, theta_field, wind_north], axis=0)
    count = lat_count
    from_south = lax.ppermute(to_north, "lat", [(i, i + 1) for i in range(count - 1)])
    from_north = lax.ppermute(to_south, "lat", [(i + 1, i) for i in range(count - 1)])
    rows = lat_rows
    mass_pad = jnp.concatenate([from_south[:rows], layer_mass, from_north[:rows]], axis=0)
    theta_pad = jnp.concatenate(
        [from_south[rows : 2 * rows], theta_field, from_north[rows : 2 * rows]], axis=0
    )
    face_rows = first_row + jnp.arange(lat_rows + 1, dtype=jnp.int32)
    coslat = jnp.sin(jnp.pi * face_rows.astype(jnp.float32) / nlat_all)[:, None, None]
    mass_faces = face_lat(mass_pad, lat_rows + 1)
    theta_faces = face_lat(theta_pad, lat_rows + 1)
    north_ext = jnp.concatenate([wind_north, from_north[2 * rows : 2 * rows + 1]], axis=0)
    flux_east = wind_east * face_lon(layer_mass)
    flux_north = north_ext * mass_faces * coslat
    mass_ext = jnp.concatenate([from_south[rows - 1 : rows], layer_mass], axis=0)
    theta_ext = jnp.concatenate([from_south[2 * rows - 1 : 2 * rows], theta_field], axis=0)
    surface_ext = jnp.concatenate([from_south[3 * rows - 1 :], surface], axis=0)
    column = jnp.sum(mass_ext, axis=1)
    above_mass = prefix_over(column, "lev", True)
    bottom = TOP_PRESSURE + above_mass[:, None] + jnp.cumsum(mass_ext, axis=1)
    top_press = bottom - mass_ext
    thickness = GAS_CONST * theta_ext * (jnp.log(bottom) - jnp.log(top_press))
    depth_sum = jnp.sum(thickness, axis=1)
    below_depth = prefix_over(depth_sum, "lev", False)
    inclusive = jnp.flip(jnp.cumsum(jnp.flip(thickness, 1), axis=1), 1)
    height_ext = surface_ext + below_depth[:, None] + (inclusive - thickness) + 0.5 * thickness
    fields = jnp.concatenate([wind_east, wind_north, flux_east, flux_north], axis=0)
    fields, height_ext = lax.optimization_barrier((fields, height_ext))
    cut_rows = jnp.concatenate([face_rows[:-1], face_rows[:-1], face_rows[:-1], face_rows])
    row_cuts = jnp.broadcast_to(
        filter_cutoff[jnp.minimum(cut_rows, nlat_all - 1)][:, None], fields.shape[:2]
    ).reshape(-1)
    smooth = filter_rows(fields.reshape(-1, length), row_cuts).reshape(fields.shape)
    east_smooth = smooth[:rows]
    north_smooth = smooth[rows : 2 * rows]
    east_flux = smooth[2 * rows : 3 * rows]
    north_full = smooth[3 * rows :]
    new_mass = layer_mass - TIME_STEP * (
        jnp.roll(east_flux, -1, -1) - east_flux + (north_full[1:] - north_full[:-1])
    )
    heat_east = east_flux * face_lon(theta_field)
    heat_north = north_full * theta_faces
    new_heat = theta_field * layer_mass - TIME_STEP * (
        jnp.roll(heat_east, -1, -1) - heat_east + (heat_north[1:] - heat_north[:-1])
    )
    height = height_ext[1:]
    new_east = east_smooth - TIME_STEP * (height - jnp.roll(height, 1, -1))
    inside = (face_rows[:-1] > 0).astype(jnp.float32)[:, None, None]
    new_north = (north_smooth - TIME_STEP * (height - height_ext[:-1])) * inside
    outputs = (new_east, new_north, new_mass, new_heat, height)
    return tuple(jnp.transpose(v, (1, 0, 2)) for v in outputs)


def solution(mesh):
    in_specs = (
        P("lev", "lat", None),
        P("lev", "lat", None),
        P("lev", "lat", None),
        P("lev", "lat", None),
        P("lat", None),
        P(),
    )
    out_specs = (
        P("lev", "lat", None),
        P("lev", "lat", None),
        P("lev", "lat", None),
        P("lev", "lat", None),
        P("lev", "lat", None),
    )
    return jax.shard_map(local, mesh=mesh, in_specs=in_specs, out_specs=out_specs, check_vma=False)
```

```python
import numpy as np
import jax
import jax.numpy as jnp
from jax import lax
from jax.experimental import pallas as pl
from jax.sharding import PartitionSpec as P

TIME_STEP = 0.25
GAS_CONST = 1.0
TOP_PRESSURE = 1.0


def face_lon(values):
    return (
        37.0 * (jnp.roll(values, 1, -1) + values)
        - 8.0 * (jnp.roll(values, 2, -1) + jnp.roll(values, -1, -1))
        + (jnp.roll(values, 3, -1) + jnp.roll(values, -2, -1))
    ) / 60.0


def face_lat(padded, count):
    return (
        37.0 * (padded[2 : 2 + count] + padded[3 : 3 + count])
        - 8.0 * (padded[1 : 1 + count] + padded[4 : 4 + count])
        + (padded[0:count] + padded[5 : 5 + count])
    ) / 60.0


FACTOR_ROWS = 9
FACTOR_LANES = 128

def fft_tables(length):
    rows, lanes = FACTOR_ROWS, FACTOR_LANES
    small = np.arange(rows)
    small_phase = 2.0 * np.pi * np.outer(small, small) / rows
    low = np.arange(rows)[:, None]
    high = np.arange(lanes)[None, :]
    twist = 2.0 * np.pi * ((low * high) % length) / length
    waves = np.arange(lanes)
    wave_phase = 2.0 * np.pi * (np.outer(waves, waves) % lanes) / lanes
    wc, ws = np.cos(wave_phase), np.sin(wave_phase)
    forward = np.block([[wc, -ws], [ws, wc]]).astype(np.float32)
    inverse = np.block([[wc, ws], [-ws, wc]]).astype(np.float32)
    number = np.arange(rows)[:, None] + rows * np.arange(lanes)[None, :]
    folded = np.minimum(number, length - number)
    folded = np.concatenate([folded, folded], axis=1).astype(np.int32)
    return (np.cos(small_phase), np.sin(small_phase), np.cos(twist).astype(np.float32),
            np.sin(twist).astype(np.float32), forward, inverse, folded)

def split_table(table):
    high = jnp.asarray(table, jnp.float32).astype(jnp.bfloat16)
    low = (jnp.asarray(table, jnp.float32) - high.astype(jnp.float32)).astype(jnp.bfloat16)
    return jnp.stack([high, low])


def split_dot(values, table_high, table_low):
    high = values.astype(jnp.bfloat16)
    low = (values - high.astype(jnp.float32)).astype(jnp.bfloat16)
    product = lambda a, b: jnp.dot(a, b, preferred_element_type=jnp.float32)
    return product(high, table_high) + (product(high, table_low) + product(low, table_high))


def filter_kernel(x_ref, cut_ref, twc_ref, tws_ref, fwd_ref, inv_ref, fold_ref, o_ref):
    rows, lanes = FACTOR_ROWS, FACTOR_LANES
    count, length = x_ref.shape
    c9, s9 = fft_tables(length)[:2]
    half = rows // 2 + 1
    parts = [x_ref[:, n * lanes : (n + 1) * lanes] for n in range(rows)]
    pieces = []
    for k in range(half):
        real_a = sum(float(c9[k, n]) * parts[n] for n in range(rows))
        imag_a = sum(float(-s9[k, n]) * parts[n] for n in range(1, rows))
        twc = twc_ref[k : k + 1, :]
        tws = tws_ref[k : k + 1, :]
        pieces.append(
            jnp.concatenate([real_a * twc + imag_a * tws, imag_a * twc - real_a * tws], axis=1)
        )
    spectrum = split_dot(jnp.concatenate(pieces, axis=0), fwd_ref[0], fwd_ref[1])
    cuts = cut_ref[...]
    keep = jnp.concatenate(
        [(fold_ref[k : k + 1, :] <= cuts).astype(jnp.float32) for k in range(half)], axis=0
    )
    back = split_dot(spectrum * keep, inv_ref[0], inv_ref[1])
    real_d, imag_d = [], []
    for k in range(half):
        twc = twc_ref[k : k + 1, :]
        tws = tws_ref[k : k + 1, :]
        real_c = back[k * count : (k + 1) * count, :lanes]
        imag_c = back[k * count : (k + 1) * count, lanes:]
        real_d.append(real_c * twc - imag_c * tws)
        imag_d.append(imag_c * twc + real_c * tws)
    for n in range(rows):
        o_ref[:, n * lanes : (n + 1) * lanes] = float(1.0 / length) * real_d[0] + sum(
            float(2.0 * c9[k, n] / length) * real_d[k] - float(2.0 * s9[k, n] / length) * imag_d[k]
            for k in range(1, half)
        )


def filter_rows(values, cuts):
    count, length = values.shape
    _, _, twc, tws, forward, inverse, folded = fft_tables(length)
    return pl.pallas_call(
        filter_kernel,
        out_shape=jax.ShapeDtypeStruct(values.shape, values.dtype),
    )(values, cuts.reshape(count, 1), jnp.asarray(twc), jnp.asarray(tws), split_table(forward),
      split_table(inverse), jnp.asarray(folded))

def prefix_over(value, axis, before):
    count = lax.axis_size(axis)
    rank = lax.axis_index(axis)
    copies = jnp.broadcast_to(value, (count, *value.shape))
    pieces = lax.all_to_all(copies, axis, split_axis=0, concat_axis=0, tiled=True)
    owners = jnp.arange(count, dtype=jnp.int32)
    chosen = owners < rank if before else owners > rank
    return jnp.sum(jnp.where(chosen[:, None, None], pieces, 0.0), axis=0)


def local(wind_east, wind_north, layer_mass, theta_field, surface_height, filter_cutoff):
    levels, lat_rows, length = wind_east.shape
    wind_east, wind_north, layer_mass, theta_field = (
        jnp.transpose(v, (1, 0, 2)) for v in (wind_east, wind_north, layer_mass, theta_field)
    )
    lat_count = lax.axis_size("lat")
    lat_rank = lax.axis_index("lat")
    nlat_all = lat_rows * lat_count
    first_row = lat_rank * lat_rows
    surface = jnp.pad(surface_height[:, None], ((0, 0), (0, levels - 1), (0, 0)))
    to_north = jnp.concatenate([layer_mass, theta_field, surface], axis=0)
    to_south = jnp.concatenate([layer_mass, theta_field, wind_north], axis=0)
    count = lat_count
    from_south = lax.ppermute(to_north, "lat", [(i, i + 1) for i in range(count - 1)])
    from_north = lax.ppermute(to_south, "lat", [(i + 1, i) for i in range(count - 1)])
    rows = lat_rows
    mass_pad = jnp.concatenate([from_south[:rows], layer_mass, from_north[:rows]], axis=0)
    theta_pad = jnp.concatenate(
        [from_south[rows : 2 * rows], theta_field, from_north[rows : 2 * rows]], axis=0
    )
    face_rows = first_row + jnp.arange(lat_rows + 1, dtype=jnp.int32)
    coslat = jnp.sin(jnp.pi * face_rows.astype(jnp.float32) / nlat_all)[:, None, None]
    mass_faces = face_lat(mass_pad, lat_rows + 1)
    theta_faces = face_lat(theta_pad, lat_rows + 1)
    north_ext = jnp.concatenate([wind_north, from_north[2 * rows : 2 * rows + 1]], axis=0)
    flux_east = wind_east * face_lon(layer_mass)
    flux_north = north_ext * mass_faces * coslat
    mass_ext = jnp.concatenate([from_south[rows - 1 : rows], layer_mass], axis=0)
    theta_ext = jnp.concatenate([from_south[2 * rows - 1 : 2 * rows], theta_field], axis=0)
    surface_ext = jnp.concatenate(
        [from_south[3 * rows - 1 :, :1], surface_height[:, None]], axis=0
    )
    column = jnp.sum(mass_ext, axis=1)
    above_mass = prefix_over(column, "lev", True)
    bottom = TOP_PRESSURE + above_mass[:, None] + jnp.cumsum(mass_ext, axis=1)
    top_press = bottom - mass_ext
    thickness = GAS_CONST * theta_ext * (jnp.log(bottom) - jnp.log(top_press))
    depth_sum = jnp.sum(thickness, axis=1)
    below_depth = prefix_over(depth_sum, "lev", False)
    inclusive = jnp.flip(jnp.cumsum(jnp.flip(thickness, 1), axis=1), 1)
    height_ext = surface_ext + below_depth[:, None] + (inclusive - thickness) + 0.5 * thickness
    fields = jnp.concatenate([wind_east, wind_north, flux_east, flux_north], axis=0)
    fields, height_ext = lax.optimization_barrier((fields, height_ext))
    cut_rows = jnp.concatenate([face_rows[:-1], face_rows[:-1], face_rows[:-1], face_rows])
    row_cuts = jnp.broadcast_to(
        filter_cutoff[jnp.minimum(cut_rows, nlat_all - 1)][:, None], fields.shape[:2]
    ).reshape(-1)
    smooth = filter_rows(fields.reshape(-1, length), row_cuts).reshape(fields.shape)
    east_smooth = smooth[:rows]
    north_smooth = smooth[rows : 2 * rows]
    east_flux = smooth[2 * rows : 3 * rows]
    north_full = smooth[3 * rows :]
    new_mass = layer_mass - TIME_STEP * (
        jnp.roll(east_flux, -1, -1) - east_flux + (north_full[1:] - north_full[:-1])
    )
    heat_east = east_flux * face_lon(theta_field)
    heat_north = north_full * theta_faces
    new_heat = theta_field * layer_mass - TIME_STEP * (
        jnp.roll(heat_east, -1, -1) - heat_east + (heat_north[1:] - heat_north[:-1])
    )
    height = height_ext[1:]
    new_east = east_smooth - TIME_STEP * (height - jnp.roll(height, 1, -1))
    inside = (face_rows[:-1] > 0).astype(jnp.float32)[:, None, None]
    new_north = (north_smooth - TIME_STEP * (height - height_ext[:-1])) * inside
    outputs = (new_east, new_north, new_mass, new_heat, height)
    return tuple(jnp.transpose(v, (1, 0, 2)) for v in outputs)


def solution(mesh):
    in_specs = (
        P("lev", "lat", None),
        P("lev", "lat", None),
        P("lev", "lat", None),
        P("lev", "lat", None),
        P("lat", None),
        P(),
    )
    out_specs = (
        P("lev", "lat", None),
        P("lev", "lat", None),
        P("lev", "lat", None),
        P("lev", "lat", None),
        P("lev", "lat", None),
    )
    return jax.shard_map(local, mesh=mesh, in_specs=in_specs, out_specs=out_specs, check_vma=False)
```

```python
import numpy as np
import jax
import jax.numpy as jnp
from jax import lax
from jax.experimental import pallas as pl
from jax.sharding import PartitionSpec as P

TIME_STEP = 0.25
GAS_CONST = 1.0
TOP_PRESSURE = 1.0


def face_lon(values):
    return (
        37.0 * (jnp.roll(values, 1, -1) + values)
        - 8.0 * (jnp.roll(values, 2, -1) + jnp.roll(values, -1, -1))
        + (jnp.roll(values, 3, -1) + jnp.roll(values, -2, -1))
    ) / 60.0


def face_lat(padded, count):
    return (
        37.0 * (padded[2 : 2 + count] + padded[3 : 3 + count])
        - 8.0 * (padded[1 : 1 + count] + padded[4 : 4 + count])
        + (padded[0:count] + padded[5 : 5 + count])
    ) / 60.0


FACTOR_ROWS = 9
FACTOR_LANES = 128

def fft_tables(length):
    rows, lanes = FACTOR_ROWS, FACTOR_LANES
    small = np.arange(rows)
    small_phase = 2.0 * np.pi * np.outer(small, small) / rows
    low = np.arange(rows)[:, None]
    high = np.arange(lanes)[None, :]
    twist = 2.0 * np.pi * ((low * high) % length) / length
    waves = np.arange(lanes)
    wave_phase = 2.0 * np.pi * (np.outer(waves, waves) % lanes) / lanes
    wc, ws = np.cos(wave_phase), np.sin(wave_phase)
    forward = np.block([[wc, -ws], [ws, wc]]).astype(np.float32)
    inverse = np.block([[wc, ws], [-ws, wc]]).astype(np.float32)
    number = np.arange(rows)[:, None] + rows * np.arange(lanes)[None, :]
    folded = np.minimum(number, length - number)
    folded = np.concatenate([folded, folded], axis=1).astype(np.int32)
    return (np.cos(small_phase), np.sin(small_phase), np.cos(twist).astype(np.float32),
            np.sin(twist).astype(np.float32), forward, inverse, folded)

def split_table(table):
    high = jnp.asarray(table, jnp.float32).astype(jnp.bfloat16)
    low = (jnp.asarray(table, jnp.float32) - high.astype(jnp.float32)).astype(jnp.bfloat16)
    return jnp.stack([high, low])


def split_dot(values, table_high, table_low):
    high = values.astype(jnp.bfloat16)
    low = (values - high.astype(jnp.float32)).astype(jnp.bfloat16)
    product = lambda a, b: jnp.dot(a, b, preferred_element_type=jnp.float32)
    return product(high, table_high) + (product(high, table_low) + product(low, table_high))


def filter_kernel(x_ref, cut_ref, twc_ref, tws_ref, fwd_ref, inv_ref, fold_ref, o_ref):
    rows, lanes = FACTOR_ROWS, FACTOR_LANES
    count, length = x_ref.shape
    c9, s9 = fft_tables(length)[:2]
    half = rows // 2 + 1
    parts = [x_ref[:, n * lanes : (n + 1) * lanes] for n in range(rows)]
    pairs = [parts[n] + parts[rows - n] for n in range(1, half)]
    gaps = [parts[n] - parts[rows - n] for n in range(1, half)]
    pieces = []
    for k in range(half):
        real_a = parts[0] + sum(float(c9[k, n]) * pairs[n - 1] for n in range(1, half))
        imag_a = sum(float(-s9[k, n]) * gaps[n - 1] for n in range(1, half))
        twc = twc_ref[k : k + 1, :]
        tws = tws_ref[k : k + 1, :]
        pieces.append(
            jnp.concatenate([real_a * twc + imag_a * tws, imag_a * twc - real_a * tws], axis=1)
        )
    spectrum = split_dot(jnp.concatenate(pieces, axis=0), fwd_ref[0], fwd_ref[1])
    cuts = cut_ref[...]
    keep = jnp.concatenate(
        [(fold_ref[k : k + 1, :] <= cuts).astype(jnp.float32) for k in range(half)], axis=0
    )
    back = split_dot(spectrum * keep, inv_ref[0], inv_ref[1])
    real_d, imag_d = [], []
    for k in range(half):
        twc = twc_ref[k : k + 1, :]
        tws = tws_ref[k : k + 1, :]
        real_c = back[k * count : (k + 1) * count, :lanes]
        imag_c = back[k * count : (k + 1) * count, lanes:]
        real_d.append(real_c * twc - imag_c * tws)
        imag_d.append(imag_c * twc + real_c * tws)
    base = float(1.0 / length) * real_d[0]
    for n in range(half):
        even = base + sum(float(2.0 * c9[k, n] / length) * real_d[k] for k in range(1, half))
        o_ref[:, n * lanes : (n + 1) * lanes] = even - sum(
            float(2.0 * s9[k, n] / length) * imag_d[k] for k in range(1, half)
        )
        if n > 0:
            o_ref[:, (rows - n) * lanes : (rows - n + 1) * lanes] = even + sum(
                float(2.0 * s9[k, n] / length) * imag_d[k] for k in range(1, half)
            )


def filter_rows(values, cuts):
    count, length = values.shape
    _, _, twc, tws, forward, inverse, folded = fft_tables(length)
    return pl.pallas_call(
        filter_kernel,
        out_shape=jax.ShapeDtypeStruct(values.shape, values.dtype),
    )(values, cuts.reshape(count, 1), jnp.asarray(twc), jnp.asarray(tws), split_table(forward),
      split_table(inverse), jnp.asarray(folded))

def prefix_over(value, axis, before):
    count = lax.axis_size(axis)
    rank = lax.axis_index(axis)
    copies = jnp.broadcast_to(value, (count, *value.shape))
    pieces = lax.all_to_all(copies, axis, split_axis=0, concat_axis=0, tiled=True)
    owners = jnp.arange(count, dtype=jnp.int32)
    chosen = owners < rank if before else owners > rank
    return jnp.sum(jnp.where(chosen[:, None, None], pieces, 0.0), axis=0)


def local(wind_east, wind_north, layer_mass, theta_field, surface_height, filter_cutoff):
    levels, lat_rows, length = wind_east.shape
    wind_east, wind_north, layer_mass, theta_field = (
        jnp.transpose(v, (1, 0, 2)) for v in (wind_east, wind_north, layer_mass, theta_field)
    )
    lat_count = lax.axis_size("lat")
    lat_rank = lax.axis_index("lat")
    nlat_all = lat_rows * lat_count
    first_row = lat_rank * lat_rows
    surface = jnp.broadcast_to(surface_height[:, None], (lat_rows, levels, length))
    to_north = jnp.concatenate([layer_mass, theta_field, surface], axis=0)
    to_south = jnp.concatenate([layer_mass, theta_field, wind_north], axis=0)
    count = lat_count
    from_south = lax.ppermute(to_north, "lat", [(i, i + 1) for i in range(count - 1)])
    from_north = lax.ppermute(to_south, "lat", [(i + 1, i) for i in range(count - 1)])
    rows = lat_rows
    mass_pad = jnp.concatenate([from_south[:rows], layer_mass, from_north[:rows]], axis=0)
    theta_pad = jnp.concatenate(
        [from_south[rows : 2 * rows], theta_field, from_north[rows : 2 * rows]], axis=0
    )
    face_rows = first_row + jnp.arange(lat_rows + 1, dtype=jnp.int32)
    coslat = jnp.sin(jnp.pi * face_rows.astype(jnp.float32) / nlat_all)[:, None, None]
    mass_faces = face_lat(mass_pad, lat_rows + 1)
    theta_faces = face_lat(theta_pad, lat_rows + 1)
    north_ext = jnp.concatenate([wind_north, from_north[2 * rows : 2 * rows + 1]], axis=0)
    flux_east = wind_east * face_lon(layer_mass)
    flux_north = north_ext * mass_faces * coslat
    mass_ext = jnp.concatenate([from_south[rows - 1 : rows], layer_mass], axis=0)
    theta_ext = jnp.concatenate([from_south[2 * rows - 1 : 2 * rows], theta_field], axis=0)
    surface_ext = jnp.concatenate([from_south[3 * rows - 1 :], surface], axis=0)
    column = jnp.sum(mass_ext, axis=1)
    above_mass = prefix_over(column, "lev", True)
    bottom = TOP_PRESSURE + above_mass[:, None] + jnp.cumsum(mass_ext, axis=1)
    top_press = bottom - mass_ext
    thickness = GAS_CONST * theta_ext * (jnp.log(bottom) - jnp.log(top_press))
    depth_sum = jnp.sum(thickness, axis=1)
    below_depth = prefix_over(depth_sum, "lev", False)
    inclusive = jnp.flip(jnp.cumsum(jnp.flip(thickness, 1), axis=1), 1)
    height_ext = surface_ext + below_depth[:, None] + (inclusive - thickness) + 0.5 * thickness
    fields = jnp.concatenate([wind_east, wind_north, flux_east, flux_north], axis=0)
    fields, height_ext = lax.optimization_barrier((fields, height_ext))
    cut_rows = jnp.concatenate([face_rows[:-1], face_rows[:-1], face_rows[:-1], face_rows])
    row_cuts = jnp.broadcast_to(
        filter_cutoff[jnp.minimum(cut_rows, nlat_all - 1)][:, None], fields.shape[:2]
    ).reshape(-1)
    smooth = filter_rows(fields.reshape(-1, length), row_cuts).reshape(fields.shape)
    east_smooth = smooth[:rows]
    north_smooth = smooth[rows : 2 * rows]
    east_flux = smooth[2 * rows : 3 * rows]
    north_full = smooth[3 * rows :]
    new_mass = layer_mass - TIME_STEP * (
        jnp.roll(east_flux, -1, -1) - east_flux + (north_full[1:] - north_full[:-1])
    )
    heat_east = east_flux * face_lon(theta_field)
    heat_north = north_full * theta_faces
    new_heat = theta_field * layer_mass - TIME_STEP * (
        jnp.roll(heat_east, -1, -1) - heat_east + (heat_north[1:] - heat_north[:-1])
    )
    height = height_ext[1:]
    new_east = east_smooth - TIME_STEP * (height - jnp.roll(height, 1, -1))
    inside = (face_rows[:-1] > 0).astype(jnp.float32)[:, None, None]
    new_north = (north_smooth - TIME_STEP * (height - height_ext[:-1])) * inside
    outputs = (new_east, new_north, new_mass, new_heat, height)
    return tuple(jnp.transpose(v, (1, 0, 2)) for v in outputs)


def solution(mesh):
    in_specs = (
        P("lev", "lat", None),
        P("lev", "lat", None),
        P("lev", "lat", None),
        P("lev", "lat", None),
        P("lat", None),
        P(),
    )
    out_specs = (
        P("lev", "lat", None),
        P("lev", "lat", None),
        P("lev", "lat", None),
        P("lev", "lat", None),
        P("lev", "lat", None),
    )
    return jax.shard_map(local, mesh=mesh, in_specs=in_specs, out_specs=out_specs, check_vma=False)
```

```python
import numpy as np
import jax
import jax.numpy as jnp
from jax import lax
from jax.experimental import pallas as pl
from jax.sharding import PartitionSpec as P

TIME_STEP = 0.25
GAS_CONST = 1.0
TOP_PRESSURE = 1.0


def face_lon(values):
    return (
        37.0 * (jnp.roll(values, 1, -1) + values)
        - 8.0 * (jnp.roll(values, 2, -1) + jnp.roll(values, -1, -1))
        + (jnp.roll(values, 3, -1) + jnp.roll(values, -2, -1))
    ) / 60.0


def face_lat(padded, count):
    return (
        37.0 * (padded[2 : 2 + count] + padded[3 : 3 + count])
        - 8.0 * (padded[1 : 1 + count] + padded[4 : 4 + count])
        + (padded[0:count] + padded[5 : 5 + count])
    ) / 60.0


FACTOR_ROWS = 9
FACTOR_LANES = 128

def fft_tables(length):
    rows, lanes = FACTOR_ROWS, FACTOR_LANES
    small = np.arange(rows)
    small_phase = 2.0 * np.pi * np.outer(small, small) / rows
    low = np.arange(rows)[:, None]
    high = np.arange(lanes)[None, :]
    twist = 2.0 * np.pi * ((low * high) % length) / length
    waves = np.arange(lanes)
    wave_phase = 2.0 * np.pi * (np.outer(waves, waves) % lanes) / lanes
    wc, ws = np.cos(wave_phase), np.sin(wave_phase)
    forward = np.block([[wc, -ws], [ws, wc]]).astype(np.float32)
    inverse = np.block([[wc, ws], [-ws, wc]]).astype(np.float32)
    number = np.arange(rows)[:, None] + rows * np.arange(lanes)[None, :]
    folded = np.minimum(number, length - number)
    folded = np.concatenate([folded, folded], axis=1).astype(np.int32)
    return (np.cos(small_phase), np.sin(small_phase), np.cos(twist).astype(np.float32),
            np.sin(twist).astype(np.float32), forward, inverse, folded)

def split_table(table):
    high = jnp.asarray(table, jnp.float32).astype(jnp.bfloat16)
    low = (jnp.asarray(table, jnp.float32) - high.astype(jnp.float32)).astype(jnp.bfloat16)
    return jnp.stack([high, low])


def split_dot(values, table_high, table_low):
    high = values.astype(jnp.bfloat16)
    low = (values - high.astype(jnp.float32)).astype(jnp.bfloat16)
    product = lambda a, b: jnp.dot(a, b, preferred_element_type=jnp.float32)
    return product(high, table_high) + (product(high, table_low) + product(low, table_high))


def filter_kernel(x_ref, cut_ref, twc_ref, tws_ref, fwd_ref, inv_ref, fold_ref, *out_refs):
    rows, lanes = FACTOR_ROWS, FACTOR_LANES
    count, length = x_ref.shape
    c9, s9 = fft_tables(length)[:2]
    half = rows // 2 + 1
    parts = [x_ref[:, n * lanes : (n + 1) * lanes] for n in range(rows)]
    pairs = [parts[n] + parts[rows - n] for n in range(1, half)]
    gaps = [parts[n] - parts[rows - n] for n in range(1, half)]
    pieces = []
    for k in range(half):
        real_a = parts[0] + sum(float(c9[k, n]) * pairs[n - 1] for n in range(1, half))
        imag_a = sum(float(-s9[k, n]) * gaps[n - 1] for n in range(1, half))
        twc = twc_ref[k : k + 1, :]
        tws = tws_ref[k : k + 1, :]
        pieces.append(
            jnp.concatenate([real_a * twc + imag_a * tws, imag_a * twc - real_a * tws], axis=1)
        )
    spectrum = split_dot(jnp.concatenate(pieces, axis=0), fwd_ref[0], fwd_ref[1])
    cuts = cut_ref[...]
    keep = jnp.concatenate(
        [(fold_ref[k : k + 1, :] <= cuts).astype(jnp.float32) for k in range(half)], axis=0
    )
    back = split_dot(spectrum * keep, inv_ref[0], inv_ref[1])
    real_d, imag_d = [], []
    for k in range(half):
        twc = twc_ref[k : k + 1, :]
        tws = tws_ref[k : k + 1, :]
        real_c = back[k * count : (k + 1) * count, :lanes]
        imag_c = back[k * count : (k + 1) * count, lanes:]
        real_d.append(real_c * twc - imag_c * tws)
        imag_d.append(imag_c * twc + real_c * tws)
    base = float(1.0 / length) * real_d[0]

    def store(n, value):
        start = 0
        for ref in out_refs:
            size = ref.shape[0]
            ref[:, n * lanes : (n + 1) * lanes] = value[start : start + size]
            start += size

    for n in range(half):
        even = base + sum(float(2.0 * c9[k, n] / length) * real_d[k] for k in range(1, half))
        store(n, even - sum(float(2.0 * s9[k, n] / length) * imag_d[k] for k in range(1, half)))
        if n > 0:
            store(
                rows - n,
                even + sum(float(2.0 * s9[k, n] / length) * imag_d[k] for k in range(1, half)),
            )


def filter_rows(values, cuts, sizes):
    count, length = values.shape
    _, _, twc, tws, forward, inverse, folded = fft_tables(length)
    return pl.pallas_call(
        filter_kernel,
        out_shape=tuple(jax.ShapeDtypeStruct((size, length), values.dtype) for size in sizes),
    )(values, cuts.reshape(count, 1), jnp.asarray(twc), jnp.asarray(tws), split_table(forward),
      split_table(inverse), jnp.asarray(folded))

def prefix_over(value, axis, before):
    count = lax.axis_size(axis)
    rank = lax.axis_index(axis)
    copies = jnp.broadcast_to(value, (count, *value.shape))
    pieces = lax.all_to_all(copies, axis, split_axis=0, concat_axis=0, tiled=True)
    owners = jnp.arange(count, dtype=jnp.int32)
    chosen = owners < rank if before else owners > rank
    return jnp.sum(jnp.where(chosen[:, None, None], pieces, 0.0), axis=0)


def local(wind_east, wind_north, layer_mass, theta_field, surface_height, filter_cutoff):
    levels, lat_rows, length = wind_east.shape
    wind_east, wind_north, layer_mass, theta_field = (
        jnp.transpose(v, (1, 0, 2)) for v in (wind_east, wind_north, layer_mass, theta_field)
    )
    lat_count = lax.axis_size("lat")
    lat_rank = lax.axis_index("lat")
    nlat_all = lat_rows * lat_count
    first_row = lat_rank * lat_rows
    surface = jnp.broadcast_to(surface_height[:, None], (lat_rows, levels, length))
    to_north = jnp.concatenate([layer_mass, theta_field, surface], axis=0)
    to_south = jnp.concatenate([layer_mass, theta_field, wind_north], axis=0)
    count = lat_count
    from_south = lax.ppermute(to_north, "lat", [(i, i + 1) for i in range(count - 1)])
    from_north = lax.ppermute(to_south, "lat", [(i + 1, i) for i in range(count - 1)])
    rows = lat_rows
    mass_pad = jnp.concatenate([from_south[:rows], layer_mass, from_north[:rows]], axis=0)
    theta_pad = jnp.concatenate(
        [from_south[rows : 2 * rows], theta_field, from_north[rows : 2 * rows]], axis=0
    )
    face_rows = first_row + jnp.arange(lat_rows + 1, dtype=jnp.int32)
    coslat = jnp.sin(jnp.pi * face_rows.astype(jnp.float32) / nlat_all)[:, None, None]
    mass_faces = face_lat(mass_pad, lat_rows + 1)
    theta_faces = face_lat(theta_pad, lat_rows + 1)
    north_ext = jnp.concatenate([wind_north, from_north[2 * rows : 2 * rows + 1]], axis=0)
    flux_east = wind_east * face_lon(layer_mass)
    flux_north = north_ext * mass_faces * coslat
    mass_ext = jnp.concatenate([from_south[rows - 1 : rows], layer_mass], axis=0)
    theta_ext = jnp.concatenate([from_south[2 * rows - 1 : 2 * rows], theta_field], axis=0)
    surface_ext = jnp.concatenate([from_south[3 * rows - 1 :], surface], axis=0)
    column = jnp.sum(mass_ext, axis=1)
    above_mass = prefix_over(column, "lev", True)
    bottom = TOP_PRESSURE + above_mass[:, None] + jnp.cumsum(mass_ext, axis=1)
    top_press = bottom - mass_ext
    thickness = GAS_CONST * theta_ext * (jnp.log(bottom) - jnp.log(top_press))
    depth_sum = jnp.sum(thickness, axis=1)
    below_depth = prefix_over(depth_sum, "lev", False)
    inclusive = jnp.flip(jnp.cumsum(jnp.flip(thickness, 1), axis=1), 1)
    height_ext = surface_ext + below_depth[:, None] + (inclusive - thickness) + 0.5 * thickness
    fields = jnp.concatenate([wind_east, wind_north, flux_east, flux_north], axis=0)
    fields, height_ext = lax.optimization_barrier((fields, height_ext))
    cut_rows = jnp.concatenate([face_rows[:-1], face_rows[:-1], face_rows[:-1], face_rows])
    row_cuts = jnp.broadcast_to(
        filter_cutoff[jnp.minimum(cut_rows, nlat_all - 1)][:, None], fields.shape[:2]
    ).reshape(-1)
    sizes = (rows * levels, rows * levels, rows * levels, (rows + 1) * levels)
    east_smooth, north_smooth, east_flux, north_full = (
        v.reshape(-1, levels, length)
        for v in filter_rows(fields.reshape(-1, length), row_cuts, sizes)
    )
    new_mass = layer_mass - TIME_STEP * (
        jnp.roll(east_flux, -1, -1) - east_flux + (north_full[1:] - north_full[:-1])
    )
    heat_east = east_flux * face_lon(theta_field)
    heat_north = north_full * theta_faces
    new_heat = theta_field * layer_mass - TIME_STEP * (
        jnp.roll(heat_east, -1, -1) - heat_east + (heat_north[1:] - heat_north[:-1])
    )
    height = height_ext[1:]
    new_east = east_smooth - TIME_STEP * (height - jnp.roll(height, 1, -1))
    inside = (face_rows[:-1] > 0).astype(jnp.float32)[:, None, None]
    new_north = (north_smooth - TIME_STEP * (height - height_ext[:-1])) * inside
    outputs = (new_east, new_north, new_mass, new_heat, height)
    return tuple(jnp.transpose(v, (1, 0, 2)) for v in outputs)


def solution(mesh):
    in_specs = (
        P("lev", "lat", None),
        P("lev", "lat", None),
        P("lev", "lat", None),
        P("lev", "lat", None),
        P("lat", None),
        P(),
    )
    out_specs = (
        P("lev", "lat", None),
        P("lev", "lat", None),
        P("lev", "lat", None),
        P("lev", "lat", None),
        P("lev", "lat", None),
    )
    return jax.shard_map(local, mesh=mesh, in_specs=in_specs, out_specs=out_specs, check_vma=False)
```

```python
import numpy as np
import jax
import jax.numpy as jnp
from jax import lax
from jax.experimental import pallas as pl
from jax.experimental.pallas import tpu as pltpu
from jax.sharding import PartitionSpec as P

TIME_STEP = 0.25
GAS_CONST = 1.0
TOP_PRESSURE = 1.0


def face_lon(values):
    return (
        37.0 * (jnp.roll(values, 1, -1) + values)
        - 8.0 * (jnp.roll(values, 2, -1) + jnp.roll(values, -1, -1))
        + (jnp.roll(values, 3, -1) + jnp.roll(values, -2, -1))
    ) / 60.0


def face_lat(padded, count):
    return (
        37.0 * (padded[2 : 2 + count] + padded[3 : 3 + count])
        - 8.0 * (padded[1 : 1 + count] + padded[4 : 4 + count])
        + (padded[0:count] + padded[5 : 5 + count])
    ) / 60.0


FACTOR_ROWS = 9
FACTOR_LANES = 128

def fft_tables(length):
    rows, lanes = FACTOR_ROWS, FACTOR_LANES
    small = np.arange(rows)
    small_phase = 2.0 * np.pi * np.outer(small, small) / rows
    low = np.arange(rows)[:, None]
    high = np.arange(lanes)[None, :]
    twist = 2.0 * np.pi * ((low * high) % length) / length
    waves = np.arange(lanes)
    wave_phase = 2.0 * np.pi * (np.outer(waves, waves) % lanes) / lanes
    wc, ws = np.cos(wave_phase), np.sin(wave_phase)
    forward = np.block([[wc, -ws], [ws, wc]]).astype(np.float32)
    inverse = np.block([[wc, ws], [-ws, wc]]).astype(np.float32)
    number = np.arange(rows)[:, None] + rows * np.arange(lanes)[None, :]
    folded = np.minimum(number, length - number)
    folded = np.concatenate([folded, folded], axis=1).astype(np.int32)
    return (np.cos(small_phase), np.sin(small_phase), np.cos(twist).astype(np.float32),
            np.sin(twist).astype(np.float32), forward, inverse, folded)

def split_table(table):
    high = jnp.asarray(table, jnp.float32).astype(jnp.bfloat16)
    low = (jnp.asarray(table, jnp.float32) - high.astype(jnp.float32)).astype(jnp.bfloat16)
    return jnp.stack([high, low])


def split_dot(values, table_high, table_low):
    high = values.astype(jnp.bfloat16)
    low = (values - high.astype(jnp.float32)).astype(jnp.bfloat16)
    product = lambda a, b: jnp.dot(a, b, preferred_element_type=jnp.float32)
    return product(high, table_high) + (product(high, table_low) + product(low, table_high))


def filter_kernel(x_ref, cut_ref, twc_ref, tws_ref, fwd_ref, inv_ref, fold_ref, o_ref, roll_ref):
    rows, lanes = FACTOR_ROWS, FACTOR_LANES
    count, length = x_ref.shape
    c9, s9 = fft_tables(length)[:2]
    half = rows // 2 + 1
    parts = [x_ref[:, n * lanes : (n + 1) * lanes] for n in range(rows)]
    pairs = [parts[n] + parts[rows - n] for n in range(1, half)]
    gaps = [parts[n] - parts[rows - n] for n in range(1, half)]
    pieces = []
    for k in range(half):
        real_a = parts[0] + sum(float(c9[k, n]) * pairs[n - 1] for n in range(1, half))
        imag_a = sum(float(-s9[k, n]) * gaps[n - 1] for n in range(1, half))
        twc = twc_ref[k : k + 1, :]
        tws = tws_ref[k : k + 1, :]
        pieces.append(
            jnp.concatenate([real_a * twc + imag_a * tws, imag_a * twc - real_a * tws], axis=1)
        )
    spectrum = split_dot(jnp.concatenate(pieces, axis=0), fwd_ref[0], fwd_ref[1])
    cuts = cut_ref[...]
    keep = jnp.concatenate(
        [(fold_ref[k : k + 1, :] <= cuts).astype(jnp.float32) for k in range(half)], axis=0
    )
    back = split_dot(spectrum * keep, inv_ref[0], inv_ref[1])
    real_d, imag_d = [], []
    for k in range(half):
        twc = twc_ref[k : k + 1, :]
        tws = tws_ref[k : k + 1, :]
        real_c = back[k * count : (k + 1) * count, :lanes]
        imag_c = back[k * count : (k + 1) * count, lanes:]
        real_d.append(real_c * twc - imag_c * tws)
        imag_d.append(imag_c * twc + real_c * tws)
    base = float(1.0 / length) * real_d[0]
    for n in range(half):
        even = base + sum(float(2.0 * c9[k, n] / length) * real_d[k] for k in range(1, half))
        o_ref[:, n * lanes : (n + 1) * lanes] = even - sum(
            float(2.0 * s9[k, n] / length) * imag_d[k] for k in range(1, half)
        )
        if n > 0:
            o_ref[:, (rows - n) * lanes : (rows - n + 1) * lanes] = even + sum(
                float(2.0 * s9[k, n] / length) * imag_d[k] for k in range(1, half)
            )
    block = roll_ref.shape[0]
    roll_ref[...] = pltpu.roll(o_ref[2 * block : 3 * block, :], length - 1, 1)


def filter_rows(values, cuts, block):
    count, length = values.shape
    _, _, twc, tws, forward, inverse, folded = fft_tables(length)
    return pl.pallas_call(
        filter_kernel,
        out_shape=(
            jax.ShapeDtypeStruct(values.shape, values.dtype),
            jax.ShapeDtypeStruct((block, length), values.dtype),
        ),
    )(values, cuts.reshape(count, 1), jnp.asarray(twc), jnp.asarray(tws), split_table(forward),
      split_table(inverse), jnp.asarray(folded))

def prefix_over(value, axis, before):
    count = lax.axis_size(axis)
    rank = lax.axis_index(axis)
    copies = jnp.broadcast_to(value, (count, *value.shape))
    pieces = lax.all_to_all(copies, axis, split_axis=0, concat_axis=0, tiled=True)
    owners = jnp.arange(count, dtype=jnp.int32)
    chosen = owners < rank if before else owners > rank
    return jnp.sum(jnp.where(chosen[:, None, None], pieces, 0.0), axis=0)


def local(wind_east, wind_north, layer_mass, theta_field, surface_height, filter_cutoff):
    levels, lat_rows, length = wind_east.shape
    wind_east, wind_north, layer_mass, theta_field = (
        jnp.transpose(v, (1, 0, 2)) for v in (wind_east, wind_north, layer_mass, theta_field)
    )
    lat_count = lax.axis_size("lat")
    lat_rank = lax.axis_index("lat")
    nlat_all = lat_rows * lat_count
    first_row = lat_rank * lat_rows
    surface = jnp.broadcast_to(surface_height[:, None], (lat_rows, levels, length))
    to_north = jnp.concatenate([layer_mass, theta_field, surface], axis=0)
    to_south = jnp.concatenate([layer_mass, theta_field, wind_north], axis=0)
    count = lat_count
    from_south = lax.ppermute(to_north, "lat", [(i, i + 1) for i in range(count - 1)])
    from_north = lax.ppermute(to_south, "lat", [(i + 1, i) for i in range(count - 1)])
    rows = lat_rows
    mass_pad = jnp.concatenate([from_south[:rows], layer_mass, from_north[:rows]], axis=0)
    theta_pad = jnp.concatenate(
        [from_south[rows : 2 * rows], theta_field, from_north[rows : 2 * rows]], axis=0
    )
    face_rows = first_row + jnp.arange(lat_rows + 1, dtype=jnp.int32)
    coslat = jnp.sin(jnp.pi * face_rows.astype(jnp.float32) / nlat_all)[:, None, None]
    mass_faces = face_lat(mass_pad, lat_rows + 1)
    theta_faces = face_lat(theta_pad, lat_rows + 1)
    north_ext = jnp.concatenate([wind_north, from_north[2 * rows : 2 * rows + 1]], axis=0)
    flux_east = wind_east * face_lon(layer_mass)
    flux_north = north_ext * mass_faces * coslat
    mass_ext = jnp.concatenate([from_south[rows - 1 : rows], layer_mass], axis=0)
    theta_ext = jnp.concatenate([from_south[2 * rows - 1 : 2 * rows], theta_field], axis=0)
    surface_ext = jnp.concatenate([from_south[3 * rows - 1 :], surface], axis=0)
    column = jnp.sum(mass_ext, axis=1)
    above_mass = prefix_over(column, "lev", True)
    bottom = TOP_PRESSURE + above_mass[:, None] + jnp.cumsum(mass_ext, axis=1)
    top_press = bottom - mass_ext
    thickness = GAS_CONST * theta_ext * (jnp.log(bottom) - jnp.log(top_press))
    depth_sum = jnp.sum(thickness, axis=1)
    below_depth = prefix_over(depth_sum, "lev", False)
    inclusive = jnp.flip(jnp.cumsum(jnp.flip(thickness, 1), axis=1), 1)
    height_ext = surface_ext + below_depth[:, None] + (inclusive - thickness) + 0.5 * thickness
    fields = jnp.concatenate([wind_east, wind_north, flux_east, flux_north], axis=0)
    fields, height_ext = lax.optimization_barrier((fields, height_ext))
    cut_rows = jnp.concatenate([face_rows[:-1], face_rows[:-1], face_rows[:-1], face_rows])
    row_cuts = jnp.broadcast_to(
        filter_cutoff[jnp.minimum(cut_rows, nlat_all - 1)][:, None], fields.shape[:2]
    ).reshape(-1)
    smooth, east_next = filter_rows(fields.reshape(-1, length), row_cuts, rows * levels)
    smooth = smooth.reshape(fields.shape)
    east_next = east_next.reshape(rows, levels, length)
    east_smooth = smooth[:rows]
    north_smooth = smooth[rows : 2 * rows]
    east_flux = smooth[2 * rows : 3 * rows]
    north_full = smooth[3 * rows :]
    new_mass = layer_mass - TIME_STEP * (
        east_next - east_flux + (north_full[1:] - north_full[:-1])
    )
    lon_theta = face_lon(theta_field)
    heat_east = east_flux * lon_theta
    heat_next = east_next * jnp.roll(lon_theta, -1, -1)
    heat_north = north_full * theta_faces
    new_heat = theta_field * layer_mass - TIME_STEP * (
        heat_next - heat_east + (heat_north[1:] - heat_north[:-1])
    )
    height = height_ext[1:]
    new_east = east_smooth - TIME_STEP * (height - jnp.roll(height, 1, -1))
    inside = (face_rows[:-1] > 0).astype(jnp.float32)[:, None, None]
    new_north = (north_smooth - TIME_STEP * (height - height_ext[:-1])) * inside
    outputs = (new_east, new_north, new_mass, new_heat, height)
    return tuple(jnp.transpose(v, (1, 0, 2)) for v in outputs)


def solution(mesh):
    in_specs = (
        P("lev", "lat", None),
        P("lev", "lat", None),
        P("lev", "lat", None),
        P("lev", "lat", None),
        P("lat", None),
        P(),
    )
    out_specs = (
        P("lev", "lat", None),
        P("lev", "lat", None),
        P("lev", "lat", None),
        P("lev", "lat", None),
        P("lev", "lat", None),
    )
    return jax.shard_map(local, mesh=mesh, in_specs=in_specs, out_specs=out_specs, check_vma=False)
```

```python
import numpy as np
import jax
import jax.numpy as jnp
from jax import lax
from jax.experimental import pallas as pl
from jax.experimental.pallas import tpu as pltpu
from jax.sharding import PartitionSpec as P

TIME_STEP = 0.25
GAS_CONST = 1.0
TOP_PRESSURE = 1.0


def face_lon(values):
    return (
        37.0 * (jnp.roll(values, 1, -1) + values)
        - 8.0 * (jnp.roll(values, 2, -1) + jnp.roll(values, -1, -1))
        + (jnp.roll(values, 3, -1) + jnp.roll(values, -2, -1))
    ) / 60.0


def face_lat(padded, count):
    return (
        37.0 * (padded[2 : 2 + count] + padded[3 : 3 + count])
        - 8.0 * (padded[1 : 1 + count] + padded[4 : 4 + count])
        + (padded[0:count] + padded[5 : 5 + count])
    ) / 60.0


FACTOR_ROWS = 9
FACTOR_LANES = 128

def fft_tables(length):
    rows, lanes = FACTOR_ROWS, FACTOR_LANES
    small = np.arange(rows)
    small_phase = 2.0 * np.pi * np.outer(small, small) / rows
    low = np.arange(rows)[:, None]
    high = np.arange(lanes)[None, :]
    twist = 2.0 * np.pi * ((low * high) % length) / length
    waves = np.arange(lanes)
    wave_phase = 2.0 * np.pi * (np.outer(waves, waves) % lanes) / lanes
    wc, ws = np.cos(wave_phase), np.sin(wave_phase)
    forward = np.block([[wc, -ws], [ws, wc]]).astype(np.float32)
    inverse = np.block([[wc, ws], [-ws, wc]]).astype(np.float32)
    number = np.arange(rows)[:, None] + rows * np.arange(lanes)[None, :]
    folded = np.minimum(number, length - number)
    folded = np.concatenate([folded, folded], axis=1).astype(np.int32)
    return (np.cos(small_phase), np.sin(small_phase), np.cos(twist).astype(np.float32),
            np.sin(twist).astype(np.float32), forward, inverse, folded)

def split_table(table):
    high = jnp.asarray(table, jnp.float32).astype(jnp.bfloat16)
    low = (jnp.asarray(table, jnp.float32) - high.astype(jnp.float32)).astype(jnp.bfloat16)
    return jnp.stack([high, low])


def split_dot(values, table_high, table_low):
    high = values.astype(jnp.bfloat16)
    low = (values - high.astype(jnp.float32)).astype(jnp.bfloat16)
    product = lambda a, b: jnp.dot(a, b, preferred_element_type=jnp.float32)
    return product(high, table_high) + (product(high, table_low) + product(low, table_high))


def filter_kernel(x_ref, cut_ref, twc_ref, tws_ref, fwd_ref, inv_ref, fold_ref, o_ref, roll_ref):
    rows, lanes = FACTOR_ROWS, FACTOR_LANES
    count, length = x_ref.shape
    c9, s9 = fft_tables(length)[:2]
    half = rows // 2 + 1
    parts = [x_ref[:, n * lanes : (n + 1) * lanes] for n in range(rows)]
    pairs = [parts[n] + parts[rows - n] for n in range(1, half)]
    gaps = [parts[n] - parts[rows - n] for n in range(1, half)]
    pieces = []
    for k in range(half):
        real_a = parts[0] + sum(float(c9[k, n]) * pairs[n - 1] for n in range(1, half))
        imag_a = sum(float(-s9[k, n]) * gaps[n - 1] for n in range(1, half))
        twc = twc_ref[k : k + 1, :]
        tws = tws_ref[k : k + 1, :]
        pieces.append(
            jnp.concatenate([real_a * twc + imag_a * tws, imag_a * twc - real_a * tws], axis=1)
        )
    spectrum = split_dot(jnp.concatenate(pieces, axis=0), fwd_ref[0], fwd_ref[1])
    cuts = cut_ref[...]
    keep = jnp.concatenate(
        [(fold_ref[k : k + 1, :] <= cuts).astype(jnp.float32) for k in range(half)], axis=0
    )
    back = split_dot(spectrum * keep, inv_ref[0], inv_ref[1])
    real_d, imag_d = [], []
    for k in range(half):
        twc = twc_ref[k : k + 1, :]
        tws = tws_ref[k : k + 1, :]
        real_c = back[k * count : (k + 1) * count, :lanes]
        imag_c = back[k * count : (k + 1) * count, lanes:]
        real_d.append(real_c * twc - imag_c * tws)
        imag_d.append(imag_c * twc + real_c * tws)
    base = float(1.0 / length) * real_d[0]
    for n in range(half):
        even = base + sum(float(2.0 * c9[k, n] / length) * real_d[k] for k in range(1, half))
        o_ref[:, n * lanes : (n + 1) * lanes] = even - sum(
            float(2.0 * s9[k, n] / length) * imag_d[k] for k in range(1, half)
        )
        if n > 0:
            o_ref[:, (rows - n) * lanes : (rows - n + 1) * lanes] = even + sum(
                float(2.0 * s9[k, n] / length) * imag_d[k] for k in range(1, half)
            )
    block = roll_ref.shape[0]
    roll_ref[...] = pltpu.roll(o_ref[2 * block : 3 * block, :], length - 1, 1)


def filter_rows(values, cuts, block):
    count, length = values.shape
    _, _, twc, tws, forward, inverse, folded = fft_tables(length)
    return pl.pallas_call(
        filter_kernel,
        out_shape=(
            jax.ShapeDtypeStruct(values.shape, values.dtype),
            jax.ShapeDtypeStruct((block, length), values.dtype),
        ),
    )(values, cuts.reshape(count, 1), jnp.asarray(twc), jnp.asarray(tws), split_table(forward),
      split_table(inverse), jnp.asarray(folded))

def prefix_over(value, axis, before):
    count = lax.axis_size(axis)
    rank = lax.axis_index(axis)
    copies = jnp.broadcast_to(value, (count, *value.shape))
    pieces = lax.all_to_all(copies, axis, split_axis=0, concat_axis=0, tiled=True)
    owners = jnp.arange(count, dtype=jnp.int32)
    chosen = owners < rank if before else owners > rank
    return jnp.sum(jnp.where(chosen[:, None, None], pieces, 0.0), axis=0)


def local(wind_east, wind_north, layer_mass, theta_field, surface_height, filter_cutoff):
    levels, lat_rows, length = wind_east.shape
    wind_east, wind_north, layer_mass, theta_field = (
        jnp.transpose(v, (1, 0, 2)) for v in (wind_east, wind_north, layer_mass, theta_field)
    )
    lat_count = lax.axis_size("lat")
    lat_rank = lax.axis_index("lat")
    nlat_all = lat_rows * lat_count
    first_row = lat_rank * lat_rows
    surface = jnp.broadcast_to(surface_height[:, None], (lat_rows, levels, length))
    to_north = jnp.concatenate([layer_mass, theta_field, surface], axis=0)
    to_south = jnp.concatenate([layer_mass, theta_field, wind_north], axis=0)
    count = lat_count
    from_south = lax.ppermute(to_north, "lat", [(i, i + 1) for i in range(count - 1)])
    from_north = lax.ppermute(to_south, "lat", [(i + 1, i) for i in range(count - 1)])
    rows = lat_rows
    mass_pad = jnp.concatenate([from_south[:rows], layer_mass, from_north[:rows]], axis=0)
    theta_pad = jnp.concatenate(
        [from_south[rows : 2 * rows], theta_field, from_north[rows : 2 * rows]], axis=0
    )
    face_rows = first_row + jnp.arange(lat_rows + 1, dtype=jnp.int32)
    coslat = jnp.sin(jnp.pi * face_rows.astype(jnp.float32) / nlat_all)[:, None, None]
    mass_faces = face_lat(mass_pad, lat_rows + 1)
    theta_faces = face_lat(theta_pad, lat_rows + 1)
    north_ext = jnp.concatenate([wind_north, from_north[2 * rows : 2 * rows + 1]], axis=0)
    flux_east = wind_east * face_lon(layer_mass)
    flux_north = north_ext * mass_faces * coslat
    mass_ext = jnp.concatenate([from_south[rows - 1 : rows], layer_mass], axis=0)
    theta_ext = jnp.concatenate([from_south[2 * rows - 1 : 2 * rows], theta_field], axis=0)
    surface_ext = jnp.concatenate([from_south[3 * rows - 1 :], surface], axis=0)
    column = jnp.sum(mass_ext, axis=1)
    above_mass = prefix_over(column, "lev", True)
    bottom = TOP_PRESSURE + above_mass[:, None] + jnp.cumsum(mass_ext, axis=1)
    top_press = bottom - mass_ext
    thickness = GAS_CONST * theta_ext * (jnp.log(bottom) - jnp.log(top_press))
    depth_sum = jnp.sum(thickness, axis=1)
    below_depth = prefix_over(depth_sum, "lev", False)
    inclusive = jnp.flip(jnp.cumsum(jnp.flip(thickness, 1), axis=1), 1)
    height_ext = surface_ext + below_depth[:, None] + (inclusive - thickness) + 0.5 * thickness
    fields = jnp.concatenate([wind_east, wind_north, flux_east, flux_north], axis=0)
    fields, height_ext = lax.optimization_barrier((fields, height_ext))
    cut_rows = jnp.concatenate([face_rows[:-1], face_rows[:-1], face_rows[:-1], face_rows])
    row_cuts = jnp.broadcast_to(
        filter_cutoff[jnp.minimum(cut_rows, nlat_all - 1)][:, None], fields.shape[:2]
    ).reshape(-1)
    smooth, east_next = filter_rows(fields.reshape(-1, length), row_cuts, rows * levels)
    smooth = smooth.reshape(fields.shape)
    east_next = east_next.reshape(rows, levels, length)
    east_smooth = smooth[:rows]
    north_smooth = smooth[rows : 2 * rows]
    east_flux = smooth[2 * rows : 3 * rows]
    north_full = smooth[3 * rows :]
    new_mass = layer_mass - TIME_STEP * (
        east_next - east_flux + (north_full[1:] - north_full[:-1])
    )
    lon_theta = face_lon(theta_field)
    heat_east = east_flux * lon_theta
    heat_next = east_next * jnp.roll(lon_theta, -1, -1)
    new_heat = theta_field * layer_mass - TIME_STEP * (
        heat_next - heat_east + (north_full[1:] * theta_faces[1:] - north_full[:-1] * theta_faces[:-1])
    )
    height = height_ext[1:]
    new_east = east_smooth - TIME_STEP * (height - jnp.roll(height, 1, -1))
    inside = (face_rows[:-1] > 0).astype(jnp.float32)[:, None, None]
    new_north = (north_smooth - TIME_STEP * (height - height_ext[:-1])) * inside
    outputs = (new_east, new_north, new_mass, new_heat, height)
    return tuple(jnp.transpose(v, (1, 0, 2)) for v in outputs)


def solution(mesh):
    in_specs = (
        P("lev", "lat", None),
        P("lev", "lat", None),
        P("lev", "lat", None),
        P("lev", "lat", None),
        P("lat", None),
        P(),
    )
    out_specs = (
        P("lev", "lat", None),
        P("lev", "lat", None),
        P("lev", "lat", None),
        P("lev", "lat", None),
        P("lev", "lat", None),
    )
    return jax.shard_map(local, mesh=mesh, in_specs=in_specs, out_specs=out_specs, check_vma=False)
```

```python
import numpy as np
import jax
import jax.numpy as jnp
from jax import lax
from jax.experimental import pallas as pl
from jax.experimental.pallas import tpu as pltpu
from jax.sharding import PartitionSpec as P

TIME_STEP = 0.25
GAS_CONST = 1.0
TOP_PRESSURE = 1.0


def face_lon(values):
    return (
        37.0 * (jnp.roll(values, 1, -1) + values)
        - 8.0 * (jnp.roll(values, 2, -1) + jnp.roll(values, -1, -1))
        + (jnp.roll(values, 3, -1) + jnp.roll(values, -2, -1))
    ) / 60.0


def face_lat(padded, count):
    return (
        37.0 * (padded[2 : 2 + count] + padded[3 : 3 + count])
        - 8.0 * (padded[1 : 1 + count] + padded[4 : 4 + count])
        + (padded[0:count] + padded[5 : 5 + count])
    ) / 60.0


FACTOR_ROWS = 9
FACTOR_LANES = 128

def fft_tables(length):
    rows, lanes = FACTOR_ROWS, FACTOR_LANES
    small = np.arange(rows)
    small_phase = 2.0 * np.pi * np.outer(small, small) / rows
    low = np.arange(rows)[:, None]
    high = np.arange(lanes)[None, :]
    twist = 2.0 * np.pi * ((low * high) % length) / length
    waves = np.arange(lanes)
    wave_phase = 2.0 * np.pi * (np.outer(waves, waves) % lanes) / lanes
    wc, ws = np.cos(wave_phase), np.sin(wave_phase)
    forward = np.block([[wc, -ws], [ws, wc]]).astype(np.float32)
    inverse = np.block([[wc, ws], [-ws, wc]]).astype(np.float32)
    number = np.arange(rows)[:, None] + rows * np.arange(lanes)[None, :]
    folded = np.minimum(number, length - number)
    folded = np.concatenate([folded, folded], axis=1).astype(np.int32)
    return (np.cos(small_phase), np.sin(small_phase), np.cos(twist).astype(np.float32),
            np.sin(twist).astype(np.float32), forward, inverse, folded)

def split_table(table):
    high = jnp.asarray(table, jnp.float32).astype(jnp.bfloat16)
    low = (jnp.asarray(table, jnp.float32) - high.astype(jnp.float32)).astype(jnp.bfloat16)
    return jnp.stack([high, low])


def split_dot(values, table_high, table_low):
    high = values.astype(jnp.bfloat16)
    low = (values - high.astype(jnp.float32)).astype(jnp.bfloat16)
    product = lambda a, b: jnp.dot(a, b, preferred_element_type=jnp.float32)
    return product(high, table_high) + (product(high, table_low) + product(low, table_high))


def filter_kernel(x_ref, cut_ref, twc_ref, tws_ref, fwd_ref, inv_ref, fold_ref, o_ref, roll_ref):
    rows, lanes = FACTOR_ROWS, FACTOR_LANES
    count, length = x_ref.shape
    c9, s9 = fft_tables(length)[:2]
    half = rows // 2 + 1
    parts = [x_ref[:, n * lanes : (n + 1) * lanes] for n in range(rows)]
    pairs = [parts[n] + parts[rows - n] for n in range(1, half)]
    gaps = [parts[n] - parts[rows - n] for n in range(1, half)]
    pieces = []
    for k in range(half):
        real_a = parts[0] + sum(float(c9[k, n]) * pairs[n - 1] for n in range(1, half))
        imag_a = sum(float(-s9[k, n]) * gaps[n - 1] for n in range(1, half))
        twc = twc_ref[k : k + 1, :]
        tws = tws_ref[k : k + 1, :]
        pieces.append(
            jnp.concatenate([real_a * twc + imag_a * tws, imag_a * twc - real_a * tws], axis=1)
        )
    spectrum = split_dot(jnp.concatenate(pieces, axis=0), fwd_ref[0], fwd_ref[1])
    cuts = cut_ref[...]
    keep = jnp.concatenate(
        [(fold_ref[k : k + 1, :] <= cuts).astype(jnp.float32) for k in range(half)], axis=0
    )
    back = split_dot(spectrum * keep, inv_ref[0], inv_ref[1])
    real_d, imag_d = [], []
    for k in range(half):
        twc = twc_ref[k : k + 1, :]
        tws = tws_ref[k : k + 1, :]
        real_c = back[k * count : (k + 1) * count, :lanes]
        imag_c = back[k * count : (k + 1) * count, lanes:]
        real_d.append(real_c * twc - imag_c * tws)
        imag_d.append(imag_c * twc + real_c * tws)
    base = float(1.0 / length) * real_d[0]
    for n in range(half):
        even = base + sum(float(2.0 * c9[k, n] / length) * real_d[k] for k in range(1, half))
        o_ref[:, n * lanes : (n + 1) * lanes] = even - sum(
            float(2.0 * s9[k, n] / length) * imag_d[k] for k in range(1, half)
        )
        if n > 0:
            o_ref[:, (rows - n) * lanes : (rows - n + 1) * lanes] = even + sum(
                float(2.0 * s9[k, n] / length) * imag_d[k] for k in range(1, half)
            )
    block = roll_ref.shape[0]
    roll_ref[...] = pltpu.roll(o_ref[2 * block : 3 * block, :], length - 1, 1)


def filter_rows(values, cuts, block):
    count, length = values.shape
    _, _, twc, tws, forward, inverse, folded = fft_tables(length)
    return pl.pallas_call(
        filter_kernel,
        out_shape=(
            jax.ShapeDtypeStruct(values.shape, values.dtype),
            jax.ShapeDtypeStruct((block, length), values.dtype),
        ),
    )(values, cuts.reshape(count, 1), jnp.asarray(twc), jnp.asarray(tws), split_table(forward),
      split_table(inverse), jnp.asarray(folded))

def prefix_over(field, axis, before):
    count = lax.axis_size(axis)
    rank = lax.axis_index(axis)
    owners = jnp.arange(count, dtype=jnp.int32)
    live = (owners < count + rank).astype(field.dtype)
    copies = jnp.sum(field[None] * live[:, None, None, None], axis=2)
    pieces = lax.all_to_all(copies, axis, split_axis=0, concat_axis=0, tiled=True)
    chosen = owners < rank if before else owners > rank
    return jnp.sum(jnp.where(chosen[:, None, None], pieces, 0.0), axis=0)


def local(wind_east, wind_north, layer_mass, theta_field, surface_height, filter_cutoff):
    levels, lat_rows, length = wind_east.shape
    wind_east, wind_north, layer_mass, theta_field = (
        jnp.transpose(v, (1, 0, 2)) for v in (wind_east, wind_north, layer_mass, theta_field)
    )
    lat_count = lax.axis_size("lat")
    lat_rank = lax.axis_index("lat")
    nlat_all = lat_rows * lat_count
    first_row = lat_rank * lat_rows
    surface = jnp.broadcast_to(surface_height[:, None], (lat_rows, levels, length))
    to_north = jnp.concatenate([layer_mass, theta_field, surface], axis=0)
    to_south = jnp.concatenate([layer_mass, theta_field, wind_north], axis=0)
    count = lat_count
    from_south = lax.ppermute(to_north, "lat", [(i, i + 1) for i in range(count - 1)])
    from_north = lax.ppermute(to_south, "lat", [(i + 1, i) for i in range(count - 1)])
    rows = lat_rows
    mass_pad = jnp.concatenate([from_south[:rows], layer_mass, from_north[:rows]], axis=0)
    theta_pad = jnp.concatenate(
        [from_south[rows : 2 * rows], theta_field, from_north[rows : 2 * rows]], axis=0
    )
    face_rows = first_row + jnp.arange(lat_rows + 1, dtype=jnp.int32)
    coslat = jnp.sin(jnp.pi * face_rows.astype(jnp.float32) / nlat_all)[:, None, None]
    mass_faces = face_lat(mass_pad, lat_rows + 1)
    theta_faces = face_lat(theta_pad, lat_rows + 1)
    north_ext = jnp.concatenate([wind_north, from_north[2 * rows : 2 * rows + 1]], axis=0)
    flux_east = wind_east * face_lon(layer_mass)
    flux_north = north_ext * mass_faces * coslat
    mass_ext = jnp.concatenate([from_south[rows - 1 : rows], layer_mass], axis=0)
    theta_ext = jnp.concatenate([from_south[2 * rows - 1 : 2 * rows], theta_field], axis=0)
    surface_ext = jnp.concatenate([from_south[3 * rows - 1 :], surface], axis=0)
    above_mass = prefix_over(mass_ext, "lev", True)
    bottom = TOP_PRESSURE + above_mass[:, None] + jnp.cumsum(mass_ext, axis=1)
    top_press = bottom - mass_ext
    thickness = GAS_CONST * theta_ext * (jnp.log(bottom) - jnp.log(top_press))
    below_depth = prefix_over(thickness, "lev", False)
    inclusive = jnp.flip(jnp.cumsum(jnp.flip(thickness, 1), axis=1), 1)
    height_ext = surface_ext + below_depth[:, None] + (inclusive - thickness) + 0.5 * thickness
    fields = jnp.concatenate([wind_east, wind_north, flux_east, flux_north], axis=0)
    fields, height_ext = lax.optimization_barrier((fields, height_ext))
    cut_rows = jnp.concatenate([face_rows[:-1], face_rows[:-1], face_rows[:-1], face_rows])
    row_cuts = jnp.broadcast_to(
        filter_cutoff[jnp.minimum(cut_rows, nlat_all - 1)][:, None], fields.shape[:2]
    ).reshape(-1)
    smooth, east_next = filter_rows(fields.reshape(-1, length), row_cuts, rows * levels)
    smooth = smooth.reshape(fields.shape)
    east_next = east_next.reshape(rows, levels, length)
    east_smooth = smooth[:rows]
    north_smooth = smooth[rows : 2 * rows]
    east_flux = smooth[2 * rows : 3 * rows]
    north_full = smooth[3 * rows :]
    new_mass = layer_mass - TIME_STEP * (
        east_next - east_flux + (north_full[1:] - north_full[:-1])
    )
    lon_theta = face_lon(theta_field)
    heat_east = east_flux * lon_theta
    heat_next = east_next * jnp.roll(lon_theta, -1, -1)
    heat_north = north_full * theta_faces
    new_heat = theta_field * layer_mass - TIME_STEP * (
        heat_next - heat_east + (heat_north[1:] - heat_north[:-1])
    )
    height = height_ext[1:]
    new_east = east_smooth - TIME_STEP * (height - jnp.roll(height, 1, -1))
    inside = (face_rows[:-1] > 0).astype(jnp.float32)[:, None, None]
    new_north = (north_smooth - TIME_STEP * (height - height_ext[:-1])) * inside
    outputs = (new_east, new_north, new_mass, new_heat, height)
    return tuple(jnp.transpose(v, (1, 0, 2)) for v in outputs)


def solution(mesh):
    in_specs = (
        P("lev", "lat", None),
        P("lev", "lat", None),
        P("lev", "lat", None),
        P("lev", "lat", None),
        P("lat", None),
        P(),
    )
    out_specs = (
        P("lev", "lat", None),
        P("lev", "lat", None),
        P("lev", "lat", None),
        P("lev", "lat", None),
        P("lev", "lat", None),
    )
    return jax.shard_map(local, mesh=mesh, in_specs=in_specs, out_specs=out_specs, check_vma=False)
```

```python
import numpy as np
import jax
import jax.numpy as jnp
from jax import lax
from jax.experimental import pallas as pl
from jax.experimental.pallas import tpu as pltpu
from jax.sharding import PartitionSpec as P

TIME_STEP = 0.25
GAS_CONST = 1.0
TOP_PRESSURE = 1.0


def face_lon(values):
    return (
        37.0 * (jnp.roll(values, 1, -1) + values)
        - 8.0 * (jnp.roll(values, 2, -1) + jnp.roll(values, -1, -1))
        + (jnp.roll(values, 3, -1) + jnp.roll(values, -2, -1))
    ) / 60.0


def face_lat(padded, count):
    return (
        37.0 * (padded[2 : 2 + count] + padded[3 : 3 + count])
        - 8.0 * (padded[1 : 1 + count] + padded[4 : 4 + count])
        + (padded[0:count] + padded[5 : 5 + count])
    ) / 60.0


FACTOR_ROWS = 9
FACTOR_LANES = 128

def fft_tables(length):
    rows, lanes = FACTOR_ROWS, FACTOR_LANES
    small = np.arange(rows)
    small_phase = 2.0 * np.pi * np.outer(small, small) / rows
    low = np.arange(rows)[:, None]
    high = np.arange(lanes)[None, :]
    twist = 2.0 * np.pi * ((low * high) % length) / length
    waves = np.arange(lanes)
    wave_phase = 2.0 * np.pi * (np.outer(waves, waves) % lanes) / lanes
    wc, ws = np.cos(wave_phase), np.sin(wave_phase)
    forward = np.block([[wc, -ws], [ws, wc]]).astype(np.float32)
    inverse = np.block([[wc, ws], [-ws, wc]]).astype(np.float32)
    number = np.arange(rows)[:, None] + rows * np.arange(lanes)[None, :]
    folded = np.minimum(number, length - number)
    folded = np.concatenate([folded, folded], axis=1).astype(np.int32)
    return (np.cos(small_phase), np.sin(small_phase), np.cos(twist).astype(np.float32),
            np.sin(twist).astype(np.float32), forward, inverse, folded)

def split_table(table):
    high = jnp.asarray(table, jnp.float32).astype(jnp.bfloat16)
    low = (jnp.asarray(table, jnp.float32) - high.astype(jnp.float32)).astype(jnp.bfloat16)
    return jnp.stack([high, low])


def split_dot(values, table_high, table_low):
    high = values.astype(jnp.bfloat16)
    low = (values - high.astype(jnp.float32)).astype(jnp.bfloat16)
    product = lambda a, b: jnp.dot(a, b, preferred_element_type=jnp.float32)
    return product(high, table_high) + (product(high, table_low) + product(low, table_high))


def filter_kernel(
    x_ref, cut_ref, twc_ref, tws_ref, fwd_ref, inv_ref, fold_ref, face_ref, o_ref, roll_ref, heat_ref
):
    rows, lanes = FACTOR_ROWS, FACTOR_LANES
    count, length = x_ref.shape
    c9, s9 = fft_tables(length)[:2]
    half = rows // 2 + 1
    parts = [x_ref[:, n * lanes : (n + 1) * lanes] for n in range(rows)]
    pairs = [parts[n] + parts[rows - n] for n in range(1, half)]
    gaps = [parts[n] - parts[rows - n] for n in range(1, half)]
    pieces = []
    for k in range(half):
        real_a = parts[0] + sum(float(c9[k, n]) * pairs[n - 1] for n in range(1, half))
        imag_a = sum(float(-s9[k, n]) * gaps[n - 1] for n in range(1, half))
        twc = twc_ref[k : k + 1, :]
        tws = tws_ref[k : k + 1, :]
        pieces.append(
            jnp.concatenate([real_a * twc + imag_a * tws, imag_a * twc - real_a * tws], axis=1)
        )
    spectrum = split_dot(jnp.concatenate(pieces, axis=0), fwd_ref[0], fwd_ref[1])
    cuts = cut_ref[...]
    keep = jnp.concatenate(
        [(fold_ref[k : k + 1, :] <= cuts).astype(jnp.float32) for k in range(half)], axis=0
    )
    back = split_dot(spectrum * keep, inv_ref[0], inv_ref[1])
    real_d, imag_d = [], []
    for k in range(half):
        twc = twc_ref[k : k + 1, :]
        tws = tws_ref[k : k + 1, :]
        real_c = back[k * count : (k + 1) * count, :lanes]
        imag_c = back[k * count : (k + 1) * count, lanes:]
        real_d.append(real_c * twc - imag_c * tws)
        imag_d.append(imag_c * twc + real_c * tws)
    base = float(1.0 / length) * real_d[0]
    for n in range(half):
        even = base + sum(float(2.0 * c9[k, n] / length) * real_d[k] for k in range(1, half))
        o_ref[:, n * lanes : (n + 1) * lanes] = even - sum(
            float(2.0 * s9[k, n] / length) * imag_d[k] for k in range(1, half)
        )
        if n > 0:
            o_ref[:, (rows - n) * lanes : (rows - n + 1) * lanes] = even + sum(
                float(2.0 * s9[k, n] / length) * imag_d[k] for k in range(1, half)
            )
    block = roll_ref.shape[0]
    roll_ref[...] = pltpu.roll(o_ref[2 * block : 3 * block, :], length - 1, 1)
    heat_ref[...] = o_ref[3 * block : count, :] * face_ref[...]


def filter_rows(values, cuts, block, faces):
    count, length = values.shape
    _, _, twc, tws, forward, inverse, folded = fft_tables(length)
    return pl.pallas_call(
        filter_kernel,
        out_shape=(
            jax.ShapeDtypeStruct(values.shape, values.dtype),
            jax.ShapeDtypeStruct((block, length), values.dtype),
            jax.ShapeDtypeStruct(faces.shape, values.dtype),
        ),
    )(values, cuts.reshape(count, 1), jnp.asarray(twc), jnp.asarray(tws), split_table(forward),
      split_table(inverse), jnp.asarray(folded), faces)

def prefix_over(value, axis, before):
    count = lax.axis_size(axis)
    rank = lax.axis_index(axis)
    copies = jnp.broadcast_to(value, (count, *value.shape))
    pieces = lax.all_to_all(copies, axis, split_axis=0, concat_axis=0, tiled=True)
    owners = jnp.arange(count, dtype=jnp.int32)
    chosen = owners < rank if before else owners > rank
    return jnp.sum(jnp.where(chosen[:, None, None], pieces, 0.0), axis=0)


def local(wind_east, wind_north, layer_mass, theta_field, surface_height, filter_cutoff):
    levels, lat_rows, length = wind_east.shape
    wind_east, wind_north, layer_mass, theta_field = (
        jnp.transpose(v, (1, 0, 2)) for v in (wind_east, wind_north, layer_mass, theta_field)
    )
    lat_count = lax.axis_size("lat")
    lat_rank = lax.axis_index("lat")
    nlat_all = lat_rows * lat_count
    first_row = lat_rank * lat_rows
    surface = jnp.broadcast_to(surface_height[:, None], (lat_rows, levels, length))
    to_north = jnp.concatenate([layer_mass, theta_field, surface], axis=0)
    to_south = jnp.concatenate([layer_mass, theta_field, wind_north], axis=0)
    count = lat_count
    from_south = lax.ppermute(to_north, "lat", [(i, i + 1) for i in range(count - 1)])
    from_north = lax.ppermute(to_south, "lat", [(i + 1, i) for i in range(count - 1)])
    rows = lat_rows
    mass_pad = jnp.concatenate([from_south[:rows], layer_mass, from_north[:rows]], axis=0)
    theta_pad = jnp.concatenate(
        [from_south[rows : 2 * rows], theta_field, from_north[rows : 2 * rows]], axis=0
    )
    face_rows = first_row + jnp.arange(lat_rows + 1, dtype=jnp.int32)
    coslat = jnp.sin(jnp.pi * face_rows.astype(jnp.float32) / nlat_all)[:, None, None]
    mass_faces = face_lat(mass_pad, lat_rows + 1)
    theta_faces = face_lat(theta_pad, lat_rows + 1)
    north_ext = jnp.concatenate([wind_north, from_north[2 * rows : 2 * rows + 1]], axis=0)
    flux_east = wind_east * face_lon(layer_mass)
    flux_north = north_ext * mass_faces * coslat
    mass_ext = jnp.concatenate([from_south[rows - 1 : rows], layer_mass], axis=0)
    theta_ext = jnp.concatenate([from_south[2 * rows - 1 : 2 * rows], theta_field], axis=0)
    surface_ext = jnp.concatenate([from_south[3 * rows - 1 :], surface], axis=0)
    column = jnp.sum(mass_ext, axis=1)
    above_mass = prefix_over(column, "lev", True)
    bottom = TOP_PRESSURE + above_mass[:, None] + jnp.cumsum(mass_ext, axis=1)
    top_press = bottom - mass_ext
    thickness = GAS_CONST * theta_ext * (jnp.log(bottom) - jnp.log(top_press))
    depth_sum = jnp.sum(thickness, axis=1)
    below_depth = prefix_over(depth_sum, "lev", False)
    inclusive = jnp.flip(jnp.cumsum(jnp.flip(thickness, 1), axis=1), 1)
    height_ext = surface_ext + below_depth[:, None] + (inclusive - thickness) + 0.5 * thickness
    fields = jnp.concatenate([wind_east, wind_north, flux_east, flux_north], axis=0)
    fields, height_ext = lax.optimization_barrier((fields, height_ext))
    cut_rows = jnp.concatenate([face_rows[:-1], face_rows[:-1], face_rows[:-1], face_rows])
    row_cuts = jnp.broadcast_to(
        filter_cutoff[jnp.minimum(cut_rows, nlat_all - 1)][:, None], fields.shape[:2]
    ).reshape(-1)
    smooth, east_next, heat_north = filter_rows(
        fields.reshape(-1, length), row_cuts, rows * levels, theta_faces.reshape(-1, length)
    )
    heat_north = heat_north.reshape(rows + 1, levels, length)
    smooth = smooth.reshape(fields.shape)
    east_next = east_next.reshape(rows, levels, length)
    east_smooth = smooth[:rows]
    north_smooth = smooth[rows : 2 * rows]
    east_flux = smooth[2 * rows : 3 * rows]
    north_full = smooth[3 * rows :]
    new_mass = layer_mass - TIME_STEP * (
        east_next - east_flux + (north_full[1:] - north_full[:-1])
    )
    lon_theta = face_lon(theta_field)
    heat_east = east_flux * lon_theta
    heat_next = east_next * jnp.roll(lon_theta, -1, -1)
    new_heat = theta_field * layer_mass - TIME_STEP * (
        heat_next - heat_east + (heat_north[1:] - heat_north[:-1])
    )
    height = height_ext[1:]
    new_east = east_smooth - TIME_STEP * (height - jnp.roll(height, 1, -1))
    inside = (face_rows[:-1] > 0).astype(jnp.float32)[:, None, None]
    new_north = (north_smooth - TIME_STEP * (height - height_ext[:-1])) * inside
    outputs = (new_east, new_north, new_mass, new_heat, height)
    return tuple(jnp.transpose(v, (1, 0, 2)) for v in outputs)


def solution(mesh):
    in_specs = (
        P("lev", "lat", None),
        P("lev", "lat", None),
        P("lev", "lat", None),
        P("lev", "lat", None),
        P("lat", None),
        P(),
    )
    out_specs = (
        P("lev", "lat", None),
        P("lev", "lat", None),
        P("lev", "lat", None),
        P("lev", "lat", None),
        P("lev", "lat", None),
    )
    return jax.shard_map(local, mesh=mesh, in_specs=in_specs, out_specs=out_specs, check_vma=False)
```

```python
import numpy as np
import jax
import jax.numpy as jnp
from jax import lax
from jax.experimental import pallas as pl
from jax.experimental.pallas import tpu as pltpu
from jax.sharding import PartitionSpec as P

TIME_STEP = 0.25
GAS_CONST = 1.0
TOP_PRESSURE = 1.0


def face_lon(values):
    return (
        37.0 * (jnp.roll(values, 1, -1) + values)
        - 8.0 * (jnp.roll(values, 2, -1) + jnp.roll(values, -1, -1))
        + (jnp.roll(values, 3, -1) + jnp.roll(values, -2, -1))
    ) / 60.0


def face_lat(padded, count):
    return (
        37.0 * (padded[2 : 2 + count] + padded[3 : 3 + count])
        - 8.0 * (padded[1 : 1 + count] + padded[4 : 4 + count])
        + (padded[0:count] + padded[5 : 5 + count])
    ) / 60.0


FACTOR_ROWS = 9
FACTOR_LANES = 128

def fft_tables(length):
    rows, lanes = FACTOR_ROWS, FACTOR_LANES
    small = np.arange(rows)
    small_phase = 2.0 * np.pi * np.outer(small, small) / rows
    low = np.arange(rows)[:, None]
    high = np.arange(lanes)[None, :]
    twist = 2.0 * np.pi * ((low * high) % length) / length
    waves = np.arange(lanes)
    wave_phase = 2.0 * np.pi * (np.outer(waves, waves) % lanes) / lanes
    wc, ws = np.cos(wave_phase), np.sin(wave_phase)
    forward = np.block([[wc, -ws], [ws, wc]]).astype(np.float32)
    inverse = np.block([[wc, ws], [-ws, wc]]).astype(np.float32)
    number = np.arange(rows)[:, None] + rows * np.arange(lanes)[None, :]
    folded = np.minimum(number, length - number)
    folded = np.concatenate([folded, folded], axis=1).astype(np.int32)
    return (np.cos(small_phase), np.sin(small_phase), np.cos(twist).astype(np.float32),
            np.sin(twist).astype(np.float32), forward, inverse, folded)

def split_table(table):
    high = jnp.asarray(table, jnp.float32).astype(jnp.bfloat16)
    low = (jnp.asarray(table, jnp.float32) - high.astype(jnp.float32)).astype(jnp.bfloat16)
    return jnp.stack([high, low])


def split_dot(values, table_high, table_low):
    high = values.astype(jnp.bfloat16)
    low = (values - high.astype(jnp.float32)).astype(jnp.bfloat16)
    product = lambda a, b: jnp.dot(a, b, preferred_element_type=jnp.float32)
    return product(high, table_high) + (product(high, table_low) + product(low, table_high))


def filter_kernel(x_ref, cut_ref, twc_ref, tws_ref, fwd_ref, inv_ref, fold_ref, o_ref, roll_ref):
    rows, lanes = FACTOR_ROWS, FACTOR_LANES
    count, length = x_ref.shape
    c9, s9 = fft_tables(length)[:2]
    half = rows // 2 + 1
    parts = [x_ref[:, n * lanes : (n + 1) * lanes] for n in range(rows)]
    pairs = [parts[n] + parts[rows - n] for n in range(1, half)]
    gaps = [parts[n] - parts[rows - n] for n in range(1, half)]
    pieces = []
    for k in range(half):
        real_a = parts[0] + sum(float(c9[k, n]) * pairs[n - 1] for n in range(1, half))
        if k == 0:
            pieces.append(jnp.concatenate([real_a, jnp.zeros_like(real_a)], axis=1))
            continue
        imag_a = sum(float(-s9[k, n]) * gaps[n - 1] for n in range(1, half))
        twc = twc_ref[k : k + 1, :]
        tws = tws_ref[k : k + 1, :]
        pieces.append(
            jnp.concatenate([real_a * twc + imag_a * tws, imag_a * twc - real_a * tws], axis=1)
        )
    spectrum = split_dot(jnp.concatenate(pieces, axis=0), fwd_ref[0], fwd_ref[1])
    cuts = cut_ref[...]
    keep = jnp.concatenate(
        [(fold_ref[k : k + 1, :] <= cuts).astype(jnp.float32) for k in range(half)], axis=0
    )
    back = split_dot(spectrum * keep, inv_ref[0], inv_ref[1])
    real_d, imag_d = [], []
    for k in range(half):
        twc = twc_ref[k : k + 1, :]
        tws = tws_ref[k : k + 1, :]
        real_c = back[k * count : (k + 1) * count, :lanes]
        imag_c = back[k * count : (k + 1) * count, lanes:]
        if k == 0:
            real_d.append(real_c)
            imag_d.append(imag_c)
            continue
        real_d.append(real_c * twc - imag_c * tws)
        imag_d.append(imag_c * twc + real_c * tws)
    base = float(1.0 / length) * real_d[0]
    for n in range(half):
        even = base + sum(float(2.0 * c9[k, n] / length) * real_d[k] for k in range(1, half))
        o_ref[:, n * lanes : (n + 1) * lanes] = even - sum(
            float(2.0 * s9[k, n] / length) * imag_d[k] for k in range(1, half)
        )
        if n > 0:
            o_ref[:, (rows - n) * lanes : (rows - n + 1) * lanes] = even + sum(
                float(2.0 * s9[k, n] / length) * imag_d[k] for k in range(1, half)
            )
    block = roll_ref.shape[0]
    roll_ref[...] = pltpu.roll(o_ref[2 * block : 3 * block, :], length - 1, 1)


def filter_rows(values, cuts, block):
    count, length = values.shape
    _, _, twc, tws, forward, inverse, folded = fft_tables(length)
    return pl.pallas_call(
        filter_kernel,
        out_shape=(
            jax.ShapeDtypeStruct(values.shape, values.dtype),
            jax.ShapeDtypeStruct((block, length), values.dtype),
        ),
    )(values, cuts.reshape(count, 1), jnp.asarray(twc), jnp.asarray(tws), split_table(forward),
      split_table(inverse), jnp.asarray(folded))

def prefix_over(value, axis, before):
    count = lax.axis_size(axis)
    rank = lax.axis_index(axis)
    copies = jnp.broadcast_to(value, (count, *value.shape))
    pieces = lax.all_to_all(copies, axis, split_axis=0, concat_axis=0, tiled=True)
    owners = jnp.arange(count, dtype=jnp.int32)
    chosen = owners < rank if before else owners > rank
    return jnp.sum(jnp.where(chosen[:, None, None], pieces, 0.0), axis=0)


def local(wind_east, wind_north, layer_mass, theta_field, surface_height, filter_cutoff):
    levels, lat_rows, length = wind_east.shape
    wind_east, wind_north, layer_mass, theta_field = (
        jnp.transpose(v, (1, 0, 2)) for v in (wind_east, wind_north, layer_mass, theta_field)
    )
    lat_count = lax.axis_size("lat")
    lat_rank = lax.axis_index("lat")
    nlat_all = lat_rows * lat_count
    first_row = lat_rank * lat_rows
    surface = jnp.broadcast_to(surface_height[:, None], (lat_rows, levels, length))
    to_north = jnp.concatenate([layer_mass, theta_field, surface], axis=0)
    to_south = jnp.concatenate([layer_mass, theta_field, wind_north], axis=0)
    count = lat_count
    from_south = lax.ppermute(to_north, "lat", [(i, i + 1) for i in range(count - 1)])
    from_north = lax.ppermute(to_south, "lat", [(i + 1, i) for i in range(count - 1)])
    rows = lat_rows
    mass_pad = jnp.concatenate([from_south[:rows], layer_mass, from_north[:rows]], axis=0)
    theta_pad = jnp.concatenate(
        [from_south[rows : 2 * rows], theta_field, from_north[rows : 2 * rows]], axis=0
    )
    face_rows = first_row + jnp.arange(lat_rows + 1, dtype=jnp.int32)
    coslat = jnp.sin(jnp.pi * face_rows.astype(jnp.float32) / nlat_all)[:, None, None]
    mass_faces = face_lat(mass_pad, lat_rows + 1)
    theta_faces = face_lat(theta_pad, lat_rows + 1)
    north_ext = jnp.concatenate([wind_north, from_north[2 * rows : 2 * rows + 1]], axis=0)
    flux_east = wind_east * face_lon(layer_mass)
    flux_north = north_ext * mass_faces * coslat
    mass_ext = jnp.concatenate([from_south[rows - 1 : rows], layer_mass], axis=0)
    theta_ext = jnp.concatenate([from_south[2 * rows - 1 : 2 * rows], theta_field], axis=0)
    surface_ext = jnp.concatenate([from_south[3 * rows - 1 :], surface], axis=0)
    column = jnp.sum(mass_ext, axis=1)
    above_mass = prefix_over(column, "lev", True)
    bottom = TOP_PRESSURE + above_mass[:, None] + jnp.cumsum(mass_ext, axis=1)
    top_press = bottom - mass_ext
    thickness = GAS_CONST * theta_ext * (jnp.log(bottom) - jnp.log(top_press))
    depth_sum = jnp.sum(thickness, axis=1)
    below_depth = prefix_over(depth_sum, "lev", False)
    inclusive = jnp.flip(jnp.cumsum(jnp.flip(thickness, 1), axis=1), 1)
    height_ext = surface_ext + below_depth[:, None] + (inclusive - thickness) + 0.5 * thickness
    fields = jnp.concatenate([wind_east, wind_north, flux_east, flux_north], axis=0)
    fields, height_ext = lax.optimization_barrier((fields, height_ext))
    cut_rows = jnp.concatenate([face_rows[:-1], face_rows[:-1], face_rows[:-1], face_rows])
    row_cuts = jnp.broadcast_to(
        filter_cutoff[jnp.minimum(cut_rows, nlat_all - 1)][:, None], fields.shape[:2]
    ).reshape(-1)
    smooth, east_next = filter_rows(fields.reshape(-1, length), row_cuts, rows * levels)
    smooth = smooth.reshape(fields.shape)
    east_next = east_next.reshape(rows, levels, length)
    east_smooth = smooth[:rows]
    north_smooth = smooth[rows : 2 * rows]
    east_flux = smooth[2 * rows : 3 * rows]
    north_full = smooth[3 * rows :]
    new_mass = layer_mass - TIME_STEP * (
        east_next - east_flux + (north_full[1:] - north_full[:-1])
    )
    lon_theta = face_lon(theta_field)
    heat_east = east_flux * lon_theta
    heat_next = east_next * jnp.roll(lon_theta, -1, -1)
    heat_north = north_full * theta_faces
    new_heat = theta_field * layer_mass - TIME_STEP * (
        heat_next - heat_east + (heat_north[1:] - heat_north[:-1])
    )
    height = height_ext[1:]
    new_east = east_smooth - TIME_STEP * (height - jnp.roll(height, 1, -1))
    inside = (face_rows[:-1] > 0).astype(jnp.float32)[:, None, None]
    new_north = (north_smooth - TIME_STEP * (height - height_ext[:-1])) * inside
    outputs = (new_east, new_north, new_mass, new_heat, height)
    return tuple(jnp.transpose(v, (1, 0, 2)) for v in outputs)


def solution(mesh):
    in_specs = (
        P("lev", "lat", None),
        P("lev", "lat", None),
        P("lev", "lat", None),
        P("lev", "lat", None),
        P("lat", None),
        P(),
    )
    out_specs = (
        P("lev", "lat", None),
        P("lev", "lat", None),
        P("lev", "lat", None),
        P("lev", "lat", None),
        P("lev", "lat", None),
    )
    return jax.shard_map(local, mesh=mesh, in_specs=in_specs, out_specs=out_specs, check_vma=False)
```

```python
import numpy as np
import jax
import jax.numpy as jnp
from jax import lax
from jax.experimental import pallas as pl
from jax.experimental.pallas import tpu as pltpu
from jax.sharding import PartitionSpec as P

TIME_STEP = 0.25
GAS_CONST = 1.0
TOP_PRESSURE = 1.0


def face_lon(values):
    return (
        37.0 * (jnp.roll(values, 1, -1) + values)
        - 8.0 * (jnp.roll(values, 2, -1) + jnp.roll(values, -1, -1))
        + (jnp.roll(values, 3, -1) + jnp.roll(values, -2, -1))
    ) / 60.0


def face_lat(padded, count):
    return (
        37.0 * (padded[2 : 2 + count] + padded[3 : 3 + count])
        - 8.0 * (padded[1 : 1 + count] + padded[4 : 4 + count])
        + (padded[0:count] + padded[5 : 5 + count])
    ) / 60.0


FACTOR_ROWS = 9
FACTOR_LANES = 128

def fft_tables(length):
    rows, lanes = FACTOR_ROWS, FACTOR_LANES
    small = np.arange(rows)
    small_phase = 2.0 * np.pi * np.outer(small, small) / rows
    low = np.arange(rows)[:, None]
    high = np.arange(lanes)[None, :]
    twist = 2.0 * np.pi * ((low * high) % length) / length
    waves = np.arange(lanes)
    wave_phase = 2.0 * np.pi * (np.outer(waves, waves) % lanes) / lanes
    wc, ws = np.cos(wave_phase), np.sin(wave_phase)
    forward = np.block([[wc, -ws], [ws, wc]]).astype(np.float32)
    inverse = np.block([[wc, ws], [-ws, wc]]).astype(np.float32)
    number = np.arange(rows)[:, None] + rows * np.arange(lanes)[None, :]
    folded = np.minimum(number, length - number)
    folded = np.concatenate([folded, folded], axis=1).astype(np.int32)
    return (np.cos(small_phase), np.sin(small_phase), np.cos(twist).astype(np.float32),
            np.sin(twist).astype(np.float32), forward, inverse, folded)

def split_table(table):
    high = jnp.asarray(table, jnp.float32).astype(jnp.bfloat16)
    low = (jnp.asarray(table, jnp.float32) - high.astype(jnp.float32)).astype(jnp.bfloat16)
    return jnp.stack([high, low])


def split_dot(values, table_high, table_low):
    high = values.astype(jnp.bfloat16)
    low = (values - high.astype(jnp.float32)).astype(jnp.bfloat16)
    product = lambda a, b: jnp.dot(a, b, preferred_element_type=jnp.float32)
    return product(high, table_high) + (product(high, table_low) + product(low, table_high))


def filter_kernel(x_ref, cut_ref, twc_ref, tws_ref, fwd_ref, inv_ref, fold_ref, o_ref, roll_ref):
    rows, lanes = FACTOR_ROWS, FACTOR_LANES
    count, length = x_ref.shape
    c9, s9 = fft_tables(length)[:2]
    half = rows // 2 + 1
    parts = [x_ref[:, n * lanes : (n + 1) * lanes] for n in range(rows)]
    pairs = [parts[n] + parts[rows - n] for n in range(1, half)]
    gaps = [parts[n] - parts[rows - n] for n in range(1, half)]
    pieces = []
    for k in range(half):
        real_a = parts[0] + sum(float(c9[k, n]) * pairs[n - 1] for n in range(1, half))
        imag_a = sum(float(-s9[k, n]) * gaps[n - 1] for n in range(1, half))
        twc = twc_ref[k : k + 1, :]
        tws = tws_ref[k : k + 1, :]
        pieces.append(
            jnp.concatenate([real_a * twc + imag_a * tws, imag_a * twc - real_a * tws], axis=1)
        )
    spectrum = split_dot(jnp.concatenate(pieces, axis=0), fwd_ref[0], fwd_ref[1])
    keep = cut_ref[...]
    back = split_dot(spectrum * keep, inv_ref[0], inv_ref[1])
    real_d, imag_d = [], []
    for k in range(half):
        twc = twc_ref[k : k + 1, :]
        tws = tws_ref[k : k + 1, :]
        real_c = back[k * count : (k + 1) * count, :lanes]
        imag_c = back[k * count : (k + 1) * count, lanes:]
        real_d.append(real_c * twc - imag_c * tws)
        imag_d.append(imag_c * twc + real_c * tws)
    base = float(1.0 / length) * real_d[0]
    for n in range(half):
        even = base + sum(float(2.0 * c9[k, n] / length) * real_d[k] for k in range(1, half))
        o_ref[:, n * lanes : (n + 1) * lanes] = even - sum(
            float(2.0 * s9[k, n] / length) * imag_d[k] for k in range(1, half)
        )
        if n > 0:
            o_ref[:, (rows - n) * lanes : (rows - n + 1) * lanes] = even + sum(
                float(2.0 * s9[k, n] / length) * imag_d[k] for k in range(1, half)
            )
    block = roll_ref.shape[0]
    roll_ref[...] = pltpu.roll(o_ref[2 * block : 3 * block, :], length - 1, 1)


def filter_rows(values, cuts, block):
    count, length = values.shape
    _, _, twc, tws, forward, inverse, folded = fft_tables(length)
    return pl.pallas_call(
        filter_kernel,
        out_shape=(
            jax.ShapeDtypeStruct(values.shape, values.dtype),
            jax.ShapeDtypeStruct((block, length), values.dtype),
        ),
    )(values, (jnp.asarray(folded)[: FACTOR_ROWS // 2 + 1, None, :] <= cuts[None, :, None])
      .astype(jnp.float32).reshape(-1, folded.shape[1]), jnp.asarray(twc), jnp.asarray(tws), split_table(forward),
      split_table(inverse), jnp.asarray(folded))

def prefix_over(value, axis, before):
    count = lax.axis_size(axis)
    rank = lax.axis_index(axis)
    copies = jnp.broadcast_to(value, (count, *value.shape))
    pieces = lax.all_to_all(copies, axis, split_axis=0, concat_axis=0, tiled=True)
    owners = jnp.arange(count, dtype=jnp.int32)
    chosen = owners < rank if before else owners > rank
    return jnp.sum(jnp.where(chosen[:, None, None], pieces, 0.0), axis=0)


def local(wind_east, wind_north, layer_mass, theta_field, surface_height, filter_cutoff):
    levels, lat_rows, length = wind_east.shape
    wind_east, wind_north, layer_mass, theta_field = (
        jnp.transpose(v, (1, 0, 2)) for v in (wind_east, wind_north, layer_mass, theta_field)
    )
    lat_count = lax.axis_size("lat")
    lat_rank = lax.axis_index("lat")
    nlat_all = lat_rows * lat_count
    first_row = lat_rank * lat_rows
    surface = jnp.broadcast_to(surface_height[:, None], (lat_rows, levels, length))
    to_north = jnp.concatenate([layer_mass, theta_field, surface], axis=0)
    to_south = jnp.concatenate([layer_mass, theta_field, wind_north], axis=0)
    count = lat_count
    from_south = lax.ppermute(to_north, "lat", [(i, i + 1) for i in range(count - 1)])
    from_north = lax.ppermute(to_south, "lat", [(i + 1, i) for i in range(count - 1)])
    rows = lat_rows
    mass_pad = jnp.concatenate([from_south[:rows], layer_mass, from_north[:rows]], axis=0)
    theta_pad = jnp.concatenate(
        [from_south[rows : 2 * rows], theta_field, from_north[rows : 2 * rows]], axis=0
    )
    face_rows = first_row + jnp.arange(lat_rows + 1, dtype=jnp.int32)
    coslat = jnp.sin(jnp.pi * face_rows.astype(jnp.float32) / nlat_all)[:, None, None]
    mass_faces = face_lat(mass_pad, lat_rows + 1)
    theta_faces = face_lat(theta_pad, lat_rows + 1)
    north_ext = jnp.concatenate([wind_north, from_north[2 * rows : 2 * rows + 1]], axis=0)
    flux_east = wind_east * face_lon(layer_mass)
    flux_north = north_ext * mass_faces * coslat
    mass_ext = jnp.concatenate([from_south[rows - 1 : rows], layer_mass], axis=0)
    theta_ext = jnp.concatenate([from_south[2 * rows - 1 : 2 * rows], theta_field], axis=0)
    surface_ext = jnp.concatenate([from_south[3 * rows - 1 :], surface], axis=0)
    column = jnp.sum(mass_ext, axis=1)
    above_mass = prefix_over(column, "lev", True)
    bottom = TOP_PRESSURE + above_mass[:, None] + jnp.cumsum(mass_ext, axis=1)
    top_press = bottom - mass_ext
    thickness = GAS_CONST * theta_ext * (jnp.log(bottom) - jnp.log(top_press))
    depth_sum = jnp.sum(thickness, axis=1)
    below_depth = prefix_over(depth_sum, "lev", False)
    inclusive = jnp.flip(jnp.cumsum(jnp.flip(thickness, 1), axis=1), 1)
    height_ext = surface_ext + below_depth[:, None] + (inclusive - thickness) + 0.5 * thickness
    fields = jnp.concatenate([wind_east, wind_north, flux_east, flux_north], axis=0)
    fields, height_ext = lax.optimization_barrier((fields, height_ext))
    cut_rows = jnp.concatenate([face_rows[:-1], face_rows[:-1], face_rows[:-1], face_rows])
    row_cuts = jnp.broadcast_to(
        filter_cutoff[jnp.minimum(cut_rows, nlat_all - 1)][:, None], fields.shape[:2]
    ).reshape(-1)
    smooth, east_next = filter_rows(fields.reshape(-1, length), row_cuts, rows * levels)
    smooth = smooth.reshape(fields.shape)
    east_next = east_next.reshape(rows, levels, length)
    east_smooth = smooth[:rows]
    north_smooth = smooth[rows : 2 * rows]
    east_flux = smooth[2 * rows : 3 * rows]
    north_full = smooth[3 * rows :]
    new_mass = layer_mass - TIME_STEP * (
        east_next - east_flux + (north_full[1:] - north_full[:-1])
    )
    lon_theta = face_lon(theta_field)
    heat_east = east_flux * lon_theta
    heat_next = east_next * jnp.roll(lon_theta, -1, -1)
    heat_north = north_full * theta_faces
    new_heat = theta_field * layer_mass - TIME_STEP * (
        heat_next - heat_east + (heat_north[1:] - heat_north[:-1])
    )
    height = height_ext[1:]
    new_east = east_smooth - TIME_STEP * (height - jnp.roll(height, 1, -1))
    inside = (face_rows[:-1] > 0).astype(jnp.float32)[:, None, None]
    new_north = (north_smooth - TIME_STEP * (height - height_ext[:-1])) * inside
    outputs = (new_east, new_north, new_mass, new_heat, height)
    return tuple(jnp.transpose(v, (1, 0, 2)) for v in outputs)


def solution(mesh):
    in_specs = (
        P("lev", "lat", None),
        P("lev", "lat", None),
        P("lev", "lat", None),
        P("lev", "lat", None),
        P("lat", None),
        P(),
    )
    out_specs = (
        P("lev", "lat", None),
        P("lev", "lat", None),
        P("lev", "lat", None),
        P("lev", "lat", None),
        P("lev", "lat", None),
    )
    return jax.shard_map(local, mesh=mesh, in_specs=in_specs, out_specs=out_specs, check_vma=False)
```
